256 devices in a mesh: row: 16 (over z, core), col: 16 (over y, x).
Axes of the slice: x: 4, y: 4, z: 8, core: 2. Of those that a mesh axis runs over, the one named last changes fastest.
Arguments:
- sigma_anc: float32 [48, 48, 128, 128], P('row', 'col'), as said below
- factor: float32 [16, 256, 128, 128], P('row', 'col'), may hold values from -1.25 to 1.25
- diag_inv: float32 [256, 128, 128], P('col'), as said below
- struct: int32 [256, 16], P('col'), may hold values from 0 to 47, all different within a row
Outputs:
- z_off: float32 [256, 48, 128, 128], P('col', 'row')
- z_diag: float32 [256, 128, 128], P(('col', 'row'))
The draws below stay inside these ranges and needn't reach their ends.
Inputs may be any that keep to these rules, and one draw needn't show every extreme that they name: Each row of struct names 16 different ancestor blocks, and every ancestor block is named by some row. sigma_anc is symmetric: block [b, a] is the transpose of block [a, b]. Each diag_inv[k] is lower triangular with a positive diagonal.
All inputs are finite; a program needn't handle non-finite values.
Results may differ from the reference program's by a relative error of at most 0.0003.
Values sent between devices are 32-bit elements; how exact they have to be, the bound alone decides.
A program may use at most 128 MiB of HBM per device.

```python
from functools import partial
import jax
import jax.numpy as jnp
from jax import lax

B = 128
S = 16
NA = 48
NK = 256


def draw_sigma_anc(key, part):
    first_key, second_key = jax.random.split(jax.random.fold_in(key, 11))
    noise = jax.random.normal(first_key, (NA, NA, B, B), jnp.float32)
    level = jax.random.uniform(second_key, (NA, B), jnp.float32, 1.0, 2.0)
    scale = (NA * B) ** (-0.5)
    mirrored = (noise + jnp.transpose(noise, (1, 0, 3, 2))) * (scale * 0.7071067811865476)
    blocks = jnp.arange(NA)
    cells = jnp.arange(B)
    same_block = blocks[:, None, None, None] == blocks[None, :, None, None]
    same_cell = cells[None, None, :, None] == cells[None, None, None, :]
    return mirrored + jnp.where(same_block & same_cell, level[:, None, :, None], 0.0)


def draw_diag_inv(key, part):
    first_key, second_key = jax.random.split(jax.random.fold_in(key, 23))
    lower = jnp.clip(jax.random.normal(first_key, (NK, B, B), jnp.float32), -4.0, 4.0)
    middle = jax.random.uniform(second_key, (NK, B), jnp.float32, 0.5, 1.5)
    cells = jnp.arange(B)
    below = cells[:, None] > cells[None, :]
    on_diag = cells[:, None] == cells[None, :]
    strict = jnp.where(below[None, :, :], lower * (0.5 * B ** (-0.5)), 0.0)
    return strict + jnp.where(on_diag[None, :, :], middle[:, :, None], 0.0)


def block_levels(own_key, dims, cuts, least, largest):
    loudness, own = 1.0, jax.random.fold_in(own_key, 6)
    for position, parts in cuts:
        heights = jnp.exp(jax.random.uniform(jax.random.fold_in(own, position), (parts,), jnp.float32, least / len(cuts), largest / len(cuts)))
        loudness = loudness * jnp.repeat(heights, dims[position] // parts).reshape([-1 if axis == position else 1 for axis in range(len(dims))])
    return loudness


def picks_of(rng, rows, amount, top, lift):
    sequence = jax.random.permutation(jax.random.fold_in(rng, 1), amount)
    favour = sequence
    for power in range(3):
        favour = favour * favour // amount
    favour = favour * lift // amount
    lots = jax.random.randint(jax.random.fold_in(rng, 2), (rows, amount), 0, 4096) + favour
    sure = jax.random.permutation(jax.random.fold_in(rng, 3), rows)[jnp.arange(amount) % rows]
    lots = jnp.where(jnp.arange(rows)[:, None] == sure[None, :], 1 << 14, lots)
    priority = lots * amount + jnp.arange(amount)
    return lax.top_k(priority.astype(jnp.int32), top)[1].astype(jnp.int32)


def bell_draw(stream_key, shape, deviation, limit, cuts=(), held_as=jnp.bfloat16):
    array = jax.random.normal(stream_key, shape, jnp.float32) * deviation
    if len(cuts) > 0:
        array = block_levels(stream_key, shape, cuts, -0.22, 0.18) * array
    return jnp.clip(array, min=-limit, max=limit).astype(held_as)


def setup_inputs(seed: int = 0) -> dict:
    key_of = jax.random.split(jax.random.key(seed), 5)
    sigma_anc = draw_sigma_anc(jax.random.fold_in(key_of[4], 71), 0)
    factor = bell_draw(key_of[1], (S, NK, B, B), 0.2, 1.25, ((0, 16), (1, 16)), jnp.float32)
    diag_inv = draw_diag_inv(jax.random.fold_in(key_of[4], 71), 0)
    struct = picks_of(key_of[3], NK, NA, S, 2730)
    return dict(sigma_anc=sigma_anc, factor=factor, diag_inv=diag_inv, struct=struct)


highest = lax.Precision.HIGHEST


def one_node(sigma_anc, element):
    factor_node, slot_ids, inverse_node = element
    u_node = jnp.einsum("sij,jl->sil", factor_node, inverse_node, precision=highest)
    picked = jnp.take(sigma_anc, slot_ids, axis=1)
    y_node = jnp.einsum("asij,sjl->ail", picked, u_node, precision=highest)
    ancestors = jnp.arange(sigma_anc.shape[0], dtype=jnp.int32)
    member = jnp.any(slot_ids[:, None] == ancestors[None, :], axis=0)
    z_block = jnp.where(member[:, None, None], -y_node, 0.0)
    y_slots = jnp.take(y_node, slot_ids, axis=0)
    inverse_part = jnp.einsum("ij,il->jl", inverse_node, inverse_node, precision=highest)
    z_middle = inverse_part + jnp.einsum("sij,sil->jl", u_node, y_slots, precision=highest)
    return z_block, z_middle


def reference(sigma_anc, factor, diag_inv, struct):
    z_off, z_diag = lax.map(partial(one_node, sigma_anc), (jnp.moveaxis(factor, 1, 0), struct, diag_inv))
    return z_off, z_diag
```

```python
import functools

import jax
import jax.numpy as jnp
from jax import lax
from jax.experimental import pallas as pl
from jax.experimental.pallas import tpu as pltpu
from jax.sharding import PartitionSpec as P

high = lax.Precision.HIGH


def node_kernel(struct_ref, base_ref, sig_ref, u_ref, zoff_ref, part_ref, y_scr, part_scr):
    k = pl.program_id(0)
    slots = u_ref.shape[0]
    rows = sig_ref.shape[0]
    width = u_ref.shape[-1]
    base = base_ref[0]

    def slot_step(s, acc):
        b = struct_ref[k, s]
        lhs = sig_ref[:, b].reshape(rows * width, width)
        return acc + jnp.dot(lhs, u_ref[s, 0], precision=high, preferred_element_type=jnp.float32)

    acc = lax.fori_loop(0, slots, slot_step, jnp.zeros((rows * width, width), jnp.float32))
    y_scr[...] = acc.reshape(rows, width, width)
    part_scr[...] = jnp.zeros_like(part_scr)

    @pl.loop(0, slots)
    def _(s):
        a = struct_ref[k, s] - base

        @pl.when((a >= 0) & (a < rows))
        def _():
            ut = jnp.transpose(u_ref[s, 0])
            part_scr[...] += jnp.dot(ut, y_scr[a], precision=high, preferred_element_type=jnp.float32)

    part_ref[0] = part_scr[...]

    for j in range(rows):
        def count(s, c):
            return c + (struct_ref[k, s] == base + j).astype(jnp.int32)

        hits = lax.fori_loop(0, slots, count, jnp.int32(0))
        zoff_ref[0, j] = jnp.where(hits > 0, -y_scr[j], 0.0)


def node_call(struct, base, sigma_rows, u_all):
    slots, nodes, width, _ = u_all.shape
    rows = sigma_rows.shape[0]
    grid_spec = pltpu.PrefetchScalarGridSpec(
        num_scalar_prefetch=2,
        grid=(nodes,),
        in_specs=[
            pl.BlockSpec(memory_space=pltpu.VMEM),
            pl.BlockSpec((slots, 1, width, width), lambda k, st, bs: (0, k, 0, 0)),
        ],
        out_specs=[
            pl.BlockSpec((1, rows, width, width), lambda k, st, bs: (k, 0, 0, 0)),
            pl.BlockSpec((1, width, width), lambda k, st, bs: (k, 0, 0)),
        ],
        scratch_shapes=[
            pltpu.VMEM((rows, width, width), jnp.float32),
            pltpu.VMEM((width, width), jnp.float32),
        ],
    )
    flops = 2 * nodes * slots * rows * width ** 3 * 3
    return pl.pallas_call(
        node_kernel,
        grid_spec=grid_spec,
        out_shape=[
            jax.ShapeDtypeStruct((nodes, rows, width, width), jnp.float32),
            jax.ShapeDtypeStruct((nodes, width, width), jnp.float32),
        ],
        compiler_params=pltpu.CompilerParams(vmem_limit_bytes=48 * 1024 * 1024),
        cost_estimate=pl.CostEstimate(flops=flops, transcendentals=0,
                                      bytes_accessed=4 * (sigma_rows.size + u_all.size + 2 * nodes * rows * width * width)),
    )(struct, base, sigma_rows, u_all)


def body(sigma_anc, factor, diag_inv, struct):
    row_count = sigma_anc.shape[0]
    row_index = lax.axis_index("row")
    base = jnp.reshape(row_index * row_count, (1,)).astype(jnp.int32)
    sigma_rows = lax.all_gather(sigma_anc, "col", axis=1, tiled=True)
    u_local = jnp.einsum("kij,kjl->kil", factor[0], diag_inv, precision=high)
    u_all = lax.all_gather(u_local, "row", axis=0, tiled=False)
    z_off, partial_sum = node_call(struct, base, sigma_rows, u_all)
    summed = lax.psum_scatter(partial_sum, "row", scatter_dimension=0, tiled=True)
    inverse_share = lax.dynamic_slice_in_dim(diag_inv, row_index, 1, 0)
    inverse_part = jnp.einsum("kij,kil->kjl", inverse_share, inverse_share, precision=high)
    return (z_off, inverse_part + summed)


def solution(mesh):
    in_specs = (
        P("row", "col", None, None),
        P("row", "col", None, None),
        P("col", None, None),
        P("col", None),
    )
    out_specs = (P("col", "row", None, None), P(("col", "row"), None, None))
    return jax.shard_map(body, mesh=mesh, in_specs=in_specs, out_specs=out_specs, check_vma=False)
```

```python
import functools

import jax
import jax.numpy as jnp
from jax import lax
from jax.experimental import pallas as pl
from jax.experimental.pallas import tpu as pltpu
from jax.sharding import PartitionSpec as P

high = lax.Precision.HIGH


def node_kernel(struct_ref, base_ref, sig_ref, u_ref, zoff_ref, part_ref, y_scr, part_scr):
    k = pl.program_id(0)
    slots = u_ref.shape[0]
    rows = sig_ref.shape[0]
    width = u_ref.shape[-1]
    base = base_ref[0]

    def slot_step(s, acc):
        b = struct_ref[k, s]
        lhs = sig_ref[:, b].reshape(rows * width, width)
        return acc + jnp.dot(lhs, u_ref[s, 0], precision=high, preferred_element_type=jnp.float32)

    acc = lax.fori_loop(0, slots, slot_step, jnp.zeros((rows * width, width), jnp.float32))
    y_scr[...] = acc.reshape(rows, width, width)
    part_scr[...] = jnp.zeros_like(part_scr)

    @pl.loop(0, slots)
    def _(s):
        a = struct_ref[k, s] - base

        @pl.when((a >= 0) & (a < rows))
        def _():
            ut = jnp.transpose(u_ref[s, 0])
            part_scr[...] += jnp.dot(ut, y_scr[a], precision=high, preferred_element_type=jnp.float32)

    part_ref[0] = part_scr[...]

    for j in range(rows):
        def count(s, c):
            return c + (struct_ref[k, s] == base + j).astype(jnp.int32)

        hits = lax.fori_loop(0, slots, count, jnp.int32(0))
        zoff_ref[0, j] = jnp.where(hits > 0, -y_scr[j], 0.0)


def node_call(struct, base, sigma_rows, u_all):
    slots, nodes, width, _ = u_all.shape
    rows = sigma_rows.shape[0]
    grid_spec = pltpu.PrefetchScalarGridSpec(
        num_scalar_prefetch=2,
        grid=(nodes,),
        in_specs=[
            pl.BlockSpec(memory_space=pltpu.VMEM),
            pl.BlockSpec((slots, 1, width, width), lambda k, st, bs: (0, k, 0, 0)),
        ],
        out_specs=[
            pl.BlockSpec((1, rows, width, width), lambda k, st, bs: (k, 0, 0, 0)),
            pl.BlockSpec((1, width, width), lambda k, st, bs: (k, 0, 0)),
        ],
        scratch_shapes=[
            pltpu.VMEM((rows, width, width), jnp.float32),
            pltpu.VMEM((width, width), jnp.float32),
        ],
    )
    flops = 2 * nodes * slots * rows * width ** 3 * 3
    return pl.pallas_call(
        node_kernel,
        grid_spec=grid_spec,
        out_shape=[
            jax.ShapeDtypeStruct((nodes, rows, width, width), jnp.float32),
            jax.ShapeDtypeStruct((nodes, width, width), jnp.float32),
        ],
        compiler_params=pltpu.CompilerParams(vmem_limit_bytes=48 * 1024 * 1024),
        cost_estimate=pl.CostEstimate(flops=flops, transcendentals=0,
                                      bytes_accessed=4 * (sigma_rows.size + u_all.size + 2 * nodes * rows * width * width)),
    )(struct, base, sigma_rows, u_all)


def ring_kernel(u_ref, out_ref, copy_sem, send_sem, recv_sem):
    n = out_ref.shape[0]
    half = n // 2
    me = lax.axis_index("row")
    col = lax.axis_index("col")
    right = lax.rem(me + 1, n)
    left = lax.rem(me + n - 1, n)

    own = pltpu.make_async_copy(u_ref, out_ref.at[me], copy_sem.at[0])
    own.start()

    barrier = pltpu.get_barrier_semaphore()
    for peer in (left, right):
        pl.semaphore_signal(barrier, inc=1, device_id=(peer, col), device_id_type=pl.DeviceIdType.MESH)
    pl.semaphore_wait(barrier, 2)
    own.wait()

    def link(step, direction):
        if direction == 0:
            slot = lax.rem(me - (step - 1) + n, n)
            peer = right
        else:
            slot = lax.rem(me + (step - 1), n)
            peer = left
        return pltpu.make_async_remote_copy(
            src_ref=out_ref.at[slot],
            dst_ref=out_ref.at[slot],
            send_sem=send_sem.at[direction, step - 1],
            recv_sem=recv_sem.at[direction, step - 1],
            device_id=(peer, col),
            device_id_type=pl.DeviceIdType.MESH,
        )

    started = []
    for step in range(1, half + 1):
        directions = (0, 1) if step < half else (0,)
        if step > 1:
            for direction in (0, 1):
                link(step - 1, direction).wait_recv()
        for direction in directions:
            copy = link(step, direction)
            copy.start()
            started.append(copy)
    link(half, 0).wait_recv()
    for copy in started:
        copy.wait_send()


def ring_gather(u_local, slots):
    nodes, width, _ = u_local.shape
    half = slots // 2
    return pl.pallas_call(
        ring_kernel,
        out_shape=jax.ShapeDtypeStruct((slots, nodes, width, width), jnp.float32),
        in_specs=[pl.BlockSpec(memory_space=pl.ANY)],
        out_specs=pl.BlockSpec(memory_space=pl.ANY),
        scratch_shapes=[
            pltpu.SemaphoreType.DMA((1,)),
            pltpu.SemaphoreType.DMA((2, half)),
            pltpu.SemaphoreType.DMA((2, half)),
        ],
        compiler_params=pltpu.CompilerParams(collective_id=0, has_side_effects=True),
    )(u_local)


def body(sigma_anc, factor, diag_inv, struct):
    row_count = sigma_anc.shape[0]
    row_index = lax.axis_index("row")
    base = jnp.reshape(row_index * row_count, (1,)).astype(jnp.int32)
    sigma_rows = lax.all_gather(sigma_anc, "col", axis=1, tiled=True)
    u_local = jnp.einsum("kij,kjl->kil", factor[0], diag_inv, precision=high)
    u_all = ring_gather(u_local, lax.axis_size("row"))
    z_off, partial_sum = node_call(struct, base, sigma_rows, u_all)
    pieces = lax.all_to_all(partial_sum, "row", 0, 0, tiled=True)
    summed = jnp.sum(pieces, axis=0, keepdims=True)
    inverse_share = lax.dynamic_slice_in_dim(diag_inv, row_index, 1, 0)
    inverse_part = jnp.einsum("kij,kil->kjl", inverse_share, inverse_share, precision=high)
    return (z_off, inverse_part + summed)


def solution(mesh):
    in_specs = (
        P("row", "col", None, None),
        P("row", "col", None, None),
        P("col", None, None),
        P("col", None),
    )
    out_specs = (P("col", "row", None, None), P(("col", "row"), None, None))
    return jax.shard_map(body, mesh=mesh, in_specs=in_specs, out_specs=out_specs, check_vma=False)
```

```python
import functools

import jax
import jax.numpy as jnp
from jax import lax
from jax.experimental import pallas as pl
from jax.experimental.pallas import tpu as pltpu
from jax.sharding import PartitionSpec as P

high = lax.Precision.HIGH


def node_kernel(struct_ref, base_ref, sig_ref, u_ref, zoff_ref, part_ref, y_scr, part_scr):
    k = pl.program_id(0)
    slots = u_ref.shape[0]
    rows = sig_ref.shape[0]
    width = u_ref.shape[-1]
    base = base_ref[0]

    def slot_pair(i, acc):
        first = 2 * i
        second = first + 1
        lhs = jnp.concatenate(
            [sig_ref[:, struct_ref[k, first]].reshape(rows * width, width),
             sig_ref[:, struct_ref[k, second]].reshape(rows * width, width)], axis=1)
        rhs = jnp.concatenate([u_ref[first, 0], u_ref[second, 0]], axis=0)
        return acc + jnp.dot(lhs, rhs, precision=high, preferred_element_type=jnp.float32)

    acc = lax.fori_loop(0, slots // 2, slot_pair, jnp.zeros((rows * width, width), jnp.float32))
    y_scr[...] = acc.reshape(rows, width, width)
    part_scr[...] = jnp.zeros_like(part_scr)

    @pl.loop(0, slots)
    def _(s):
        a = struct_ref[k, s] - base

        @pl.when((a >= 0) & (a < rows))
        def _():
            ut = jnp.transpose(u_ref[s, 0])
            part_scr[...] += jnp.dot(ut, y_scr[a], precision=high, preferred_element_type=jnp.float32)

    part_ref[0] = part_scr[...]

    for j in range(rows):
        def count(s, c):
            return c + (struct_ref[k, s] == base + j).astype(jnp.int32)

        hits = lax.fori_loop(0, slots, count, jnp.int32(0))
        zoff_ref[0, j] = jnp.where(hits > 0, -y_scr[j], 0.0)


def node_call(struct, base, sigma_rows, u_all):
    slots, nodes, width, _ = u_all.shape
    rows = sigma_rows.shape[0]
    grid_spec = pltpu.PrefetchScalarGridSpec(
        num_scalar_prefetch=2,
        grid=(nodes,),
        in_specs=[
            pl.BlockSpec(memory_space=pltpu.VMEM),
            pl.BlockSpec((slots, 1, width, width), lambda k, st, bs: (0, k, 0, 0)),
        ],
        out_specs=[
            pl.BlockSpec((1, rows, width, width), lambda k, st, bs: (k, 0, 0, 0)),
            pl.BlockSpec((1, width, width), lambda k, st, bs: (k, 0, 0)),
        ],
        scratch_shapes=[
            pltpu.VMEM((rows, width, width), jnp.float32),
            pltpu.VMEM((width, width), jnp.float32),
        ],
    )
    flops = 2 * nodes * slots * rows * width ** 3 * 3
    return pl.pallas_call(
        node_kernel,
        grid_spec=grid_spec,
        out_shape=[
            jax.ShapeDtypeStruct((nodes, rows, width, width), jnp.float32),
            jax.ShapeDtypeStruct((nodes, width, width), jnp.float32),
        ],
        compiler_params=pltpu.CompilerParams(vmem_limit_bytes=48 * 1024 * 1024),
        cost_estimate=pl.CostEstimate(flops=flops, transcendentals=0,
                                      bytes_accessed=4 * (sigma_rows.size + u_all.size + 2 * nodes * rows * width * width)),
    )(struct, base, sigma_rows, u_all)


def ring_kernel(parts, u_ref, out_ref, copy_sem, send_sem, recv_sem):
    n = out_ref.shape[0]
    half = n // 2
    chunk = out_ref.shape[1] // parts
    me = lax.axis_index("row")
    col = lax.axis_index("col")
    right = lax.rem(me + 1, n)
    left = lax.rem(me + n - 1, n)

    own = pltpu.make_async_copy(u_ref, out_ref.at[me], copy_sem.at[0])
    own.start()

    barrier = pltpu.get_barrier_semaphore()
    for peer in (left, right):
        pl.semaphore_signal(barrier, inc=1, device_id=(peer, col), device_id_type=pl.DeviceIdType.MESH)
    pl.semaphore_wait(barrier, 2)
    own.wait()

    def link(step, direction, part):
        if direction == 0:
            slot = lax.rem(me - (step - 1) + n, n)
            peer = right
        else:
            slot = lax.rem(me + (step - 1), n)
            peer = left
        piece = pl.ds(part * chunk, chunk)
        return pltpu.make_async_remote_copy(
            src_ref=out_ref.at[slot, piece],
            dst_ref=out_ref.at[slot, piece],
            send_sem=send_sem.at[direction, step - 1, part],
            recv_sem=recv_sem.at[direction, step - 1, part],
            device_id=(peer, col),
            device_id_type=pl.DeviceIdType.MESH,
        )

    started = []
    for step in range(1, half + 1):
        directions = (0, 1) if step < half else (0,)
        for direction in directions:
            for part in range(parts):
                if step > 1:
                    link(step - 1, direction, part).wait_recv()
                copy = link(step, direction, part)
                copy.start()
                started.append(copy)
    for part in range(parts):
        link(half, 0, part).wait_recv()
        link(half - 1, 1, part).wait_recv()
    for copy in started:
        copy.wait_send()


def ring_gather(u_local, slots, parts=4):
    nodes, width, _ = u_local.shape
    half = slots // 2
    return pl.pallas_call(
        functools.partial(ring_kernel, parts),
        out_shape=jax.ShapeDtypeStruct((slots, nodes, width, width), jnp.float32),
        in_specs=[pl.BlockSpec(memory_space=pl.ANY)],
        out_specs=pl.BlockSpec(memory_space=pl.ANY),
        scratch_shapes=[
            pltpu.SemaphoreType.DMA((1,)),
            pltpu.SemaphoreType.DMA((2, half, parts)),
            pltpu.SemaphoreType.DMA((2, half, parts)),
        ],
        compiler_params=pltpu.CompilerParams(collective_id=0, has_side_effects=True),
    )(u_local)


def body(sigma_anc, factor, diag_inv, struct):
    row_count = sigma_anc.shape[0]
    row_index = lax.axis_index("row")
    base = jnp.reshape(row_index * row_count, (1,)).astype(jnp.int32)
    sigma_rows = lax.all_gather(sigma_anc, "col", axis=1, tiled=True)
    u_local = jnp.einsum("kij,kjl->kil", factor[0], diag_inv, precision=high)
    u_all = ring_gather(u_local, lax.axis_size("row"))
    z_off, partial_sum = node_call(struct, base, sigma_rows, u_all)
    pieces = lax.all_to_all(partial_sum, "row", 0, 0, tiled=True)
    summed = jnp.sum(pieces, axis=0, keepdims=True)
    inverse_share = lax.dynamic_slice_in_dim(diag_inv, row_index, 1, 0)
    inverse_part = jnp.einsum("kij,kil->kjl", inverse_share, inverse_share, precision=high)
    return (z_off, inverse_part + summed)


def solution(mesh):
    in_specs = (
        P("row", "col", None, None),
        P("row", "col", None, None),
        P("col", None, None),
        P("col", None),
    )
    out_specs = (P("col", "row", None, None), P(("col", "row"), None, None))
    return jax.shard_map(body, mesh=mesh, in_specs=in_specs, out_specs=out_specs, check_vma=False)
```

```python
import functools

import jax
import jax.numpy as jnp
from jax import lax
from jax.experimental import pallas as pl
from jax.experimental.pallas import tpu as pltpu
from jax.sharding import PartitionSpec as P

high = lax.Precision.HIGH


def node_kernel(struct_ref, base_ref, sig_ref, u_ref, zoff_ref, part_ref, y_scr, part_scr):
    k = pl.program_id(0)
    slots = u_ref.shape[0]
    rows = sig_ref.shape[0]
    width = u_ref.shape[-1]
    base = base_ref[0]

    def slot_pair(i, acc):
        first = 2 * i
        second = first + 1
        lhs = jnp.concatenate(
            [sig_ref[:, struct_ref[k, first]].reshape(rows * width, width),
             sig_ref[:, struct_ref[k, second]].reshape(rows * width, width)], axis=1)
        rhs = jnp.concatenate([u_ref[first, 0], u_ref[second, 0]], axis=0)
        return acc + jnp.dot(lhs, rhs, precision=high, preferred_element_type=jnp.float32)

    acc = lax.fori_loop(0, slots // 2, slot_pair, jnp.zeros((rows * width, width), jnp.float32))
    y_scr[...] = acc.reshape(rows, width, width)
    part_scr[...] = jnp.zeros_like(part_scr)

    @pl.loop(0, slots)
    def _(s):
        a = struct_ref[k, s] - base

        @pl.when((a >= 0) & (a < rows))
        def _():
            ut = jnp.transpose(u_ref[s, 0])
            part_scr[...] += jnp.dot(ut, y_scr[a], precision=high, preferred_element_type=jnp.float32)

    part_ref[0] = part_scr[...]

    for j in range(rows):
        def count(s, c):
            return c + (struct_ref[k, s] == base + j).astype(jnp.int32)

        hits = lax.fori_loop(0, slots, count, jnp.int32(0))
        zoff_ref[0, j] = jnp.where(hits > 0, -y_scr[j], 0.0)


def node_call(struct, base, sigma_rows, u_all):
    slots, nodes, width, _ = u_all.shape
    rows = sigma_rows.shape[0]
    grid_spec = pltpu.PrefetchScalarGridSpec(
        num_scalar_prefetch=2,
        grid=(nodes,),
        in_specs=[
            pl.BlockSpec(memory_space=pltpu.VMEM),
            pl.BlockSpec((slots, 1, width, width), lambda k, st, bs: (0, k, 0, 0)),
        ],
        out_specs=[
            pl.BlockSpec((1, rows, width, width), lambda k, st, bs: (k, 0, 0, 0)),
            pl.BlockSpec((1, width, width), lambda k, st, bs: (k, 0, 0)),
        ],
        scratch_shapes=[
            pltpu.VMEM((rows, width, width), jnp.float32),
            pltpu.VMEM((width, width), jnp.float32),
        ],
    )
    flops = 2 * nodes * slots * rows * width ** 3 * 3
    return pl.pallas_call(
        node_kernel,
        grid_spec=grid_spec,
        out_shape=[
            jax.ShapeDtypeStruct((nodes, rows, width, width), jnp.float32),
            jax.ShapeDtypeStruct((nodes, width, width), jnp.float32),
        ],
        compiler_params=pltpu.CompilerParams(vmem_limit_bytes=48 * 1024 * 1024),
        cost_estimate=pl.CostEstimate(flops=flops, transcendentals=0,
                                      bytes_accessed=4 * (sigma_rows.size + u_all.size + 2 * nodes * rows * width * width)),
    )(struct, base, sigma_rows, u_all)


def greet_neighbours(me, col, n):
    barrier = pltpu.get_barrier_semaphore()
    for peer in (lax.rem(me + n - 1, n), lax.rem(me + 1, n)):
        pl.semaphore_signal(barrier, inc=1, device_id=(peer, col), device_id_type=pl.DeviceIdType.MESH)
    pl.semaphore_wait(barrier, 2)


def step_parts(step, direction, half, parts):
    if step < half:
        return range(parts)
    if direction == 0:
        return range(parts // 2)
    return range(parts // 2, parts)


def ring_kernel(steps, parts, u_ref, out_ref, copy_sem, send_sem, recv_sem):
    n = out_ref.shape[0]
    chunk = out_ref.shape[1] // parts
    me = lax.axis_index("row")
    col = lax.axis_index("col")

    def link(step, direction, part):
        if direction == 0:
            slot = lax.rem(me - (step - 1) + n, n)
            peer = lax.rem(me + 1, n)
        else:
            slot = lax.rem(me + (step - 1), n)
            peer = lax.rem(me + n - 1, n)
        piece = pl.ds(part * chunk, chunk)
        return pltpu.make_async_remote_copy(
            src_ref=out_ref.at[slot, piece], dst_ref=out_ref.at[slot, piece],
            send_sem=send_sem.at[direction, step - 1, part],
            recv_sem=recv_sem.at[direction, step - 1, part],
            device_id=(peer, col), device_id_type=pl.DeviceIdType.MESH)

    own = pltpu.make_async_copy(u_ref, out_ref.at[me], copy_sem.at[0])
    own.start()
    greet_neighbours(me, col, n)
    own.wait()

    started = []
    for step in range(1, steps + 1):
        for direction in (0, 1):
            for part in range(parts):
                if step > 1:
                    link(step - 1, direction, part).wait_recv()
                copy = link(step, direction, part)
                copy.start()
                started.append(copy)
    for direction in (0, 1):
        for part in range(parts):
            link(steps, direction, part).wait_recv()
    for copy in started:
        copy.wait_send()


def ring_gather(u_local, slots, steps, parts):
    nodes, width, _ = u_local.shape
    return pl.pallas_call(
        functools.partial(ring_kernel, steps, parts),
        out_shape=jax.ShapeDtypeStruct((slots, nodes, width, width), jnp.float32),
        in_specs=[pl.BlockSpec(memory_space=pl.ANY)],
        out_specs=pl.BlockSpec(memory_space=pl.ANY),
        scratch_shapes=[
            pltpu.SemaphoreType.DMA((1,)),
            pltpu.SemaphoreType.DMA((2, steps, parts)),
            pltpu.SemaphoreType.DMA((2, steps, parts)),
        ],
        compiler_params=pltpu.CompilerParams(collective_id=0, has_side_effects=True),
    )(u_local)


def fused_kernel(first, parts, struct_ref, base_ref, sig_ref, u_in, u_out, zoff_ref, part_ref,
                 u_vmem, y_acc, load_sem, send_sem, recv_sem):
    n = u_out.shape[0]
    half = n // 2
    nodes = u_out.shape[1]
    chunk = nodes // parts
    rows = sig_ref.shape[0]
    width = sig_ref.shape[-1]
    me = lax.axis_index("row")
    col = lax.axis_index("col")
    base = base_ref[0]

    def link(step, direction, part):
        if direction == 0:
            slot = lax.rem(me - (step - 1) + n, n)
            peer = lax.rem(me + 1, n)
        else:
            slot = lax.rem(me + (step - 1), n)
            peer = lax.rem(me + n - 1, n)
        piece = pl.ds(part * chunk, chunk)
        return pltpu.make_async_remote_copy(
            src_ref=u_out.at[slot, piece], dst_ref=u_out.at[slot, piece],
            send_sem=send_sem.at[direction, step - 1 - first, part],
            recv_sem=recv_sem.at[direction, step - 1 - first, part],
            device_id=(peer, col), device_id_type=pl.DeviceIdType.MESH)

    def load(slot):
        return pltpu.make_async_copy(u_out.at[slot], u_vmem.at[slot], load_sem.at[slot])

    def wrap(offset):
        return lax.rem(me + offset + 2 * n, n)

    greet_neighbours(me, col, n)
    for offset in range(-first, first + 1):
        load(wrap(offset)).start()

    started = []

    def send_step(step):
        for direction in (0, 1):
            for part in step_parts(step, direction, half, parts):
                copy = link(step, direction, part)
                copy.start()
                started.append(copy)

    send_step(first + 1)

    def lhs_block(k, slot):
        return sig_ref[:, struct_ref[k, slot]].reshape(rows * width, width)

    def add_single(slot):
        def node(k, carry):
            y_acc[k] += jnp.dot(lhs_block(k, slot), u_vmem[slot, k], precision=high,
                                preferred_element_type=jnp.float32)
            return carry
        lax.fori_loop(0, nodes, node, 0)

    def add_pair(one, two):
        def node(k, carry):
            lhs = jnp.concatenate([lhs_block(k, one), lhs_block(k, two)], axis=1)
            rhs = jnp.concatenate([u_vmem[one, k], u_vmem[two, k]], axis=0)
            y_acc[k] += jnp.dot(lhs, rhs, precision=high, preferred_element_type=jnp.float32)
            return carry
        lax.fori_loop(0, nodes, node, 0)

    load(me).wait()
    y_acc[...] = jnp.zeros_like(y_acc)
    add_single(me)
    for offset in range(1, first + 1):
        load(wrap(-offset)).wait()
        load(wrap(offset)).wait()
        add_pair(wrap(-offset), wrap(offset))

    for step in range(first + 1, half + 1):
        for direction in (0, 1):
            for part in step_parts(step, direction, half, parts):
                link(step, direction, part).wait_recv()
        if step < half:
            send_step(step + 1)
            one, two = wrap(-step), wrap(step)
            load(one).start()
            load(two).start()
            load(one).wait()
            load(two).wait()
            add_pair(one, two)
        else:
            last = wrap(half)
            load(last).start()
            load(last).wait()
            add_single(last)

    for copy in started:
        copy.wait_send()

    def finish(k, carry):
        y = y_acc[k].reshape(rows, width, width)
        total = jnp.zeros((width, width), jnp.float32)
        for j in range(rows):
            def scan(s, acc):
                hit = (struct_ref[k, s] == base + j).astype(jnp.int32)
                return acc[0] + hit, acc[1] + hit * s
            hits, slot = lax.fori_loop(0, n, scan, (jnp.int32(0), jnp.int32(0)))
            slot = jnp.minimum(slot, n - 1)
            term = jnp.dot(jnp.transpose(u_vmem[slot, k]), y[j], precision=high,
                           preferred_element_type=jnp.float32)
            total = total + jnp.where(hits > 0, term, 0.0)
            zoff_ref[k, j] = jnp.where(hits > 0, -y[j], 0.0)
        part_ref[k] = total
        return carry

    lax.fori_loop(0, nodes, finish, 0)


def fused_call(struct, base, sigma_rows, u_all, first, parts):
    slots, nodes, width, _ = u_all.shape
    rows = sigma_rows.shape[0]
    later = slots // 2 - first
    flops = 2 * nodes * slots * rows * width ** 3 * 3
    return pl.pallas_call(
        functools.partial(fused_kernel, first, parts),
        out_shape=[
            jax.ShapeDtypeStruct(u_all.shape, jnp.float32),
            jax.ShapeDtypeStruct((nodes, rows, width, width), jnp.float32),
            jax.ShapeDtypeStruct((nodes, width, width), jnp.float32),
        ],
        in_specs=[
            pl.BlockSpec(memory_space=pltpu.SMEM),
            pl.BlockSpec(memory_space=pltpu.SMEM),
            pl.BlockSpec(memory_space=pltpu.VMEM),
            pl.BlockSpec(memory_space=pl.ANY),
        ],
        out_specs=[
            pl.BlockSpec(memory_space=pl.ANY),
            pl.BlockSpec(memory_space=pltpu.VMEM),
            pl.BlockSpec(memory_space=pltpu.VMEM),
        ],
        scratch_shapes=[
            pltpu.VMEM(u_all.shape, jnp.float32),
            pltpu.VMEM((nodes, rows * width, width), jnp.float32),
            pltpu.SemaphoreType.DMA((slots,)),
            pltpu.SemaphoreType.DMA((2, later, parts)),
            pltpu.SemaphoreType.DMA((2, later, parts)),
        ],
        input_output_aliases={3: 0},
        compiler_params=pltpu.CompilerParams(collective_id=1, has_side_effects=True,
                                             vmem_limit_bytes=60 * 1024 * 1024),
        cost_estimate=pl.CostEstimate(flops=flops, transcendentals=0,
                                      bytes_accessed=4 * (sigma_rows.size + u_all.size)),
    )(struct, base, sigma_rows, u_all)


def body(sigma_anc, factor, diag_inv, struct):
    row_count = sigma_anc.shape[0]
    row_index = lax.axis_index("row")
    base = jnp.reshape(row_index * row_count, (1,)).astype(jnp.int32)
    sigma_rows = lax.all_gather(sigma_anc, "col", axis=1, tiled=True)
    u_local = jnp.einsum("kij,kjl->kil", factor[0], diag_inv, precision=high)
    first, parts = 5, 4
    u_head = ring_gather(u_local, lax.axis_size("row"), first, parts)
    unused_u, z_off, partial_sum = fused_call(struct, base, sigma_rows, u_head, first, parts)
    pieces = lax.all_to_all(partial_sum, "row", 0, 0, tiled=True)
    summed = jnp.sum(pieces, axis=0, keepdims=True)
    inverse_share = lax.dynamic_slice_in_dim(diag_inv, row_index, 1, 0)
    inverse_part = jnp.einsum("kij,kil->kjl", inverse_share, inverse_share, precision=high)
    return (z_off, inverse_part + summed)


def solution(mesh):
    in_specs = (
        P("row", "col", None, None),
        P("row", "col", None, None),
        P("col", None, None),
        P("col", None),
    )
    out_specs = (P("col", "row", None, None), P(("col", "row"), None, None))
    return jax.shard_map(body, mesh=mesh, in_specs=in_specs, out_specs=out_specs, check_vma=False)
```

```python
import functools

import jax
import jax.numpy as jnp
from jax import lax
from jax.experimental import pallas as pl
from jax.experimental.pallas import tpu as pltpu
from jax.sharding import PartitionSpec as P

high = lax.Precision.HIGH


def node_kernel(struct_ref, base_ref, sig_ref, u_ref, zoff_ref, part_ref, y_scr, part_scr):
    k = pl.program_id(0)
    slots = u_ref.shape[0]
    rows = sig_ref.shape[0]
    width = u_ref.shape[-1]
    base = base_ref[0]

    def slot_pair(i, acc):
        first = 2 * i
        second = first + 1
        lhs = jnp.concatenate(
            [sig_ref[:, struct_ref[k, first]].reshape(rows * width, width),
             sig_ref[:, struct_ref[k, second]].reshape(rows * width, width)], axis=1)
        rhs = jnp.concatenate([u_ref[first, 0], u_ref[second, 0]], axis=0)
        return acc + jnp.dot(lhs, rhs, precision=high, preferred_element_type=jnp.float32)

    acc = lax.fori_loop(0, slots // 2, slot_pair, jnp.zeros((rows * width, width), jnp.float32))
    y_scr[...] = acc.reshape(rows, width, width)
    part_scr[...] = jnp.zeros_like(part_scr)

    @pl.loop(0, slots)
    def _(s):
        a = struct_ref[k, s] - base

        @pl.when((a >= 0) & (a < rows))
        def _():
            ut = jnp.transpose(u_ref[s, 0])
            part_scr[...] += jnp.dot(ut, y_scr[a], precision=high, preferred_element_type=jnp.float32)

    part_ref[0] = part_scr[...]

    for j in range(rows):
        def count(s, c):
            return c + (struct_ref[k, s] == base + j).astype(jnp.int32)

        hits = lax.fori_loop(0, slots, count, jnp.int32(0))
        zoff_ref[0, j] = jnp.where(hits > 0, -y_scr[j], 0.0)


def node_call(struct, base, sigma_rows, u_all):
    slots, nodes, width, _ = u_all.shape
    rows = sigma_rows.shape[0]
    grid_spec = pltpu.PrefetchScalarGridSpec(
        num_scalar_prefetch=2,
        grid=(nodes,),
        in_specs=[
            pl.BlockSpec(memory_space=pltpu.VMEM),
            pl.BlockSpec((slots, 1, width, width), lambda k, st, bs: (0, k, 0, 0)),
        ],
        out_specs=[
            pl.BlockSpec((1, rows, width, width), lambda k, st, bs: (k, 0, 0, 0)),
            pl.BlockSpec((1, width, width), lambda k, st, bs: (k, 0, 0)),
        ],
        scratch_shapes=[
            pltpu.VMEM((rows, width, width), jnp.float32),
            pltpu.VMEM((width, width), jnp.float32),
        ],
    )
    flops = 2 * nodes * slots * rows * width ** 3 * 3
    return pl.pallas_call(
        node_kernel,
        grid_spec=grid_spec,
        out_shape=[
            jax.ShapeDtypeStruct((nodes, rows, width, width), jnp.float32),
            jax.ShapeDtypeStruct((nodes, width, width), jnp.float32),
        ],
        compiler_params=pltpu.CompilerParams(vmem_limit_bytes=48 * 1024 * 1024),
        cost_estimate=pl.CostEstimate(flops=flops, transcendentals=0,
                                      bytes_accessed=4 * (sigma_rows.size + u_all.size + 2 * nodes * rows * width * width)),
    )(struct, base, sigma_rows, u_all)


def greet_neighbours(me, col, n):
    barrier = pltpu.get_barrier_semaphore()
    for peer in (lax.rem(me + n - 1, n), lax.rem(me + 1, n)):
        pl.semaphore_signal(barrier, inc=1, device_id=(peer, col), device_id_type=pl.DeviceIdType.MESH)
    pl.semaphore_wait(barrier, 2)


def step_parts(step, direction, half, parts):
    if step < half:
        return range(parts)
    if direction == 0:
        return range(parts // 2)
    return range(parts // 2, parts)


def ring_kernel(steps, parts, u_ref, out_ref, copy_sem, send_sem, recv_sem):
    n = out_ref.shape[0]
    chunk = out_ref.shape[1] // parts
    me = lax.axis_index("row")
    col = lax.axis_index("col")

    def link(step, direction, part):
        if direction == 0:
            slot = lax.rem(me - (step - 1) + n, n)
            peer = lax.rem(me + 1, n)
        else:
            slot = lax.rem(me + (step - 1), n)
            peer = lax.rem(me + n - 1, n)
        piece = pl.ds(part * chunk, chunk)
        return pltpu.make_async_remote_copy(
            src_ref=out_ref.at[slot, piece], dst_ref=out_ref.at[slot, piece],
            send_sem=send_sem.at[direction, step - 1, part],
            recv_sem=recv_sem.at[direction, step - 1, part],
            device_id=(peer, col), device_id_type=pl.DeviceIdType.MESH)

    own = pltpu.make_async_copy(u_ref, out_ref.at[me], copy_sem.at[0])
    own.start()
    greet_neighbours(me, col, n)
    own.wait()

    started = []
    for step in range(1, steps + 1):
        for direction in (0, 1):
            for part in range(parts):
                if step > 1:
                    link(step - 1, direction, part).wait_recv()
                copy = link(step, direction, part)
                copy.start()
                started.append(copy)
    for direction in (0, 1):
        for part in range(parts):
            link(steps, direction, part).wait_recv()
    for copy in started:
        copy.wait_send()


def ring_gather(u_local, slots, steps, parts):
    nodes, width, _ = u_local.shape
    return pl.pallas_call(
        functools.partial(ring_kernel, steps, parts),
        out_shape=jax.ShapeDtypeStruct((slots, nodes, width, width), jnp.float32),
        in_specs=[pl.BlockSpec(memory_space=pl.ANY)],
        out_specs=pl.BlockSpec(memory_space=pl.ANY),
        scratch_shapes=[
            pltpu.SemaphoreType.DMA((1,)),
            pltpu.SemaphoreType.DMA((2, steps, parts)),
            pltpu.SemaphoreType.DMA((2, steps, parts)),
        ],
        compiler_params=pltpu.CompilerParams(collective_id=0, has_side_effects=True),
    )(u_local)


def fused_kernel(first, parts, struct_ref, base_ref, sig_ref, u_in, u_out, zoff_ref, part_ref,
                 u_vmem, y_acc, load_sem, send_sem, recv_sem):
    n = u_out.shape[0]
    half = n // 2
    nodes = u_out.shape[1]
    chunk = nodes // parts
    rows = sig_ref.shape[0]
    width = sig_ref.shape[-1]
    me = lax.axis_index("row")
    col = lax.axis_index("col")
    base = base_ref[0]

    def link(step, direction, part):
        if direction == 0:
            slot = lax.rem(me - (step - 1) + n, n)
            peer = lax.rem(me + 1, n)
        else:
            slot = lax.rem(me + (step - 1), n)
            peer = lax.rem(me + n - 1, n)
        piece = pl.ds(part * chunk, chunk)
        return pltpu.make_async_remote_copy(
            src_ref=u_out.at[slot, piece], dst_ref=u_out.at[slot, piece],
            send_sem=send_sem.at[direction, step - 1 - first, part],
            recv_sem=recv_sem.at[direction, step - 1 - first, part],
            device_id=(peer, col), device_id_type=pl.DeviceIdType.MESH)

    def load(slot):
        return pltpu.make_async_copy(u_out.at[slot], u_vmem.at[slot], load_sem.at[slot])

    def wrap(offset):
        return lax.rem(me + offset + 2 * n, n)

    greet_neighbours(me, col, n)
    for offset in range(-first, first + 1):
        load(wrap(offset)).start()

    started = []

    def send_step(step):
        for direction in (0, 1):
            for part in step_parts(step, direction, half, parts):
                copy = link(step, direction, part)
                copy.start()
                started.append(copy)

    send_step(first + 1)

    def lhs_block(k, slot):
        return sig_ref[:, struct_ref[k, slot]].reshape(rows * width, width)

    def add_single(slot):
        def node(k, carry):
            y_acc[k] += jnp.dot(lhs_block(k, slot), u_vmem[slot, k], precision=high,
                                preferred_element_type=jnp.float32)
            return carry
        lax.fori_loop(0, nodes, node, 0)

    def add_pair(one, two):
        def node(k, carry):
            lhs = jnp.concatenate([lhs_block(k, one), lhs_block(k, two)], axis=1)
            rhs = jnp.concatenate([u_vmem[one, k], u_vmem[two, k]], axis=0)
            y_acc[k] += jnp.dot(lhs, rhs, precision=high, preferred_element_type=jnp.float32)
            return carry
        lax.fori_loop(0, nodes, node, 0)

    load(me).wait()
    y_acc[...] = jnp.zeros_like(y_acc)
    add_single(me)
    for offset in range(1, first + 1):
        load(wrap(-offset)).wait()
        load(wrap(offset)).wait()
        add_pair(wrap(-offset), wrap(offset))

    for step in range(first + 1, half + 1):
        for direction in (0, 1):
            for part in step_parts(step, direction, half, parts):
                link(step, direction, part).wait_recv()
        if step < half:
            send_step(step + 1)
            one, two = wrap(-step), wrap(step)
            load(one).start()
            load(two).start()
            load(one).wait()
            load(two).wait()
            add_pair(one, two)
        else:
            last = wrap(half)
            load(last).start()
            load(last).wait()
            add_single(last)

    for copy in started:
        copy.wait_send()

    def finish(k, carry):
        y = y_acc[k].reshape(rows, width, width)
        total = jnp.zeros((width, width), jnp.float32)
        for j in range(rows):
            def scan(s, acc):
                hit = (struct_ref[k, s] == base + j).astype(jnp.int32)
                return acc[0] + hit, acc[1] + hit * s
            hits, slot = lax.fori_loop(0, n, scan, (jnp.int32(0), jnp.int32(0)))
            slot = jnp.minimum(slot, n - 1)
            term = jnp.dot(jnp.transpose(u_vmem[slot, k]), y[j], precision=high,
                           preferred_element_type=jnp.float32)
            total = total + jnp.where(hits > 0, term, 0.0)
            zoff_ref[k, j] = jnp.where(hits > 0, -y[j], 0.0)
        part_ref[k] = total
        return carry

    lax.fori_loop(0, nodes, finish, 0)


def fused_call(struct, base, sigma_rows, u_all, first, parts):
    slots, nodes, width, _ = u_all.shape
    rows = sigma_rows.shape[0]
    later = slots // 2 - first
    flops = 2 * nodes * slots * rows * width ** 3 * 3
    return pl.pallas_call(
        functools.partial(fused_kernel, first, parts),
        out_shape=[
            jax.ShapeDtypeStruct(u_all.shape, jnp.float32),
            jax.ShapeDtypeStruct((nodes, rows, width, width), jnp.float32),
            jax.ShapeDtypeStruct((nodes, width, width), jnp.float32),
        ],
        in_specs=[
            pl.BlockSpec(memory_space=pltpu.SMEM),
            pl.BlockSpec(memory_space=pltpu.SMEM),
            pl.BlockSpec(memory_space=pltpu.VMEM),
            pl.BlockSpec(memory_space=pl.ANY),
        ],
        out_specs=[
            pl.BlockSpec(memory_space=pl.ANY),
            pl.BlockSpec(memory_space=pltpu.VMEM),
            pl.BlockSpec(memory_space=pltpu.VMEM),
        ],
        scratch_shapes=[
            pltpu.VMEM(u_all.shape, jnp.float32),
            pltpu.VMEM((nodes, rows * width, width), jnp.float32),
            pltpu.SemaphoreType.DMA((slots,)),
            pltpu.SemaphoreType.DMA((2, later, parts)),
            pltpu.SemaphoreType.DMA((2, later, parts)),
        ],
        input_output_aliases={3: 0},
        compiler_params=pltpu.CompilerParams(collective_id=1, has_side_effects=True,
                                             vmem_limit_bytes=60 * 1024 * 1024),
        cost_estimate=pl.CostEstimate(flops=flops, transcendentals=0,
                                      bytes_accessed=4 * (sigma_rows.size + u_all.size)),
    )(struct, base, sigma_rows, u_all)


def body(sigma_anc, factor, diag_inv, struct):
    row_count = sigma_anc.shape[0]
    row_index = lax.axis_index("row")
    base = jnp.reshape(row_index * row_count, (1,)).astype(jnp.int32)
    sigma_rows = lax.all_gather(sigma_anc, "col", axis=1, tiled=True)
    u_local = jnp.einsum("kij,kjl->kil", factor[0], diag_inv, precision=high)
    first, parts = 3, 4
    u_head = ring_gather(u_local, lax.axis_size("row"), first, parts)
    unused_u, z_off, partial_sum = fused_call(struct, base, sigma_rows, u_head, first, parts)
    pieces = lax.all_to_all(partial_sum, "row", 0, 0, tiled=True)
    summed = jnp.sum(pieces, axis=0, keepdims=True)
    inverse_share = lax.dynamic_slice_in_dim(diag_inv, row_index, 1, 0)
    inverse_part = jnp.einsum("kij,kil->kjl", inverse_share, inverse_share, precision=high)
    return (z_off, inverse_part + summed)


def solution(mesh):
    in_specs = (
        P("row", "col", None, None),
        P("row", "col", None, None),
        P("col", None, None),
        P("col", None),
    )
    out_specs = (P("col", "row", None, None), P(("col", "row"), None, None))
    return jax.shard_map(body, mesh=mesh, in_specs=in_specs, out_specs=out_specs, check_vma=False)
```

```python
import functools

import jax
import jax.numpy as jnp
from jax import lax
from jax.experimental import pallas as pl
from jax.experimental.pallas import tpu as pltpu
from jax.sharding import PartitionSpec as P

high = lax.Precision.HIGH


def node_kernel(struct_ref, base_ref, sig_ref, u_ref, zoff_ref, part_ref, y_scr, part_scr):
    k = pl.program_id(0)
    slots = u_ref.shape[0]
    rows = sig_ref.shape[0]
    width = u_ref.shape[-1]
    base = base_ref[0]

    def slot_pair(i, acc):
        first = 2 * i
        second = first + 1
        lhs = jnp.concatenate(
            [sig_ref[:, struct_ref[k, first]].reshape(rows * width, width),
             sig_ref[:, struct_ref[k, second]].reshape(rows * width, width)], axis=1)
        rhs = jnp.concatenate([u_ref[first, 0], u_ref[second, 0]], axis=0)
        return acc + jnp.dot(lhs, rhs, precision=high, preferred_element_type=jnp.float32)

    acc = lax.fori_loop(0, slots // 2, slot_pair, jnp.zeros((rows * width, width), jnp.float32))
    y_scr[...] = acc.reshape(rows, width, width)
    part_scr[...] = jnp.zeros_like(part_scr)

    @pl.loop(0, slots)
    def _(s):
        a = struct_ref[k, s] - base

        @pl.when((a >= 0) & (a < rows))
        def _():
            ut = jnp.transpose(u_ref[s, 0])
            part_scr[...] += jnp.dot(ut, y_scr[a], precision=high, preferred_element_type=jnp.float32)

    part_ref[0] = part_scr[...]

    for j in range(rows):
        def count(s, c):
            return c + (struct_ref[k, s] == base + j).astype(jnp.int32)

        hits = lax.fori_loop(0, slots, count, jnp.int32(0))
        zoff_ref[0, j] = jnp.where(hits > 0, -y_scr[j], 0.0)


def node_call(struct, base, sigma_rows, u_all):
    slots, nodes, width, _ = u_all.shape
    rows = sigma_rows.shape[0]
    grid_spec = pltpu.PrefetchScalarGridSpec(
        num_scalar_prefetch=2,
        grid=(nodes,),
        in_specs=[
            pl.BlockSpec(memory_space=pltpu.VMEM),
            pl.BlockSpec((slots, 1, width, width), lambda k, st, bs: (0, k, 0, 0)),
        ],
        out_specs=[
            pl.BlockSpec((1, rows, width, width), lambda k, st, bs: (k, 0, 0, 0)),
            pl.BlockSpec((1, width, width), lambda k, st, bs: (k, 0, 0)),
        ],
        scratch_shapes=[
            pltpu.VMEM((rows, width, width), jnp.float32),
            pltpu.VMEM((width, width), jnp.float32),
        ],
    )
    flops = 2 * nodes * slots * rows * width ** 3 * 3
    return pl.pallas_call(
        node_kernel,
        grid_spec=grid_spec,
        out_shape=[
            jax.ShapeDtypeStruct((nodes, rows, width, width), jnp.float32),
            jax.ShapeDtypeStruct((nodes, width, width), jnp.float32),
        ],
        compiler_params=pltpu.CompilerParams(vmem_limit_bytes=48 * 1024 * 1024),
        cost_estimate=pl.CostEstimate(flops=flops, transcendentals=0,
                                      bytes_accessed=4 * (sigma_rows.size + u_all.size + 2 * nodes * rows * width * width)),
    )(struct, base, sigma_rows, u_all)


def greet_neighbours(me, col, n):
    barrier = pltpu.get_barrier_semaphore()
    for peer in (lax.rem(me + n - 1, n), lax.rem(me + 1, n)):
        pl.semaphore_signal(barrier, inc=1, device_id=(peer, col), device_id_type=pl.DeviceIdType.MESH)
    pl.semaphore_wait(barrier, 2)


def step_parts(step, direction, half, parts):
    if step < half:
        return range(parts)
    if direction == 0:
        return range(parts // 2)
    return range(parts // 2, parts)


def ring_kernel(steps, parts, u_ref, out_ref, copy_sem, send_sem, recv_sem):
    n = out_ref.shape[0]
    chunk = out_ref.shape[1] // parts
    me = lax.axis_index("row")
    col = lax.axis_index("col")

    def link(step, direction, part):
        if direction == 0:
            slot = lax.rem(me - (step - 1) + n, n)
            peer = lax.rem(me + 1, n)
        else:
            slot = lax.rem(me + (step - 1), n)
            peer = lax.rem(me + n - 1, n)
        piece = pl.ds(part * chunk, chunk)
        return pltpu.make_async_remote_copy(
            src_ref=out_ref.at[slot, piece], dst_ref=out_ref.at[slot, piece],
            send_sem=send_sem.at[direction, step - 1, part],
            recv_sem=recv_sem.at[direction, step - 1, part],
            device_id=(peer, col), device_id_type=pl.DeviceIdType.MESH)

    own = pltpu.make_async_copy(u_ref, out_ref.at[me], copy_sem.at[0])
    own.start()
    greet_neighbours(me, col, n)
    own.wait()

    started = []
    for step in range(1, steps + 1):
        for direction in (0, 1):
            for part in range(parts):
                if step > 1:
                    link(step - 1, direction, part).wait_recv()
                copy = link(step, direction, part)
                copy.start()
                started.append(copy)
    for direction in (0, 1):
        for part in range(parts):
            link(steps, direction, part).wait_recv()
    for copy in started:
        copy.wait_send()


def ring_gather(u_local, slots, steps, parts):
    nodes, width, _ = u_local.shape
    return pl.pallas_call(
        functools.partial(ring_kernel, steps, parts),
        out_shape=jax.ShapeDtypeStruct((slots, nodes, width, width), jnp.float32),
        in_specs=[pl.BlockSpec(memory_space=pl.ANY)],
        out_specs=pl.BlockSpec(memory_space=pl.ANY),
        scratch_shapes=[
            pltpu.SemaphoreType.DMA((1,)),
            pltpu.SemaphoreType.DMA((2, steps, parts)),
            pltpu.SemaphoreType.DMA((2, steps, parts)),
        ],
        compiler_params=pltpu.CompilerParams(collective_id=0, has_side_effects=True),
    )(u_local)


def fused_kernel(first, parts, struct_ref, base_ref, sig_ref, u_in, u_out, zoff_ref, sum_ref,
                 u_vmem, y_acc, part_ref, gather_buf, load_sem, send_sem, recv_sem, out_sem, in_sem):
    n = u_out.shape[0]
    half = n // 2
    nodes = u_out.shape[1]
    chunk = nodes // parts
    rows = sig_ref.shape[0]
    width = sig_ref.shape[-1]
    me = lax.axis_index("row")
    col = lax.axis_index("col")
    base = base_ref[0]

    def link(step, direction, part):
        if direction == 0:
            slot = lax.rem(me - (step - 1) + n, n)
            peer = lax.rem(me + 1, n)
        else:
            slot = lax.rem(me + (step - 1), n)
            peer = lax.rem(me + n - 1, n)
        piece = pl.ds(part * chunk, chunk)
        return pltpu.make_async_remote_copy(
            src_ref=u_out.at[slot, piece], dst_ref=u_out.at[slot, piece],
            send_sem=send_sem.at[direction, step - 1 - first, part],
            recv_sem=recv_sem.at[direction, step - 1 - first, part],
            device_id=(peer, col), device_id_type=pl.DeviceIdType.MESH)

    def load(slot):
        return pltpu.make_async_copy(u_out.at[slot], u_vmem.at[slot], load_sem.at[slot])

    def wrap(offset):
        return lax.rem(me + offset + 2 * n, n)

    barrier = pltpu.get_barrier_semaphore()
    for offset in range(1, n):
        pl.semaphore_signal(barrier, inc=1, device_id=(lax.rem(me + offset, n), col),
                            device_id_type=pl.DeviceIdType.MESH)
    pl.semaphore_wait(barrier, n - 1)
    for offset in range(-first, first + 1):
        load(wrap(offset)).start()

    started = []

    def send_step(step):
        for direction in (0, 1):
            for part in step_parts(step, direction, half, parts):
                copy = link(step, direction, part)
                copy.start()
                started.append(copy)

    send_step(first + 1)

    def lhs_block(k, slot):
        return sig_ref[:, struct_ref[k, slot]].reshape(rows * width, width)

    def add_single(slot):
        def node(k, carry):
            y_acc[k] += jnp.dot(lhs_block(k, slot), u_vmem[slot, k], precision=high,
                                preferred_element_type=jnp.float32)
            return carry
        lax.fori_loop(0, nodes, node, 0)

    def add_pair(one, two):
        def node(k, carry):
            lhs = jnp.concatenate([lhs_block(k, one), lhs_block(k, two)], axis=1)
            rhs = jnp.concatenate([u_vmem[one, k], u_vmem[two, k]], axis=0)
            y_acc[k] += jnp.dot(lhs, rhs, precision=high, preferred_element_type=jnp.float32)
            return carry
        lax.fori_loop(0, nodes, node, 0)

    load(me).wait()
    y_acc[...] = jnp.zeros_like(y_acc)
    add_single(me)
    for offset in range(1, first + 1):
        load(wrap(-offset)).wait()
        load(wrap(offset)).wait()
        add_pair(wrap(-offset), wrap(offset))

    for step in range(first + 1, half + 1):
        for direction in (0, 1):
            for part in step_parts(step, direction, half, parts):
                link(step, direction, part).wait_recv()
        if step < half:
            send_step(step + 1)
            one, two = wrap(-step), wrap(step)
            load(one).start()
            load(two).start()
            load(one).wait()
            load(two).wait()
            add_pair(one, two)
        else:
            last = wrap(half)
            load(last).start()
            load(last).wait()
            add_single(last)

    for copy in started:
        copy.wait_send()

    def finish(k, carry):
        y = y_acc[k].reshape(rows, width, width)
        total = jnp.zeros((width, width), jnp.float32)
        for j in range(rows):
            def scan(s, acc):
                hit = (struct_ref[k, s] == base + j).astype(jnp.int32)
                return acc[0] + hit, acc[1] + hit * s
            hits, slot = lax.fori_loop(0, n, scan, (jnp.int32(0), jnp.int32(0)))
            slot = jnp.minimum(slot, n - 1)
            term = jnp.dot(jnp.transpose(u_vmem[slot, k]), y[j], precision=high,
                           preferred_element_type=jnp.float32)
            total = total + jnp.where(hits > 0, term, 0.0)
            zoff_ref[k, j] = jnp.where(hits > 0, -y[j], 0.0)
        part_ref[k] = total
        return carry

    lax.fori_loop(0, nodes, finish, 0)

    def share(offset):
        return pltpu.make_async_remote_copy(
            src_ref=part_ref.at[lax.rem(me + offset, n)], dst_ref=gather_buf.at[me],
            send_sem=out_sem.at[offset], recv_sem=in_sem.at[offset],
            device_id=(lax.rem(me + offset, n), col), device_id_type=pl.DeviceIdType.MESH)

    for offset in range(1, n):
        share(offset).start()
    gather_buf[me] = part_ref[me]
    for offset in range(1, n):
        share(offset).wait_send()
        share(offset).wait_recv()
    sum_ref[0] = jnp.sum(gather_buf[...], axis=0)


def fused_call(struct, base, sigma_rows, u_all, first, parts):
    slots, nodes, width, _ = u_all.shape
    rows = sigma_rows.shape[0]
    later = slots // 2 - first
    flops = 2 * nodes * slots * rows * width ** 3 * 3
    return pl.pallas_call(
        functools.partial(fused_kernel, first, parts),
        out_shape=[
            jax.ShapeDtypeStruct(u_all.shape, jnp.float32),
            jax.ShapeDtypeStruct((nodes, rows, width, width), jnp.float32),
            jax.ShapeDtypeStruct((1, width, width), jnp.float32),
        ],
        in_specs=[
            pl.BlockSpec(memory_space=pltpu.SMEM),
            pl.BlockSpec(memory_space=pltpu.SMEM),
            pl.BlockSpec(memory_space=pltpu.VMEM),
            pl.BlockSpec(memory_space=pl.ANY),
        ],
        out_specs=[
            pl.BlockSpec(memory_space=pl.ANY),
            pl.BlockSpec(memory_space=pltpu.VMEM),
            pl.BlockSpec(memory_space=pltpu.VMEM),
        ],
        scratch_shapes=[
            pltpu.VMEM(u_all.shape, jnp.float32),
            pltpu.VMEM((nodes, rows * width, width), jnp.float32),
            pltpu.VMEM((nodes, width, width), jnp.float32),
            pltpu.VMEM((slots, width, width), jnp.float32),
            pltpu.SemaphoreType.DMA((slots,)),
            pltpu.SemaphoreType.DMA((2, later, parts)),
            pltpu.SemaphoreType.DMA((2, later, parts)),
            pltpu.SemaphoreType.DMA((slots,)),
            pltpu.SemaphoreType.DMA((slots,)),
        ],
        input_output_aliases={3: 0},
        compiler_params=pltpu.CompilerParams(collective_id=1, has_side_effects=True,
                                             vmem_limit_bytes=60 * 1024 * 1024),
        cost_estimate=pl.CostEstimate(flops=flops, transcendentals=0,
                                      bytes_accessed=4 * (sigma_rows.size + u_all.size)),
    )(struct, base, sigma_rows, u_all)


def body(sigma_anc, factor, diag_inv, struct):
    row_count = sigma_anc.shape[0]
    row_index = lax.axis_index("row")
    base = jnp.reshape(row_index * row_count, (1,)).astype(jnp.int32)
    sigma_rows = lax.all_gather(sigma_anc, "col", axis=1, tiled=True)
    u_local = jnp.einsum("kij,kjl->kil", factor[0], diag_inv, precision=high)
    first, parts = 5, 4
    u_head = ring_gather(u_local, lax.axis_size("row"), first, parts)
    unused_u, z_off, summed = fused_call(struct, base, sigma_rows, u_head, first, parts)
    inverse_share = lax.dynamic_slice_in_dim(diag_inv, row_index, 1, 0)
    inverse_part = jnp.einsum("kij,kil->kjl", inverse_share, inverse_share, precision=high)
    return (z_off, inverse_part + summed)


def solution(mesh):
    in_specs = (
        P("row", "col", None, None),
        P("row", "col", None, None),
        P("col", None, None),
        P("col", None),
    )
    out_specs = (P("col", "row", None, None), P(("col", "row"), None, None))
    return jax.shard_map(body, mesh=mesh, in_specs=in_specs, out_specs=out_specs, check_vma=False)
```

```python
import functools

import jax
import jax.numpy as jnp
from jax import lax
from jax.experimental import pallas as pl
from jax.experimental.pallas import tpu as pltpu
from jax.sharding import PartitionSpec as P

high = lax.Precision.HIGH


def node_kernel(struct_ref, base_ref, sig_ref, u_ref, zoff_ref, part_ref, y_scr, part_scr):
    k = pl.program_id(0)
    slots = u_ref.shape[0]
    rows = sig_ref.shape[0]
    width = u_ref.shape[-1]
    base = base_ref[0]

    def slot_pair(i, acc):
        first = 2 * i
        second = first + 1
        lhs = jnp.concatenate(
            [sig_ref[:, struct_ref[k, first]].reshape(rows * width, width),
             sig_ref[:, struct_ref[k, second]].reshape(rows * width, width)], axis=1)
        rhs = jnp.concatenate([u_ref[first, 0], u_ref[second, 0]], axis=0)
        return acc + jnp.dot(lhs, rhs, precision=high, preferred_element_type=jnp.float32)

    acc = lax.fori_loop(0, slots // 2, slot_pair, jnp.zeros((rows * width, width), jnp.float32))
    y_scr[...] = acc.reshape(rows, width, width)
    part_scr[...] = jnp.zeros_like(part_scr)

    @pl.loop(0, slots)
    def _(s):
        a = struct_ref[k, s] - base

        @pl.when((a >= 0) & (a < rows))
        def _():
            ut = jnp.transpose(u_ref[s, 0])
            part_scr[...] += jnp.dot(ut, y_scr[a], precision=high, preferred_element_type=jnp.float32)

    part_ref[0] = part_scr[...]

    for j in range(rows):
        def count(s, c):
            return c + (struct_ref[k, s] == base + j).astype(jnp.int32)

        hits = lax.fori_loop(0, slots, count, jnp.int32(0))
        zoff_ref[0, j] = jnp.where(hits > 0, -y_scr[j], 0.0)


def node_call(struct, base, sigma_rows, u_all):
    slots, nodes, width, _ = u_all.shape
    rows = sigma_rows.shape[0]
    grid_spec = pltpu.PrefetchScalarGridSpec(
        num_scalar_prefetch=2,
        grid=(nodes,),
        in_specs=[
            pl.BlockSpec(memory_space=pltpu.VMEM),
            pl.BlockSpec((slots, 1, width, width), lambda k, st, bs: (0, k, 0, 0)),
        ],
        out_specs=[
            pl.BlockSpec((1, rows, width, width), lambda k, st, bs: (k, 0, 0, 0)),
            pl.BlockSpec((1, width, width), lambda k, st, bs: (k, 0, 0)),
        ],
        scratch_shapes=[
            pltpu.VMEM((rows, width, width), jnp.float32),
            pltpu.VMEM((width, width), jnp.float32),
        ],
    )
    flops = 2 * nodes * slots * rows * width ** 3 * 3
    return pl.pallas_call(
        node_kernel,
        grid_spec=grid_spec,
        out_shape=[
            jax.ShapeDtypeStruct((nodes, rows, width, width), jnp.float32),
            jax.ShapeDtypeStruct((nodes, width, width), jnp.float32),
        ],
        compiler_params=pltpu.CompilerParams(vmem_limit_bytes=48 * 1024 * 1024),
        cost_estimate=pl.CostEstimate(flops=flops, transcendentals=0,
                                      bytes_accessed=4 * (sigma_rows.size + u_all.size + 2 * nodes * rows * width * width)),
    )(struct, base, sigma_rows, u_all)


def greet_neighbours(me, col, n):
    barrier = pltpu.get_barrier_semaphore()
    for peer in (lax.rem(me + n - 1, n), lax.rem(me + 1, n)):
        pl.semaphore_signal(barrier, inc=1, device_id=(peer, col), device_id_type=pl.DeviceIdType.MESH)
    pl.semaphore_wait(barrier, 2)


def step_parts(step, direction, half, parts):
    if step < half:
        return range(parts)
    if direction == 0:
        return range(parts // 2)
    return range(parts // 2, parts)


def ring_kernel(steps, parts, u_ref, out_ref, copy_sem, send_sem, recv_sem):
    n = out_ref.shape[0]
    chunk = out_ref.shape[1] // parts
    me = lax.axis_index("row")
    col = lax.axis_index("col")

    def link(step, direction, part):
        if direction == 0:
            slot = lax.rem(me - (step - 1) + n, n)
            peer = lax.rem(me + 1, n)
        else:
            slot = lax.rem(me + (step - 1), n)
            peer = lax.rem(me + n - 1, n)
        piece = pl.ds(part * chunk, chunk)
        return pltpu.make_async_remote_copy(
            src_ref=out_ref.at[slot, piece], dst_ref=out_ref.at[slot, piece],
            send_sem=send_sem.at[direction, step - 1, part],
            recv_sem=recv_sem.at[direction, step - 1, part],
            device_id=(peer, col), device_id_type=pl.DeviceIdType.MESH)

    own = pltpu.make_async_copy(u_ref, out_ref.at[me], copy_sem.at[0])
    own.start()
    greet_neighbours(me, col, n)
    own.wait()

    started = []
    for step in range(1, steps + 1):
        for direction in (0, 1):
            for part in range(parts):
                if step > 1:
                    link(step - 1, direction, part).wait_recv()
                copy = link(step, direction, part)
                copy.start()
                started.append(copy)
    for direction in (0, 1):
        for part in range(parts):
            link(steps, direction, part).wait_recv()
    for copy in started:
        copy.wait_send()


def ring_gather(u_local, slots, steps, parts):
    nodes, width, _ = u_local.shape
    return pl.pallas_call(
        functools.partial(ring_kernel, steps, parts),
        out_shape=jax.ShapeDtypeStruct((slots, nodes, width, width), jnp.float32),
        in_specs=[pl.BlockSpec(memory_space=pl.ANY)],
        out_specs=pl.BlockSpec(memory_space=pl.ANY),
        scratch_shapes=[
            pltpu.SemaphoreType.DMA((1,)),
            pltpu.SemaphoreType.DMA((2, steps, parts)),
            pltpu.SemaphoreType.DMA((2, steps, parts)),
        ],
        compiler_params=pltpu.CompilerParams(collective_id=0, has_side_effects=True),
    )(u_local)


def fused_kernel(first, parts, struct_ref, base_ref, sig_ref, u_in, u_out, zoff_ref, sum_ref,
                 u_vmem, y_acc, part_ref, gather_buf, load_sem, send_sem, recv_sem, out_sem, in_sem):
    n = u_out.shape[0]
    half = n // 2
    nodes = u_out.shape[1]
    chunk = nodes // parts
    rows = sig_ref.shape[0]
    width = sig_ref.shape[-1]
    me = lax.axis_index("row")
    col = lax.axis_index("col")
    base = base_ref[0]

    def link(step, direction, part):
        if direction == 0:
            slot = lax.rem(me - (step - 1) + n, n)
            peer = lax.rem(me + 1, n)
        else:
            slot = lax.rem(me + (step - 1), n)
            peer = lax.rem(me + n - 1, n)
        piece = pl.ds(part * chunk, chunk)
        return pltpu.make_async_remote_copy(
            src_ref=u_out.at[slot, piece], dst_ref=u_out.at[slot, piece],
            send_sem=send_sem.at[direction, step - 1 - first, part],
            recv_sem=recv_sem.at[direction, step - 1 - first, part],
            device_id=(peer, col), device_id_type=pl.DeviceIdType.MESH)

    def load(slot):
        return pltpu.make_async_copy(u_out.at[slot], u_vmem.at[slot], load_sem.at[slot])

    def wrap(offset):
        return lax.rem(me + offset + 2 * n, n)

    barrier = pltpu.get_barrier_semaphore()
    for offset in range(1, n):
        pl.semaphore_signal(barrier, inc=1, device_id=(lax.rem(me + offset, n), col),
                            device_id_type=pl.DeviceIdType.MESH)
    pl.semaphore_wait(barrier, n - 1)
    for offset in range(-first, first + 1):
        load(wrap(offset)).start()

    started = []

    def send_step(step):
        for direction in (0, 1):
            for part in step_parts(step, direction, half, parts):
                copy = link(step, direction, part)
                copy.start()
                started.append(copy)

    send_step(first + 1)

    def lhs_block(k, slot):
        return sig_ref[:, struct_ref[k, slot]].reshape(rows * width, width)

    def add_single(slot):
        def node(k, carry):
            y_acc[k] += jnp.dot(lhs_block(k, slot), u_vmem[slot, k], precision=high,
                                preferred_element_type=jnp.float32)
            return carry
        lax.fori_loop(0, nodes, node, 0)

    def add_pair(one, two):
        def node(k, carry):
            lhs = jnp.concatenate([lhs_block(k, one), lhs_block(k, two)], axis=1)
            rhs = jnp.concatenate([u_vmem[one, k], u_vmem[two, k]], axis=0)
            y_acc[k] += jnp.dot(lhs, rhs, precision=high, preferred_element_type=jnp.float32)
            return carry
        lax.fori_loop(0, nodes, node, 0)

    def ring_event(step):
        for direction in (0, 1):
            for part in step_parts(step, direction, half, parts):
                link(step, direction, part).wait_recv()
        if step < half:
            send_step(step + 1)
            load(wrap(-step)).start()
            load(wrap(step)).start()
        else:
            load(wrap(half)).start()

    def arrived(step):
        if step < half:
            one, two = wrap(-step), wrap(step)
            load(one).wait()
            load(two).wait()
            add_pair(one, two)
        else:
            last = wrap(half)
            load(last).wait()
            add_single(last)

    processed = first
    load(me).wait()
    y_acc[...] = jnp.zeros_like(y_acc)
    add_single(me)
    for offset in range(1, first + 1):
        load(wrap(-offset)).wait()
        load(wrap(offset)).wait()
        add_pair(wrap(-offset), wrap(offset))
        if offset % 2 == 0 and processed < half:
            processed += 1
            ring_event(processed)
    done = first + 1
    while done <= half:
        if done <= processed:
            arrived(done)
            done += 1
        else:
            processed += 1
            ring_event(processed)

    for copy in started:
        copy.wait_send()

    def share_to(k):
        return pltpu.make_async_remote_copy(
            src_ref=part_ref.at[k], dst_ref=gather_buf.at[me],
            send_sem=out_sem.at[k], recv_sem=in_sem.at[me],
            device_id=(k, col), device_id_type=pl.DeviceIdType.MESH)

    def share_from(j):
        return pltpu.make_async_remote_copy(
            src_ref=part_ref.at[j], dst_ref=gather_buf.at[j],
            send_sem=out_sem.at[j], recv_sem=in_sem.at[j],
            device_id=(j, col), device_id_type=pl.DeviceIdType.MESH)

    def finish(k, carry):
        y = y_acc[k].reshape(rows, width, width)
        total = jnp.zeros((width, width), jnp.float32)
        for j in range(rows):
            def scan(s, acc):
                hit = (struct_ref[k, s] == base + j).astype(jnp.int32)
                return acc[0] + hit, acc[1] + hit * s
            hits, slot = lax.fori_loop(0, n, scan, (jnp.int32(0), jnp.int32(0)))
            slot = jnp.minimum(slot, n - 1)
            term = jnp.dot(jnp.transpose(u_vmem[slot, k]), y[j], precision=high,
                           preferred_element_type=jnp.float32)
            total = total + jnp.where(hits > 0, term, 0.0)
            zoff_ref[k, j] = jnp.where(hits > 0, -y[j], 0.0)
        part_ref[k] = total

        @pl.when((k >= 1) & (k - 1 != me))
        def _():
            share_to(k - 1).start()

        return carry

    lax.fori_loop(0, nodes, finish, 0)

    @pl.when(me != nodes - 1)
    def _():
        share_to(nodes - 1).start()

    gather_buf[me] = part_ref[me]
    for j in range(n):
        @pl.when(me != j)
        def _():
            share_to(j).wait_send()
            share_from(j).wait_recv()

    sum_ref[0] = jnp.sum(gather_buf[...], axis=0)


def fused_call(struct, base, sigma_rows, u_all, first, parts):
    slots, nodes, width, _ = u_all.shape
    rows = sigma_rows.shape[0]
    later = slots // 2 - first
    flops = 2 * nodes * slots * rows * width ** 3 * 3
    return pl.pallas_call(
        functools.partial(fused_kernel, first, parts),
        out_shape=[
            jax.ShapeDtypeStruct(u_all.shape, jnp.float32),
            jax.ShapeDtypeStruct((nodes, rows, width, width), jnp.float32),
            jax.ShapeDtypeStruct((1, width, width), jnp.float32),
        ],
        in_specs=[
            pl.BlockSpec(memory_space=pltpu.SMEM),
            pl.BlockSpec(memory_space=pltpu.SMEM),
            pl.BlockSpec(memory_space=pltpu.VMEM),
            pl.BlockSpec(memory_space=pl.ANY),
        ],
        out_specs=[
            pl.BlockSpec(memory_space=pl.ANY),
            pl.BlockSpec(memory_space=pltpu.VMEM),
            pl.BlockSpec(memory_space=pltpu.VMEM),
        ],
        scratch_shapes=[
            pltpu.VMEM(u_all.shape, jnp.float32),
            pltpu.VMEM((nodes, rows * width, width), jnp.float32),
            pltpu.VMEM((nodes, width, width), jnp.float32),
            pltpu.VMEM((slots, width, width), jnp.float32),
            pltpu.SemaphoreType.DMA((slots,)),
            pltpu.SemaphoreType.DMA((2, later, parts)),
            pltpu.SemaphoreType.DMA((2, later, parts)),
            pltpu.SemaphoreType.DMA((slots,)),
            pltpu.SemaphoreType.DMA((slots,)),
        ],
        input_output_aliases={3: 0},
        compiler_params=pltpu.CompilerParams(collective_id=1, has_side_effects=True,
                                             vmem_limit_bytes=60 * 1024 * 1024),
        cost_estimate=pl.CostEstimate(flops=flops, transcendentals=0,
                                      bytes_accessed=4 * (sigma_rows.size + u_all.size)),
    )(struct, base, sigma_rows, u_all)


def body(sigma_anc, factor, diag_inv, struct):
    row_count = sigma_anc.shape[0]
    row_index = lax.axis_index("row")
    base = jnp.reshape(row_index * row_count, (1,)).astype(jnp.int32)
    sigma_rows = lax.all_gather(sigma_anc, "col", axis=1, tiled=True)
    u_local = jnp.einsum("kij,kjl->kil", factor[0], diag_inv, precision=high)
    first, parts = 5, 4
    u_head = ring_gather(u_local, lax.axis_size("row"), first, parts)
    unused_u, z_off, summed = fused_call(struct, base, sigma_rows, u_head, first, parts)
    inverse_share = lax.dynamic_slice_in_dim(diag_inv, row_index, 1, 0)
    inverse_part = jnp.einsum("kij,kil->kjl", inverse_share, inverse_share, precision=high)
    return (z_off, inverse_part + summed)


def solution(mesh):
    in_specs = (
        P("row", "col", None, None),
        P("row", "col", None, None),
        P("col", None, None),
        P("col", None),
    )
    out_specs = (P("col", "row", None, None), P(("col", "row"), None, None))
    return jax.shard_map(body, mesh=mesh, in_specs=in_specs, out_specs=out_specs, check_vma=False)
```

```python
import functools

import jax
import jax.numpy as jnp
from jax import lax
from jax.experimental import pallas as pl
from jax.experimental.pallas import tpu as pltpu
from jax.sharding import PartitionSpec as P

high = lax.Precision.HIGH


def node_kernel(struct_ref, base_ref, sig_ref, u_ref, zoff_ref, part_ref, y_scr, part_scr):
    k = pl.program_id(0)
    slots = u_ref.shape[0]
    rows = sig_ref.shape[0]
    width = u_ref.shape[-1]
    base = base_ref[0]

    def slot_pair(i, acc):
        first = 2 * i
        second = first + 1
        lhs = jnp.concatenate(
            [sig_ref[:, struct_ref[k, first]].reshape(rows * width, width),
             sig_ref[:, struct_ref[k, second]].reshape(rows * width, width)], axis=1)
        rhs = jnp.concatenate([u_ref[first, 0], u_ref[second, 0]], axis=0)
        return acc + jnp.dot(lhs, rhs, precision=high, preferred_element_type=jnp.float32)

    acc = lax.fori_loop(0, slots // 2, slot_pair, jnp.zeros((rows * width, width), jnp.float32))
    y_scr[...] = acc.reshape(rows, width, width)
    part_scr[...] = jnp.zeros_like(part_scr)

    @pl.loop(0, slots)
    def _(s):
        a = struct_ref[k, s] - base

        @pl.when((a >= 0) & (a < rows))
        def _():
            ut = jnp.transpose(u_ref[s, 0])
            part_scr[...] += jnp.dot(ut, y_scr[a], precision=high, preferred_element_type=jnp.float32)

    part_ref[0] = part_scr[...]

    for j in range(rows):
        def count(s, c):
            return c + (struct_ref[k, s] == base + j).astype(jnp.int32)

        hits = lax.fori_loop(0, slots, count, jnp.int32(0))
        zoff_ref[0, j] = jnp.where(hits > 0, -y_scr[j], 0.0)


def node_call(struct, base, sigma_rows, u_all):
    slots, nodes, width, _ = u_all.shape
    rows = sigma_rows.shape[0]
    grid_spec = pltpu.PrefetchScalarGridSpec(
        num_scalar_prefetch=2,
        grid=(nodes,),
        in_specs=[
            pl.BlockSpec(memory_space=pltpu.VMEM),
            pl.BlockSpec((slots, 1, width, width), lambda k, st, bs: (0, k, 0, 0)),
        ],
        out_specs=[
            pl.BlockSpec((1, rows, width, width), lambda k, st, bs: (k, 0, 0, 0)),
            pl.BlockSpec((1, width, width), lambda k, st, bs: (k, 0, 0)),
        ],
        scratch_shapes=[
            pltpu.VMEM((rows, width, width), jnp.float32),
            pltpu.VMEM((width, width), jnp.float32),
        ],
    )
    flops = 2 * nodes * slots * rows * width ** 3 * 3
    return pl.pallas_call(
        node_kernel,
        grid_spec=grid_spec,
        out_shape=[
            jax.ShapeDtypeStruct((nodes, rows, width, width), jnp.float32),
            jax.ShapeDtypeStruct((nodes, width, width), jnp.float32),
        ],
        compiler_params=pltpu.CompilerParams(vmem_limit_bytes=48 * 1024 * 1024),
        cost_estimate=pl.CostEstimate(flops=flops, transcendentals=0,
                                      bytes_accessed=4 * (sigma_rows.size + u_all.size + 2 * nodes * rows * width * width)),
    )(struct, base, sigma_rows, u_all)


def greet_neighbours(me, col, n):
    barrier = pltpu.get_barrier_semaphore()
    for peer in (lax.rem(me + n - 1, n), lax.rem(me + 1, n)):
        pl.semaphore_signal(barrier, inc=1, device_id=(peer, col), device_id_type=pl.DeviceIdType.MESH)
    pl.semaphore_wait(barrier, 2)


def step_parts(step, direction, half, parts):
    if step < half:
        return range(parts)
    if direction == 0:
        return range(parts // 2)
    return range(parts // 2, parts)


def ring_kernel(steps, parts, u_ref, out_ref, copy_sem, send_sem, recv_sem):
    n = out_ref.shape[0]
    chunk = out_ref.shape[1] // parts
    me = lax.axis_index("row")
    col = lax.axis_index("col")

    def link(step, direction, part):
        if direction == 0:
            slot = lax.rem(me - (step - 1) + n, n)
            peer = lax.rem(me + 1, n)
        else:
            slot = lax.rem(me + (step - 1), n)
            peer = lax.rem(me + n - 1, n)
        piece = pl.ds(part * chunk, chunk)
        return pltpu.make_async_remote_copy(
            src_ref=out_ref.at[slot, piece], dst_ref=out_ref.at[slot, piece],
            send_sem=send_sem.at[direction, step - 1, part],
            recv_sem=recv_sem.at[direction, step - 1, part],
            device_id=(peer, col), device_id_type=pl.DeviceIdType.MESH)

    own = pltpu.make_async_copy(u_ref, out_ref.at[me], copy_sem.at[0])
    own.start()
    greet_neighbours(me, col, n)
    own.wait()

    started = []
    for step in range(1, steps + 1):
        for direction in (0, 1):
            for part in range(parts):
                if step > 1:
                    link(step - 1, direction, part).wait_recv()
                copy = link(step, direction, part)
                copy.start()
                started.append(copy)
    for direction in (0, 1):
        for part in range(parts):
            link(steps, direction, part).wait_recv()
    for copy in started:
        copy.wait_send()


def ring_gather(u_local, slots, steps, parts):
    nodes, width, _ = u_local.shape
    return pl.pallas_call(
        functools.partial(ring_kernel, steps, parts),
        out_shape=jax.ShapeDtypeStruct((slots, nodes, width, width), jnp.float32),
        in_specs=[pl.BlockSpec(memory_space=pl.ANY)],
        out_specs=pl.BlockSpec(memory_space=pl.ANY),
        scratch_shapes=[
            pltpu.SemaphoreType.DMA((1,)),
            pltpu.SemaphoreType.DMA((2, steps, parts)),
            pltpu.SemaphoreType.DMA((2, steps, parts)),
        ],
        compiler_params=pltpu.CompilerParams(collective_id=0, has_side_effects=True),
    )(u_local)


def fused_kernel(first, parts, struct_ref, base_ref, sig_ref, u_in, u_out, zoff_ref, sum_ref,
                 u_vmem, y_acc, part_ref, gather_buf, load_sem, send_sem, recv_sem, out_sem, in_sem):
    n = u_out.shape[0]
    half = n // 2
    nodes = u_out.shape[1]
    chunk = nodes // parts
    rows = sig_ref.shape[0]
    width = sig_ref.shape[-1]
    me = lax.axis_index("row")
    col = lax.axis_index("col")
    base = base_ref[0]

    def link(step, direction, part):
        if direction == 0:
            slot = lax.rem(me - (step - 1) + n, n)
            peer = lax.rem(me + 1, n)
        else:
            slot = lax.rem(me + (step - 1), n)
            peer = lax.rem(me + n - 1, n)
        piece = pl.ds(part * chunk, chunk)
        return pltpu.make_async_remote_copy(
            src_ref=u_out.at[slot, piece], dst_ref=u_out.at[slot, piece],
            send_sem=send_sem.at[direction, step - 1 - first, part],
            recv_sem=recv_sem.at[direction, step - 1 - first, part],
            device_id=(peer, col), device_id_type=pl.DeviceIdType.MESH)

    def load(slot):
        return pltpu.make_async_copy(u_out.at[slot], u_vmem.at[slot], load_sem.at[slot])

    def wrap(offset):
        return lax.rem(me + offset + 2 * n, n)

    barrier = pltpu.get_barrier_semaphore()
    for offset in range(1, n):
        pl.semaphore_signal(barrier, inc=1, device_id=(lax.rem(me + offset, n), col),
                            device_id_type=pl.DeviceIdType.MESH)
    pl.semaphore_wait(barrier, n - 1)
    for offset in range(-first, first + 1):
        load(wrap(offset)).start()

    started = []

    def send_step(step):
        for direction in (0, 1):
            for part in step_parts(step, direction, half, parts):
                copy = link(step, direction, part)
                copy.start()
                started.append(copy)

    send_step(first + 1)

    def lhs_block(k, slot):
        return sig_ref[:, struct_ref[k, slot]].reshape(rows * width, width)

    def add_single(slot):
        def node(k, carry):
            y_acc[k] += jnp.dot(lhs_block(k, slot), u_vmem[slot, k], precision=high,
                                preferred_element_type=jnp.float32)
            return carry
        lax.fori_loop(0, nodes, node, 0)

    def add_pair(one, two):
        def node(k, carry):
            lhs = jnp.concatenate([lhs_block(k, one), lhs_block(k, two)], axis=1)
            rhs = jnp.concatenate([u_vmem[one, k], u_vmem[two, k]], axis=0)
            y_acc[k] += jnp.dot(lhs, rhs, precision=high, preferred_element_type=jnp.float32)
            return carry
        lax.fori_loop(0, nodes, node, 0)

    def ring_event(step):
        for direction in (0, 1):
            for part in step_parts(step, direction, half, parts):
                link(step, direction, part).wait_recv()
        if step < half:
            send_step(step + 1)
            load(wrap(-step)).start()
            load(wrap(step)).start()
        else:
            load(wrap(half)).start()

    def arrived(step):
        if step < half:
            one, two = wrap(-step), wrap(step)
            load(one).wait()
            load(two).wait()
            add_pair(one, two)
        else:
            last = wrap(half)
            load(last).wait()
            add_single(last)

    processed = first
    load(me).wait()
    y_acc[...] = jnp.zeros_like(y_acc)
    add_single(me)
    for offset in range(1, first + 1):
        load(wrap(-offset)).wait()
        load(wrap(offset)).wait()
        add_pair(wrap(-offset), wrap(offset))
        if offset % 2 == 0 and processed < half:
            processed += 1
            ring_event(processed)
    done = first + 1
    while done <= half:
        if done <= processed:
            arrived(done)
            done += 1
        else:
            processed += 1
            ring_event(processed)

    for copy in started:
        copy.wait_send()

    def share_to(k):
        return pltpu.make_async_remote_copy(
            src_ref=part_ref.at[k], dst_ref=gather_buf.at[me],
            send_sem=out_sem.at[k], recv_sem=in_sem.at[me],
            device_id=(k, col), device_id_type=pl.DeviceIdType.MESH)

    def share_from(j):
        return pltpu.make_async_remote_copy(
            src_ref=part_ref.at[j], dst_ref=gather_buf.at[j],
            send_sem=out_sem.at[j], recv_sem=in_sem.at[j],
            device_id=(j, col), device_id_type=pl.DeviceIdType.MESH)

    def finish(k, carry):
        y = y_acc[k].reshape(rows, width, width)
        total = jnp.zeros((width, width), jnp.float32)
        for j in range(rows):
            def scan(s, acc):
                hit = (struct_ref[k, s] == base + j).astype(jnp.int32)
                return acc[0] + hit, acc[1] + hit * s
            hits, slot = lax.fori_loop(0, n, scan, (jnp.int32(0), jnp.int32(0)))
            slot = jnp.minimum(slot, n - 1)
            term = jnp.dot(jnp.transpose(u_vmem[slot, k]), y[j], precision=high,
                           preferred_element_type=jnp.float32)
            total = total + jnp.where(hits > 0, term, 0.0)
            zoff_ref[k, j] = jnp.where(hits > 0, -y[j], 0.0)
        part_ref[k] = total

        @pl.when((k >= 1) & (k - 1 != me))
        def _():
            share_to(k - 1).start()

        return carry

    lax.fori_loop(0, nodes, finish, 0)

    @pl.when(me != nodes - 1)
    def _():
        share_to(nodes - 1).start()

    gather_buf[me] = part_ref[me]
    for j in range(n):
        @pl.when(me != j)
        def _():
            share_to(j).wait_send()
            share_from(j).wait_recv()

    sum_ref[0] = jnp.sum(gather_buf[...], axis=0)


def fused_call(struct, base, sigma_rows, u_all, first, parts):
    slots, nodes, width, _ = u_all.shape
    rows = sigma_rows.shape[0]
    later = slots // 2 - first
    flops = 2 * nodes * slots * rows * width ** 3 * 3
    return pl.pallas_call(
        functools.partial(fused_kernel, first, parts),
        out_shape=[
            jax.ShapeDtypeStruct(u_all.shape, jnp.float32),
            jax.ShapeDtypeStruct((nodes, rows, width, width), jnp.float32),
            jax.ShapeDtypeStruct((1, width, width), jnp.float32),
        ],
        in_specs=[
            pl.BlockSpec(memory_space=pltpu.SMEM),
            pl.BlockSpec(memory_space=pltpu.SMEM),
            pl.BlockSpec(memory_space=pltpu.VMEM),
            pl.BlockSpec(memory_space=pl.ANY),
        ],
        out_specs=[
            pl.BlockSpec(memory_space=pl.ANY),
            pl.BlockSpec(memory_space=pltpu.VMEM),
            pl.BlockSpec(memory_space=pltpu.VMEM),
        ],
        scratch_shapes=[
            pltpu.VMEM(u_all.shape, jnp.float32),
            pltpu.VMEM((nodes, rows * width, width), jnp.float32),
            pltpu.VMEM((nodes, width, width), jnp.float32),
            pltpu.VMEM((slots, width, width), jnp.float32),
            pltpu.SemaphoreType.DMA((slots,)),
            pltpu.SemaphoreType.DMA((2, later, parts)),
            pltpu.SemaphoreType.DMA((2, later, parts)),
            pltpu.SemaphoreType.DMA((slots,)),
            pltpu.SemaphoreType.DMA((slots,)),
        ],
        input_output_aliases={3: 0},
        compiler_params=pltpu.CompilerParams(collective_id=1, has_side_effects=True,
                                             vmem_limit_bytes=60 * 1024 * 1024),
        cost_estimate=pl.CostEstimate(flops=flops, transcendentals=0,
                                      bytes_accessed=4 * (sigma_rows.size + u_all.size)),
    )(struct, base, sigma_rows, u_all)


def body(sigma_anc, factor, diag_inv, struct):
    row_count = sigma_anc.shape[0]
    row_index = lax.axis_index("row")
    base = jnp.reshape(row_index * row_count, (1,)).astype(jnp.int32)
    sigma_rows = lax.all_gather(sigma_anc, "col", axis=1, tiled=True)
    u_local = jnp.einsum("kij,kjl->kil", factor[0], diag_inv, precision=high)
    first, parts = 4, 4
    u_head = ring_gather(u_local, lax.axis_size("row"), first, parts)
    unused_u, z_off, summed = fused_call(struct, base, sigma_rows, u_head, first, parts)
    inverse_share = lax.dynamic_slice_in_dim(diag_inv, row_index, 1, 0)
    inverse_part = jnp.einsum("kij,kil->kjl", inverse_share, inverse_share, precision=high)
    return (z_off, inverse_part + summed)


def solution(mesh):
    in_specs = (
        P("row", "col", None, None),
        P("row", "col", None, None),
        P("col", None, None),
        P("col", None),
    )
    out_specs = (P("col", "row", None, None), P(("col", "row"), None, None))
    return jax.shard_map(body, mesh=mesh, in_specs=in_specs, out_specs=out_specs, check_vma=False)
```

```python
import functools

import jax
import jax.numpy as jnp
from jax import lax
from jax.experimental import pallas as pl
from jax.experimental.pallas import tpu as pltpu
from jax.sharding import PartitionSpec as P

high = lax.Precision.HIGH


def greet_neighbours(me, col, n):
    barrier = pltpu.get_barrier_semaphore()
    for peer in (lax.rem(me + n - 1, n), lax.rem(me + 1, n)):
        pl.semaphore_signal(barrier, inc=1, device_id=(peer, col), device_id_type=pl.DeviceIdType.MESH)
    pl.semaphore_wait(barrier, 2)


def step_parts(step, direction, half, parts):
    if step < half:
        return range(parts)
    if direction == 0:
        return range(parts // 2)
    return range(parts // 2, parts)


def ring_kernel(steps, parts, u_ref, out_ref, copy_sem, send_sem, recv_sem):
    n = out_ref.shape[0]
    chunk = out_ref.shape[1] // parts
    me = lax.axis_index("row")
    col = lax.axis_index("col")

    def link(step, direction, part):
        if direction == 0:
            slot = lax.rem(me - (step - 1) + n, n)
            peer = lax.rem(me + 1, n)
        else:
            slot = lax.rem(me + (step - 1), n)
            peer = lax.rem(me + n - 1, n)
        piece = pl.ds(part * chunk, chunk)
        return pltpu.make_async_remote_copy(
            src_ref=out_ref.at[slot, piece], dst_ref=out_ref.at[slot, piece],
            send_sem=send_sem.at[direction, step - 1, part],
            recv_sem=recv_sem.at[direction, step - 1, part],
            device_id=(peer, col), device_id_type=pl.DeviceIdType.MESH)

    own = pltpu.make_async_copy(u_ref, out_ref.at[me], copy_sem.at[0])
    own.start()
    greet_neighbours(me, col, n)
    own.wait()

    started = []
    for step in range(1, steps + 1):
        for direction in (0, 1):
            for part in range(parts):
                if step > 1:
                    link(step - 1, direction, part).wait_recv()
                copy = link(step, direction, part)
                copy.start()
                started.append(copy)
    for direction in (0, 1):
        for part in range(parts):
            link(steps, direction, part).wait_recv()
    for copy in started:
        copy.wait_send()


def ring_gather(u_local, slots, steps, parts):
    nodes, width, _ = u_local.shape
    return pl.pallas_call(
        functools.partial(ring_kernel, steps, parts),
        out_shape=jax.ShapeDtypeStruct((slots, nodes, width, width), jnp.float32),
        in_specs=[pl.BlockSpec(memory_space=pl.ANY)],
        out_specs=pl.BlockSpec(memory_space=pl.ANY),
        scratch_shapes=[
            pltpu.SemaphoreType.DMA((1,)),
            pltpu.SemaphoreType.DMA((2, steps, parts)),
            pltpu.SemaphoreType.DMA((2, steps, parts)),
        ],
        compiler_params=pltpu.CompilerParams(collective_id=0, has_side_effects=True),
    )(u_local)


def fused_kernel(first, parts, struct_ref, hit_ref, slot_ref, sig_ref, u_in, u_out, zoff_ref, sum_ref,
                 u_vmem, y_acc, part_ref, gather_buf, load_sem, send_sem, recv_sem, out_sem, in_sem):
    n = u_out.shape[0]
    half = n // 2
    nodes = u_out.shape[1]
    chunk = nodes // parts
    rows = sig_ref.shape[0]
    width = sig_ref.shape[-1]
    me = lax.axis_index("row")
    col = lax.axis_index("col")

    def link(step, direction, part):
        if direction == 0:
            slot = lax.rem(me - (step - 1) + n, n)
            peer = lax.rem(me + 1, n)
        else:
            slot = lax.rem(me + (step - 1), n)
            peer = lax.rem(me + n - 1, n)
        piece = pl.ds(part * chunk, chunk)
        return pltpu.make_async_remote_copy(
            src_ref=u_out.at[slot, piece], dst_ref=u_out.at[slot, piece],
            send_sem=send_sem.at[direction, step - 1 - first, part],
            recv_sem=recv_sem.at[direction, step - 1 - first, part],
            device_id=(peer, col), device_id_type=pl.DeviceIdType.MESH)

    def load(slot):
        return pltpu.make_async_copy(u_out.at[slot], u_vmem.at[slot], load_sem.at[slot])

    def wrap(offset):
        return lax.rem(me + offset + 2 * n, n)

    barrier = pltpu.get_barrier_semaphore()
    for offset in range(1, n):
        pl.semaphore_signal(barrier, inc=1, device_id=(lax.rem(me + offset, n), col),
                            device_id_type=pl.DeviceIdType.MESH)
    pl.semaphore_wait(barrier, n - 1)
    for offset in range(-first, first + 1):
        load(wrap(offset)).start()

    started = []

    def send_step(step):
        for direction in (0, 1):
            for part in step_parts(step, direction, half, parts):
                copy = link(step, direction, part)
                copy.start()
                started.append(copy)

    send_step(first + 1)

    def lhs_block(k, slot):
        return sig_ref[:, struct_ref[k, slot]].reshape(rows * width, width)

    def add_single(slot):
        def node(k, carry):
            y_acc[k] += jnp.dot(lhs_block(k, slot), u_vmem[slot, k], precision=high,
                                preferred_element_type=jnp.float32)
            return carry
        lax.fori_loop(0, nodes, node, 0)

    def add_pair(one, two):
        def node(k, carry):
            lhs = jnp.concatenate([lhs_block(k, one), lhs_block(k, two)], axis=1)
            rhs = jnp.concatenate([u_vmem[one, k], u_vmem[two, k]], axis=0)
            y_acc[k] += jnp.dot(lhs, rhs, precision=high, preferred_element_type=jnp.float32)
            return carry
        lax.fori_loop(0, nodes, node, 0)

    def ring_event(step):
        for direction in (0, 1):
            for part in step_parts(step, direction, half, parts):
                link(step, direction, part).wait_recv()
        if step < half:
            send_step(step + 1)
            load(wrap(-step)).start()
            load(wrap(step)).start()
        else:
            load(wrap(half)).start()

    def arrived(step):
        if step < half:
            one, two = wrap(-step), wrap(step)
            load(one).wait()
            load(two).wait()
            add_pair(one, two)
        else:
            last = wrap(half)
            load(last).wait()
            add_single(last)

    processed = first
    load(me).wait()
    y_acc[...] = jnp.zeros_like(y_acc)
    add_single(me)
    for offset in range(1, first + 1):
        load(wrap(-offset)).wait()
        load(wrap(offset)).wait()
        add_pair(wrap(-offset), wrap(offset))
        if offset % 2 == 0 and processed < half:
            processed += 1
            ring_event(processed)
    done = first + 1
    while done < half:
        if done <= processed:
            arrived(done)
            done += 1
        else:
            processed += 1
            ring_event(processed)
    while processed < half:
        processed += 1
        ring_event(processed)
    last = wrap(half)
    load(last).wait()

    for copy in started:
        copy.wait_send()

    def share_to(k):
        return pltpu.make_async_remote_copy(
            src_ref=part_ref.at[k], dst_ref=gather_buf.at[me],
            send_sem=out_sem.at[k], recv_sem=in_sem.at[me],
            device_id=(k, col), device_id_type=pl.DeviceIdType.MESH)

    def share_from(j):
        return pltpu.make_async_remote_copy(
            src_ref=part_ref.at[j], dst_ref=gather_buf.at[j],
            send_sem=out_sem.at[j], recv_sem=in_sem.at[j],
            device_id=(j, col), device_id_type=pl.DeviceIdType.MESH)

    def finish(k, carry):
        y = y_acc[k] + jnp.dot(lhs_block(k, last), u_vmem[last, k], precision=high,
                               preferred_element_type=jnp.float32)
        y = y.reshape(rows, width, width)
        total = jnp.zeros((width, width), jnp.float32)
        for j in range(rows):
            hits = hit_ref[k, j]
            slot = jnp.minimum(slot_ref[k, j], n - 1)
            term = jnp.dot(jnp.transpose(u_vmem[slot, k]), y[j], precision=high,
                           preferred_element_type=jnp.float32)
            total = total + jnp.where(hits > 0, term, 0.0)
            zoff_ref[k, j] = jnp.where(hits > 0, -y[j], 0.0)
        part_ref[k] = total

        @pl.when((k >= 1) & (k - 1 != me))
        def _():
            share_to(k - 1).start()

        return carry

    lax.fori_loop(0, nodes, finish, 0)

    @pl.when(me != nodes - 1)
    def _():
        share_to(nodes - 1).start()

    gather_buf[me] = part_ref[me]
    for j in range(n):
        @pl.when(me != j)
        def _():
            share_to(j).wait_send()
            share_from(j).wait_recv()

    sum_ref[0] = jnp.sum(gather_buf[...], axis=0)


def fused_call(struct, hit, slot, sigma_rows, u_all, first, parts):
    slots, nodes, width, _ = u_all.shape
    rows = sigma_rows.shape[0]
    later = slots // 2 - first
    flops = 2 * nodes * slots * rows * width ** 3 * 3
    return pl.pallas_call(
        functools.partial(fused_kernel, first, parts),
        out_shape=[
            jax.ShapeDtypeStruct(u_all.shape, jnp.float32),
            jax.ShapeDtypeStruct((nodes, rows, width, width), jnp.float32),
            jax.ShapeDtypeStruct((1, width, width), jnp.float32),
        ],
        in_specs=[
            pl.BlockSpec(memory_space=pltpu.SMEM),
            pl.BlockSpec(memory_space=pltpu.SMEM),
            pl.BlockSpec(memory_space=pltpu.SMEM),
            pl.BlockSpec(memory_space=pltpu.VMEM),
            pl.BlockSpec(memory_space=pl.ANY),
        ],
        out_specs=[
            pl.BlockSpec(memory_space=pl.ANY),
            pl.BlockSpec(memory_space=pltpu.VMEM),
            pl.BlockSpec(memory_space=pltpu.VMEM),
        ],
        scratch_shapes=[
            pltpu.VMEM(u_all.shape, jnp.float32),
            pltpu.VMEM((nodes, rows * width, width), jnp.float32),
            pltpu.VMEM((nodes, width, width), jnp.float32),
            pltpu.VMEM((slots, width, width), jnp.float32),
            pltpu.SemaphoreType.DMA((slots,)),
            pltpu.SemaphoreType.DMA((2, later, parts)),
            pltpu.SemaphoreType.DMA((2, later, parts)),
            pltpu.SemaphoreType.DMA((slots,)),
            pltpu.SemaphoreType.DMA((slots,)),
        ],
        input_output_aliases={4: 0},
        compiler_params=pltpu.CompilerParams(collective_id=1, has_side_effects=True,
                                             vmem_limit_bytes=60 * 1024 * 1024),
        cost_estimate=pl.CostEstimate(flops=flops, transcendentals=0,
                                      bytes_accessed=4 * (sigma_rows.size + u_all.size)),
    )(struct, hit, slot, sigma_rows, u_all)


def body(sigma_anc, factor, diag_inv, struct):
    row_count = sigma_anc.shape[0]
    row_index = lax.axis_index("row")
    sigma_rows = lax.all_gather(sigma_anc, "col", axis=1, tiled=True)
    u_local = jnp.einsum("kij,kjl->kil", factor[0], diag_inv, precision=high)
    first, parts = 4, 4
    u_head = ring_gather(u_local, lax.axis_size("row"), first, parts)
    wanted = row_index * row_count + jnp.arange(row_count, dtype=jnp.int32)
    match = struct[:, :, None] == wanted[None, None, :]
    hit = jnp.any(match, axis=1).astype(jnp.int32)
    slot = jnp.argmax(match, axis=1).astype(jnp.int32)
    unused_u, z_off, summed = fused_call(struct, hit, slot, sigma_rows, u_head, first, parts)
    inverse_share = lax.dynamic_slice_in_dim(diag_inv, row_index, 1, 0)
    inverse_part = jnp.einsum("kij,kil->kjl", inverse_share, inverse_share, precision=high)
    return (z_off, inverse_part + summed)


def solution(mesh):
    in_specs = (
        P("row", "col", None, None),
        P("row", "col", None, None),
        P("col", None, None),
        P("col", None),
    )
    out_specs = (P("col", "row", None, None), P(("col", "row"), None, None))
    return jax.shard_map(body, mesh=mesh, in_specs=in_specs, out_specs=out_specs, check_vma=False)
```

```python
import functools

import jax
import jax.numpy as jnp
from jax import lax
from jax.experimental import pallas as pl
from jax.experimental.pallas import tpu as pltpu
from jax.sharding import PartitionSpec as P

high = lax.Precision.HIGH


def greet_neighbours(me, col, n):
    barrier = pltpu.get_barrier_semaphore()
    for peer in (lax.rem(me + n - 1, n), lax.rem(me + 1, n)):
        pl.semaphore_signal(barrier, inc=1, device_id=(peer, col), device_id_type=pl.DeviceIdType.MESH)
    pl.semaphore_wait(barrier, 2)


def step_parts(step, direction, half, parts):
    if step < half:
        return range(parts)
    if direction == 0:
        return range(parts // 2)
    return range(parts // 2, parts)


def ring_kernel(steps, parts, u_ref, out_ref, copy_sem, send_sem, recv_sem):
    n = out_ref.shape[0]
    chunk = out_ref.shape[1] // parts
    me = lax.axis_index("row")
    col = lax.axis_index("col")

    def link(step, direction, part):
        if direction == 0:
            slot = lax.rem(me - (step - 1) + n, n)
            peer = lax.rem(me + 1, n)
        else:
            slot = lax.rem(me + (step - 1), n)
            peer = lax.rem(me + n - 1, n)
        piece = pl.ds(part * chunk, chunk)
        return pltpu.make_async_remote_copy(
            src_ref=out_ref.at[slot, piece], dst_ref=out_ref.at[slot, piece],
            send_sem=send_sem.at[direction, step - 1, part],
            recv_sem=recv_sem.at[direction, step - 1, part],
            device_id=(peer, col), device_id_type=pl.DeviceIdType.MESH)

    own = pltpu.make_async_copy(u_ref, out_ref.at[me], copy_sem.at[0])
    own.start()
    greet_neighbours(me, col, n)
    own.wait()

    started = []
    for step in range(1, steps + 1):
        for direction in (0, 1):
            for part in range(parts):
                if step > 1:
                    link(step - 1, direction, part).wait_recv()
                copy = link(step, direction, part)
                copy.start()
                started.append(copy)
    for direction in (0, 1):
        for part in range(parts):
            link(steps, direction, part).wait_recv()
    for copy in started:
        copy.wait_send()


def ring_gather(u_local, slots, steps, parts):
    nodes, width, _ = u_local.shape
    return pl.pallas_call(
        functools.partial(ring_kernel, steps, parts),
        out_shape=jax.ShapeDtypeStruct((slots, nodes, width, width), jnp.float32),
        in_specs=[pl.BlockSpec(memory_space=pl.ANY)],
        out_specs=pl.BlockSpec(memory_space=pl.ANY),
        scratch_shapes=[
            pltpu.SemaphoreType.DMA((1,)),
            pltpu.SemaphoreType.DMA((2, steps, parts)),
            pltpu.SemaphoreType.DMA((2, steps, parts)),
        ],
        compiler_params=pltpu.CompilerParams(collective_id=0, has_side_effects=True),
    )(u_local)


def fused_kernel(first, parts, struct_ref, hit_ref, slot_ref, sig_ref, u_in, zoff_ref, sum_ref,
                 u_vmem, y_acc, part_ref, gather_buf, load_sem, send_sem, recv_sem, out_sem, in_sem):
    n = u_in.shape[0]
    half = n // 2
    nodes = u_in.shape[1]
    chunk = nodes // parts
    rows = sig_ref.shape[0]
    width = sig_ref.shape[-1]
    me = lax.axis_index("row")
    col = lax.axis_index("col")

    def link(step, direction, part):
        if direction == 0:
            slot = lax.rem(me - (step - 1) + n, n)
            peer = lax.rem(me + 1, n)
        else:
            slot = lax.rem(me + (step - 1), n)
            peer = lax.rem(me + n - 1, n)
        piece = pl.ds(part * chunk, chunk)
        source = u_in if step == first + 1 else u_vmem
        return pltpu.make_async_remote_copy(
            src_ref=source.at[slot, piece], dst_ref=u_vmem.at[slot, piece],
            send_sem=send_sem.at[direction, step - 1 - first, part],
            recv_sem=recv_sem.at[direction, step - 1 - first, part],
            device_id=(peer, col), device_id_type=pl.DeviceIdType.MESH)

    def load(slot):
        return pltpu.make_async_copy(u_in.at[slot], u_vmem.at[slot], load_sem.at[slot])

    def wrap(offset):
        return lax.rem(me + offset + 2 * n, n)

    barrier = pltpu.get_barrier_semaphore()
    for offset in range(1, n):
        pl.semaphore_signal(barrier, inc=1, device_id=(lax.rem(me + offset, n), col),
                            device_id_type=pl.DeviceIdType.MESH)
    pl.semaphore_wait(barrier, n - 1)
    for offset in range(-first, first + 1):
        load(wrap(offset)).start()

    started = []

    def send_step(step):
        for direction in (0, 1):
            for part in step_parts(step, direction, half, parts):
                copy = link(step, direction, part)
                copy.start()
                started.append(copy)

    send_step(first + 1)

    def lhs_block(k, slot):
        return sig_ref[:, struct_ref[k, slot]].reshape(rows * width, width)

    def add_single(slot):
        def node(k, carry):
            y_acc[k] += jnp.dot(lhs_block(k, slot), u_vmem[slot, k], precision=high,
                                preferred_element_type=jnp.float32)
            return carry
        lax.fori_loop(0, nodes, node, 0)

    def add_pair(one, two):
        def node(k, carry):
            lhs = jnp.concatenate([lhs_block(k, one), lhs_block(k, two)], axis=1)
            rhs = jnp.concatenate([u_vmem[one, k], u_vmem[two, k]], axis=0)
            y_acc[k] += jnp.dot(lhs, rhs, precision=high, preferred_element_type=jnp.float32)
            return carry
        lax.fori_loop(0, nodes, node, 0)

    def ring_event(step):
        for direction in (0, 1):
            for part in step_parts(step, direction, half, parts):
                link(step, direction, part).wait_recv()
        if step < half:
            send_step(step + 1)

    def arrived(step):
        if step < half:
            add_pair(wrap(-step), wrap(step))
        else:
            add_single(wrap(half))

    processed = first
    load(me).wait()
    y_acc[...] = jnp.zeros_like(y_acc)
    add_single(me)
    for offset in range(1, first + 1):
        load(wrap(-offset)).wait()
        load(wrap(offset)).wait()
        add_pair(wrap(-offset), wrap(offset))
        if offset % 2 == 0 and processed < half:
            processed += 1
            ring_event(processed)
    done = first + 1
    while done < half:
        if done <= processed:
            arrived(done)
            done += 1
        else:
            processed += 1
            ring_event(processed)
    while processed < half:
        processed += 1
        ring_event(processed)
    last = wrap(half)

    for copy in started:
        copy.wait_send()

    def share_to(k):
        return pltpu.make_async_remote_copy(
            src_ref=part_ref.at[k], dst_ref=gather_buf.at[me],
            send_sem=out_sem.at[k], recv_sem=in_sem.at[me],
            device_id=(k, col), device_id_type=pl.DeviceIdType.MESH)

    def share_from(j):
        return pltpu.make_async_remote_copy(
            src_ref=part_ref.at[j], dst_ref=gather_buf.at[j],
            send_sem=out_sem.at[j], recv_sem=in_sem.at[j],
            device_id=(j, col), device_id_type=pl.DeviceIdType.MESH)

    def finish(k, carry):
        y = y_acc[k] + jnp.dot(lhs_block(k, last), u_vmem[last, k], precision=high,
                               preferred_element_type=jnp.float32)
        y = y.reshape(rows, width, width)
        total = jnp.zeros((width, width), jnp.float32)
        for j in range(rows):
            hits = hit_ref[k, j]
            slot = jnp.minimum(slot_ref[k, j], n - 1)
            term = jnp.dot(jnp.transpose(u_vmem[slot, k]), y[j], precision=high,
                           preferred_element_type=jnp.float32)
            total = total + jnp.where(hits > 0, term, 0.0)
            zoff_ref[k, j] = jnp.where(hits > 0, -y[j], 0.0)
        part_ref[k] = total

        @pl.when((k >= 1) & (k - 1 != me))
        def _():
            share_to(k - 1).start()

        return carry

    lax.fori_loop(0, nodes, finish, 0)

    @pl.when(me != nodes - 1)
    def _():
        share_to(nodes - 1).start()

    gather_buf[me] = part_ref[me]
    for j in range(n):
        @pl.when(me != j)
        def _():
            share_to(j).wait_send()
            share_from(j).wait_recv()

    sum_ref[0] = jnp.sum(gather_buf[...], axis=0)


def fused_call(struct, hit, slot, sigma_rows, u_all, first, parts):
    slots, nodes, width, _ = u_all.shape
    rows = sigma_rows.shape[0]
    later = slots // 2 - first
    flops = 2 * nodes * slots * rows * width ** 3 * 3
    return pl.pallas_call(
        functools.partial(fused_kernel, first, parts),
        out_shape=[
            jax.ShapeDtypeStruct((nodes, rows, width, width), jnp.float32),
            jax.ShapeDtypeStruct((1, width, width), jnp.float32),
        ],
        in_specs=[
            pl.BlockSpec(memory_space=pltpu.SMEM),
            pl.BlockSpec(memory_space=pltpu.SMEM),
            pl.BlockSpec(memory_space=pltpu.SMEM),
            pl.BlockSpec(memory_space=pltpu.VMEM),
            pl.BlockSpec(memory_space=pl.ANY),
        ],
        out_specs=[
            pl.BlockSpec(memory_space=pltpu.VMEM),
            pl.BlockSpec(memory_space=pltpu.VMEM),
        ],
        scratch_shapes=[
            pltpu.VMEM(u_all.shape, jnp.float32),
            pltpu.VMEM((nodes, rows * width, width), jnp.float32),
            pltpu.VMEM((nodes, width, width), jnp.float32),
            pltpu.VMEM((slots, width, width), jnp.float32),
            pltpu.SemaphoreType.DMA((slots,)),
            pltpu.SemaphoreType.DMA((2, later, parts)),
            pltpu.SemaphoreType.DMA((2, later, parts)),
            pltpu.SemaphoreType.DMA((slots,)),
            pltpu.SemaphoreType.DMA((slots,)),
        ],
        compiler_params=pltpu.CompilerParams(collective_id=1, has_side_effects=True,
                                             vmem_limit_bytes=60 * 1024 * 1024),
        cost_estimate=pl.CostEstimate(flops=flops, transcendentals=0,
                                      bytes_accessed=4 * (sigma_rows.size + u_all.size)),
    )(struct, hit, slot, sigma_rows, u_all)


def body(sigma_anc, factor, diag_inv, struct):
    row_count = sigma_anc.shape[0]
    row_index = lax.axis_index("row")
    sigma_rows = lax.all_gather(sigma_anc, "col", axis=1, tiled=True)
    u_local = jnp.einsum("kij,kjl->kil", factor[0], diag_inv, precision=high)
    first, parts = 4, 4
    u_head = ring_gather(u_local, lax.axis_size("row"), first, parts)
    wanted = row_index * row_count + jnp.arange(row_count, dtype=jnp.int32)
    match = struct[:, :, None] == wanted[None, None, :]
    hit = jnp.any(match, axis=1).astype(jnp.int32)
    slot = jnp.argmax(match, axis=1).astype(jnp.int32)
    z_off, summed = fused_call(struct, hit, slot, sigma_rows, u_head, first, parts)
    inverse_share = lax.dynamic_slice_in_dim(diag_inv, row_index, 1, 0)
    inverse_part = jnp.einsum("kij,kil->kjl", inverse_share, inverse_share, precision=high)
    return (z_off, inverse_part + summed)


def solution(mesh):
    in_specs = (
        P("row", "col", None, None),
        P("row", "col", None, None),
        P("col", None, None),
        P("col", None),
    )
    out_specs = (P("col", "row", None, None), P(("col", "row"), None, None))
    return jax.shard_map(body, mesh=mesh, in_specs=in_specs, out_specs=out_specs, check_vma=False)
```

```python
import functools

import jax
import jax.numpy as jnp
from jax import lax
from jax.experimental import pallas as pl
from jax.experimental.pallas import tpu as pltpu
from jax.sharding import PartitionSpec as P

high = lax.Precision.HIGH


def greet_neighbours(me, col, n):
    barrier = pltpu.get_barrier_semaphore()
    for peer in (lax.rem(me + n - 1, n), lax.rem(me + 1, n)):
        pl.semaphore_signal(barrier, inc=1, device_id=(peer, col), device_id_type=pl.DeviceIdType.MESH)
    pl.semaphore_wait(barrier, 2)


def step_parts(step, direction, half, parts):
    if step < half:
        return range(parts)
    if direction == 0:
        return range(parts // 2)
    return range(parts // 2, parts)


def ring_kernel(steps, parts, u_ref, out_ref, copy_sem, send_sem, recv_sem):
    n = out_ref.shape[0]
    chunk = out_ref.shape[1] // parts
    me = lax.axis_index("row")
    col = lax.axis_index("col")

    def link(step, direction, part):
        if direction == 0:
            slot = lax.rem(me - (step - 1) + n, n)
            peer = lax.rem(me + 1, n)
        else:
            slot = lax.rem(me + (step - 1), n)
            peer = lax.rem(me + n - 1, n)
        piece = pl.ds(part * chunk, chunk)
        return pltpu.make_async_remote_copy(
            src_ref=out_ref.at[slot, piece], dst_ref=out_ref.at[slot, piece],
            send_sem=send_sem.at[direction, step - 1, part],
            recv_sem=recv_sem.at[direction, step - 1, part],
            device_id=(peer, col), device_id_type=pl.DeviceIdType.MESH)

    own = pltpu.make_async_copy(u_ref, out_ref.at[me], copy_sem.at[0])
    own.start()
    greet_neighbours(me, col, n)
    own.wait()

    started = []
    for step in range(1, steps + 1):
        for direction in (0, 1):
            for part in range(parts):
                if step > 1:
                    link(step - 1, direction, part).wait_recv()
                copy = link(step, direction, part)
                copy.start()
                started.append(copy)
    for direction in (0, 1):
        for part in range(parts):
            link(steps, direction, part).wait_recv()
    for copy in started:
        copy.wait_send()


def ring_gather(u_local, slots, steps, parts):
    nodes, width, _ = u_local.shape
    return pl.pallas_call(
        functools.partial(ring_kernel, steps, parts),
        out_shape=jax.ShapeDtypeStruct((slots, nodes, width, width), jnp.float32),
        in_specs=[pl.BlockSpec(memory_space=pl.ANY)],
        out_specs=pl.BlockSpec(memory_space=pl.ANY),
        scratch_shapes=[
            pltpu.SemaphoreType.DMA((1,)),
            pltpu.SemaphoreType.DMA((2, steps, parts)),
            pltpu.SemaphoreType.DMA((2, steps, parts)),
        ],
        compiler_params=pltpu.CompilerParams(collective_id=0, has_side_effects=True),
    )(u_local)


def fused_kernel(first, parts, struct_ref, hit_ref, slot_ref, sig_ref, inv_ref, u_in, zoff_ref, sum_ref,
                 u_vmem, y_acc, part_ref, gather_buf, load_sem, send_sem, recv_sem, out_sem, in_sem):
    n = u_in.shape[0]
    half = n // 2
    nodes = u_in.shape[1]
    chunk = nodes // parts
    rows = sig_ref.shape[0]
    width = sig_ref.shape[-1]
    me = lax.axis_index("row")
    col = lax.axis_index("col")

    def link(step, direction, part):
        if direction == 0:
            slot = lax.rem(me - (step - 1) + n, n)
            peer = lax.rem(me + 1, n)
        else:
            slot = lax.rem(me + (step - 1), n)
            peer = lax.rem(me + n - 1, n)
        piece = pl.ds(part * chunk, chunk)
        source = u_in if step == first + 1 else u_vmem
        return pltpu.make_async_remote_copy(
            src_ref=source.at[slot, piece], dst_ref=u_vmem.at[slot, piece],
            send_sem=send_sem.at[direction, step - 1 - first, part],
            recv_sem=recv_sem.at[direction, step - 1 - first, part],
            device_id=(peer, col), device_id_type=pl.DeviceIdType.MESH)

    def load(slot):
        return pltpu.make_async_copy(u_in.at[slot], u_vmem.at[slot], load_sem.at[slot])

    def wrap(offset):
        return lax.rem(me + offset + 2 * n, n)

    barrier = pltpu.get_barrier_semaphore()
    for offset in range(1, n):
        pl.semaphore_signal(barrier, inc=1, device_id=(lax.rem(me + offset, n), col),
                            device_id_type=pl.DeviceIdType.MESH)
    pl.semaphore_wait(barrier, n - 1)
    for offset in range(-first, first + 1):
        load(wrap(offset)).start()

    started = []

    def send_step(step):
        for direction in (0, 1):
            for part in step_parts(step, direction, half, parts):
                copy = link(step, direction, part)
                copy.start()
                started.append(copy)

    send_step(first + 1)

    def lhs_block(k, slot):
        return sig_ref[:, struct_ref[k, slot]].reshape(rows * width, width)

    def add_single(slot):
        def node(k, carry):
            y_acc[k] += jnp.dot(lhs_block(k, slot), u_vmem[slot, k], precision=high,
                                preferred_element_type=jnp.float32)
            return carry
        lax.fori_loop(0, nodes, node, 0)

    def add_pair(one, two):
        def node(k, carry):
            lhs = jnp.concatenate([lhs_block(k, one), lhs_block(k, two)], axis=1)
            rhs = jnp.concatenate([u_vmem[one, k], u_vmem[two, k]], axis=0)
            y_acc[k] += jnp.dot(lhs, rhs, precision=high, preferred_element_type=jnp.float32)
            return carry
        lax.fori_loop(0, nodes, node, 0)

    def ring_event(step):
        for direction in (0, 1):
            for part in step_parts(step, direction, half, parts):
                link(step, direction, part).wait_recv()
        if step < half:
            send_step(step + 1)

    def arrived(step):
        if step < half:
            add_pair(wrap(-step), wrap(step))
        else:
            add_single(wrap(half))

    processed = first
    load(me).wait()
    y_acc[...] = jnp.zeros_like(y_acc)
    add_single(me)
    for offset in range(1, first + 1):
        load(wrap(-offset)).wait()
        load(wrap(offset)).wait()
        add_pair(wrap(-offset), wrap(offset))
        if offset % 2 == 0 and processed < half:
            processed += 1
            ring_event(processed)
    done = first + 1
    while done < half:
        if done <= processed:
            arrived(done)
            done += 1
        else:
            processed += 1
            ring_event(processed)
    while processed < half:
        processed += 1
        ring_event(processed)
    last = wrap(half)

    for copy in started:
        copy.wait_send()

    def share_to(k):
        return pltpu.make_async_remote_copy(
            src_ref=part_ref.at[k], dst_ref=gather_buf.at[me],
            send_sem=out_sem.at[k], recv_sem=in_sem.at[me],
            device_id=(k, col), device_id_type=pl.DeviceIdType.MESH)

    def share_from(j):
        return pltpu.make_async_remote_copy(
            src_ref=part_ref.at[j], dst_ref=gather_buf.at[j],
            send_sem=out_sem.at[j], recv_sem=in_sem.at[j],
            device_id=(j, col), device_id_type=pl.DeviceIdType.MESH)

    def finish(k, carry):
        y = y_acc[k] + jnp.dot(lhs_block(k, last), u_vmem[last, k], precision=high,
                               preferred_element_type=jnp.float32)
        y = y.reshape(rows, width, width)
        total = jnp.zeros((width, width), jnp.float32)
        for j in range(rows):
            hits = hit_ref[k, j]
            slot = jnp.minimum(slot_ref[k, j], n - 1)
            term = jnp.dot(jnp.transpose(u_vmem[slot, k]), y[j], precision=high,
                           preferred_element_type=jnp.float32)
            total = total + jnp.where(hits > 0, term, 0.0)
            zoff_ref[k, j] = jnp.where(hits > 0, -y[j], 0.0)
        part_ref[k] = total

        @pl.when((k >= 1) & (k - 1 != me))
        def _():
            share_to(k - 1).start()

        return carry

    lax.fori_loop(0, nodes, finish, 0)

    @pl.when(me != nodes - 1)
    def _():
        share_to(nodes - 1).start()

    gather_buf[me] = part_ref[me]
    for j in range(n):
        @pl.when(me != j)
        def _():
            share_to(j).wait_send()
            share_from(j).wait_recv()

    inverse = inv_ref[0]
    inverse_part = jnp.dot(jnp.transpose(inverse), inverse, precision=high,
                           preferred_element_type=jnp.float32)
    sum_ref[0] = inverse_part + jnp.sum(gather_buf[...], axis=0)


def fused_call(struct, hit, slot, sigma_rows, inverse_share, u_all, first, parts):
    slots, nodes, width, _ = u_all.shape
    rows = sigma_rows.shape[0]
    later = slots // 2 - first
    flops = 2 * nodes * slots * rows * width ** 3 * 3
    return pl.pallas_call(
        functools.partial(fused_kernel, first, parts),
        out_shape=[
            jax.ShapeDtypeStruct((nodes, rows, width, width), jnp.float32),
            jax.ShapeDtypeStruct((1, width, width), jnp.float32),
        ],
        in_specs=[
            pl.BlockSpec(memory_space=pltpu.SMEM),
            pl.BlockSpec(memory_space=pltpu.SMEM),
            pl.BlockSpec(memory_space=pltpu.SMEM),
            pl.BlockSpec(memory_space=pltpu.VMEM),
            pl.BlockSpec(memory_space=pltpu.VMEM),
            pl.BlockSpec(memory_space=pl.ANY),
        ],
        out_specs=[
            pl.BlockSpec(memory_space=pltpu.VMEM),
            pl.BlockSpec(memory_space=pltpu.VMEM),
        ],
        scratch_shapes=[
            pltpu.VMEM(u_all.shape, jnp.float32),
            pltpu.VMEM((nodes, rows * width, width), jnp.float32),
            pltpu.VMEM((nodes, width, width), jnp.float32),
            pltpu.VMEM((slots, width, width), jnp.float32),
            pltpu.SemaphoreType.DMA((slots,)),
            pltpu.SemaphoreType.DMA((2, later, parts)),
            pltpu.SemaphoreType.DMA((2, later, parts)),
            pltpu.SemaphoreType.DMA((slots,)),
            pltpu.SemaphoreType.DMA((slots,)),
        ],
        compiler_params=pltpu.CompilerParams(collective_id=1, has_side_effects=True,
                                             vmem_limit_bytes=60 * 1024 * 1024),
        cost_estimate=pl.CostEstimate(flops=flops, transcendentals=0,
                                      bytes_accessed=4 * (sigma_rows.size + u_all.size)),
    )(struct, hit, slot, sigma_rows, inverse_share, u_all)


def body(sigma_anc, factor, diag_inv, struct):
    row_count = sigma_anc.shape[0]
    row_index = lax.axis_index("row")
    sigma_rows = lax.all_gather(sigma_anc, "col", axis=1, tiled=True)
    u_local = jnp.einsum("kij,kjl->kil", factor[0], diag_inv, precision=high)
    first, parts = 4, 4
    u_head = ring_gather(u_local, lax.axis_size("row"), first, parts)
    struct, u_head = lax.optimization_barrier((struct, u_head))
    wanted = row_index * row_count + jnp.arange(row_count, dtype=jnp.int32)
    match = struct[:, :, None] == wanted[None, None, :]
    hit = jnp.any(match, axis=1).astype(jnp.int32)
    slot = jnp.argmax(match, axis=1).astype(jnp.int32)
    inverse_share = lax.dynamic_slice_in_dim(diag_inv, row_index, 1, 0)
    z_off, z_diag = fused_call(struct, hit, slot, sigma_rows, inverse_share, u_head, first, parts)
    return (z_off, z_diag)


def solution(mesh):
    in_specs = (
        P("row", "col", None, None),
        P("row", "col", None, None),
        P("col", None, None),
        P("col", None),
    )
    out_specs = (P("col", "row", None, None), P(("col", "row"), None, None))
    return jax.shard_map(body, mesh=mesh, in_specs=in_specs, out_specs=out_specs, check_vma=False)
```

```python
import functools

import jax
import jax.numpy as jnp
from jax import lax
from jax.experimental import pallas as pl
from jax.experimental.pallas import tpu as pltpu
from jax.sharding import PartitionSpec as P

high = lax.Precision.HIGH


def greet_neighbours(me, col, n):
    barrier = pltpu.get_barrier_semaphore()
    for peer in (lax.rem(me + n - 1, n), lax.rem(me + 1, n)):
        pl.semaphore_signal(barrier, inc=1, device_id=(peer, col), device_id_type=pl.DeviceIdType.MESH)
    pl.semaphore_wait(barrier, 2)


def step_parts(step, direction, half, parts):
    if step < half:
        return range(parts)
    if direction == 0:
        return range(parts // 2)
    return range(parts // 2, parts)


def ring_kernel(steps, parts, rows, struct_ref, u_ref, out_ref, hit_ref, slot_ref, copy_sem, send_sem, recv_sem):
    n = out_ref.shape[0]
    chunk = out_ref.shape[1] // parts
    me = lax.axis_index("row")
    col = lax.axis_index("col")

    def link(step, direction, part):
        if direction == 0:
            slot = lax.rem(me - (step - 1) + n, n)
            peer = lax.rem(me + 1, n)
        else:
            slot = lax.rem(me + (step - 1), n)
            peer = lax.rem(me + n - 1, n)
        piece = pl.ds(part * chunk, chunk)
        return pltpu.make_async_remote_copy(
            src_ref=out_ref.at[slot, piece], dst_ref=out_ref.at[slot, piece],
            send_sem=send_sem.at[direction, step - 1, part],
            recv_sem=recv_sem.at[direction, step - 1, part],
            device_id=(peer, col), device_id_type=pl.DeviceIdType.MESH)

    own = pltpu.make_async_copy(u_ref, out_ref.at[me], copy_sem.at[0])
    own.start()
    greet_neighbours(me, col, n)
    own.wait()

    started = []
    for step in range(1, steps + 1):
        for direction in (0, 1):
            for part in range(parts):
                if step > 1:
                    link(step - 1, direction, part).wait_recv()
                copy = link(step, direction, part)
                copy.start()
                started.append(copy)
        if step == 1:
            base = me * rows

            def member(k, carry):
                for j in range(rows):
                    def scan(s, acc):
                        hit = (struct_ref[k, s] == base + j).astype(jnp.int32)
                        return acc[0] + hit, acc[1] + hit * s
                    hits, slot = lax.fori_loop(0, n, scan, (jnp.int32(0), jnp.int32(0)))
                    hit_ref[k, j] = hits
                    slot_ref[k, j] = slot
                return carry

            lax.fori_loop(0, struct_ref.shape[0], member, 0)
    for direction in (0, 1):
        for part in range(parts):
            link(steps, direction, part).wait_recv()
    for copy in started:
        copy.wait_send()


def ring_gather(struct, u_local, slots, rows, steps, parts):
    nodes, width, _ = u_local.shape
    return pl.pallas_call(
        functools.partial(ring_kernel, steps, parts, rows),
        out_shape=[
            jax.ShapeDtypeStruct((slots, nodes, width, width), jnp.float32),
            jax.ShapeDtypeStruct((nodes, rows), jnp.int32),
            jax.ShapeDtypeStruct((nodes, rows), jnp.int32),
        ],
        in_specs=[pl.BlockSpec(memory_space=pltpu.SMEM), pl.BlockSpec(memory_space=pl.ANY)],
        out_specs=[
            pl.BlockSpec(memory_space=pl.ANY),
            pl.BlockSpec(memory_space=pltpu.SMEM),
            pl.BlockSpec(memory_space=pltpu.SMEM),
        ],
        scratch_shapes=[
            pltpu.SemaphoreType.DMA((1,)),
            pltpu.SemaphoreType.DMA((2, steps, parts)),
            pltpu.SemaphoreType.DMA((2, steps, parts)),
        ],
        compiler_params=pltpu.CompilerParams(collective_id=0, has_side_effects=True),
    )(struct, u_local)


def fused_kernel(first, parts, struct_ref, hit_ref, slot_ref, sig_ref, inv_ref, u_in, zoff_ref, sum_ref,
                 u_vmem, y_acc, part_ref, gather_buf, inv_vmem, load_sem, send_sem, recv_sem, out_sem, in_sem,
                 inv_sem):
    n = u_in.shape[0]
    half = n // 2
    nodes = u_in.shape[1]
    chunk = nodes // parts
    rows = sig_ref.shape[0]
    width = sig_ref.shape[-1]
    me = lax.axis_index("row")
    col = lax.axis_index("col")

    def link(step, direction, part):
        if direction == 0:
            slot = lax.rem(me - (step - 1) + n, n)
            peer = lax.rem(me + 1, n)
        else:
            slot = lax.rem(me + (step - 1), n)
            peer = lax.rem(me + n - 1, n)
        piece = pl.ds(part * chunk, chunk)
        source = u_in if step == first + 1 else u_vmem
        return pltpu.make_async_remote_copy(
            src_ref=source.at[slot, piece], dst_ref=u_vmem.at[slot, piece],
            send_sem=send_sem.at[direction, step - 1 - first, part],
            recv_sem=recv_sem.at[direction, step - 1 - first, part],
            device_id=(peer, col), device_id_type=pl.DeviceIdType.MESH)

    def load(slot):
        return pltpu.make_async_copy(u_in.at[slot], u_vmem.at[slot], load_sem.at[slot])

    def wrap(offset):
        return lax.rem(me + offset + 2 * n, n)

    barrier = pltpu.get_barrier_semaphore()
    for offset in range(1, n):
        pl.semaphore_signal(barrier, inc=1, device_id=(lax.rem(me + offset, n), col),
                            device_id_type=pl.DeviceIdType.MESH)
    pl.semaphore_wait(barrier, n - 1)
    for offset in range(-first, first + 1):
        load(wrap(offset)).start()
    inv_copy = pltpu.make_async_copy(inv_ref.at[me], inv_vmem, inv_sem.at[0])
    inv_copy.start()

    started = []

    def send_step(step):
        for direction in (0, 1):
            for part in step_parts(step, direction, half, parts):
                copy = link(step, direction, part)
                copy.start()
                started.append(copy)

    send_step(first + 1)

    def lhs_block(k, slot):
        return sig_ref[:, struct_ref[k, slot]].reshape(rows * width, width)

    def add_single(slot):
        def node(k, carry):
            y_acc[k] += jnp.dot(lhs_block(k, slot), u_vmem[slot, k], precision=high,
                                preferred_element_type=jnp.float32)
            return carry
        lax.fori_loop(0, nodes, node, 0)

    def add_pair(one, two):
        def node(k, carry):
            lhs = jnp.concatenate([lhs_block(k, one), lhs_block(k, two)], axis=1)
            rhs = jnp.concatenate([u_vmem[one, k], u_vmem[two, k]], axis=0)
            y_acc[k] += jnp.dot(lhs, rhs, precision=high, preferred_element_type=jnp.float32)
            return carry
        lax.fori_loop(0, nodes, node, 0)

    def ring_event(step):
        for direction in (0, 1):
            for part in step_parts(step, direction, half, parts):
                link(step, direction, part).wait_recv()
        if step < half:
            send_step(step + 1)

    def arrived(step):
        if step < half:
            add_pair(wrap(-step), wrap(step))
        else:
            add_single(wrap(half))

    processed = first
    load(me).wait()
    y_acc[...] = jnp.zeros_like(y_acc)
    add_single(me)
    for offset in range(1, first + 1):
        load(wrap(-offset)).wait()
        load(wrap(offset)).wait()
        add_pair(wrap(-offset), wrap(offset))
        if offset % 2 == 0 and processed < half:
            processed += 1
            ring_event(processed)
    done = first + 1
    while done < half:
        if done <= processed:
            arrived(done)
            done += 1
        else:
            processed += 1
            ring_event(processed)
    while processed < half:
        processed += 1
        ring_event(processed)
    last = wrap(half)

    for copy in started:
        copy.wait_send()

    def share_to(k):
        return pltpu.make_async_remote_copy(
            src_ref=part_ref.at[k], dst_ref=gather_buf.at[me],
            send_sem=out_sem.at[k], recv_sem=in_sem.at[me],
            device_id=(k, col), device_id_type=pl.DeviceIdType.MESH)

    def share_from(j):
        return pltpu.make_async_remote_copy(
            src_ref=part_ref.at[j], dst_ref=gather_buf.at[j],
            send_sem=out_sem.at[j], recv_sem=in_sem.at[j],
            device_id=(j, col), device_id_type=pl.DeviceIdType.MESH)

    def finish(k, carry):
        y = y_acc[k] + jnp.dot(lhs_block(k, last), u_vmem[last, k], precision=high,
                               preferred_element_type=jnp.float32)
        y = y.reshape(rows, width, width)
        total = jnp.zeros((width, width), jnp.float32)
        for j in range(rows):
            hits = hit_ref[k, j]
            slot = jnp.minimum(slot_ref[k, j], n - 1)
            term = jnp.dot(jnp.transpose(u_vmem[slot, k]), y[j], precision=high,
                           preferred_element_type=jnp.float32)
            total = total + jnp.where(hits > 0, term, 0.0)
            zoff_ref[k, j] = jnp.where(hits > 0, -y[j], 0.0)
        part_ref[k] = total

        @pl.when((k >= 1) & (k - 1 != me))
        def _():
            share_to(k - 1).start()

        return carry

    lax.fori_loop(0, nodes, finish, 0)

    @pl.when(me != nodes - 1)
    def _():
        share_to(nodes - 1).start()

    gather_buf[me] = part_ref[me]
    for j in range(n):
        @pl.when(me != j)
        def _():
            share_to(j).wait_send()
            share_from(j).wait_recv()

    inv_copy.wait()
    inverse = inv_vmem[...]
    inverse_part = jnp.dot(jnp.transpose(inverse), inverse, precision=high,
                           preferred_element_type=jnp.float32)
    sum_ref[0] = inverse_part + jnp.sum(gather_buf[...], axis=0)


def fused_call(struct, hit, slot, sigma_rows, inverse_share, u_all, first, parts):
    slots, nodes, width, _ = u_all.shape
    rows = sigma_rows.shape[0]
    later = slots // 2 - first
    flops = 2 * nodes * slots * rows * width ** 3 * 3
    return pl.pallas_call(
        functools.partial(fused_kernel, first, parts),
        out_shape=[
            jax.ShapeDtypeStruct((nodes, rows, width, width), jnp.float32),
            jax.ShapeDtypeStruct((1, width, width), jnp.float32),
        ],
        in_specs=[
            pl.BlockSpec(memory_space=pltpu.SMEM),
            pl.BlockSpec(memory_space=pltpu.SMEM),
            pl.BlockSpec(memory_space=pltpu.SMEM),
            pl.BlockSpec(memory_space=pltpu.VMEM),
            pl.BlockSpec(memory_space=pl.ANY),
            pl.BlockSpec(memory_space=pl.ANY),
        ],
        out_specs=[
            pl.BlockSpec(memory_space=pltpu.VMEM),
            pl.BlockSpec(memory_space=pltpu.VMEM),
        ],
        scratch_shapes=[
            pltpu.VMEM(u_all.shape, jnp.float32),
            pltpu.VMEM((nodes, rows * width, width), jnp.float32),
            pltpu.VMEM((nodes, width, width), jnp.float32),
            pltpu.VMEM((slots, width, width), jnp.float32),
            pltpu.VMEM((width, width), jnp.float32),
            pltpu.SemaphoreType.DMA((slots,)),
            pltpu.SemaphoreType.DMA((2, later, parts)),
            pltpu.SemaphoreType.DMA((2, later, parts)),
            pltpu.SemaphoreType.DMA((slots,)),
            pltpu.SemaphoreType.DMA((slots,)),
            pltpu.SemaphoreType.DMA((1,)),
        ],
        compiler_params=pltpu.CompilerParams(collective_id=1, has_side_effects=True,
                                             vmem_limit_bytes=60 * 1024 * 1024),
        cost_estimate=pl.CostEstimate(flops=flops, transcendentals=0,
                                      bytes_accessed=4 * (sigma_rows.size + u_all.size)),
    )(struct, hit, slot, sigma_rows, inverse_share, u_all)


def body(sigma_anc, factor, diag_inv, struct):
    row_count = sigma_anc.shape[0]
    sigma_rows = lax.all_gather(sigma_anc, "col", axis=1, tiled=True)
    u_local = jnp.einsum("kij,kjl->kil", factor[0], diag_inv, precision=high)
    first, parts = 4, 4
    u_head, hit, slot = ring_gather(struct, u_local, lax.axis_size("row"), row_count, first, parts)
    z_off, z_diag = fused_call(struct, hit, slot, sigma_rows, diag_inv, u_head, first, parts)
    return (z_off, z_diag)


def solution(mesh):
    in_specs = (
        P("row", "col", None, None),
        P("row", "col", None, None),
        P("col", None, None),
        P("col", None),
    )
    out_specs = (P("col", "row", None, None), P(("col", "row"), None, None))
    return jax.shard_map(body, mesh=mesh, in_specs=in_specs, out_specs=out_specs, check_vma=False)
```

```python
import functools

import jax
import jax.numpy as jnp
from jax import lax
from jax.experimental import pallas as pl
from jax.experimental.pallas import tpu as pltpu
from jax.sharding import PartitionSpec as P

high = lax.Precision.HIGH


def greet_neighbours(me, col, n):
    barrier = pltpu.get_barrier_semaphore()
    for peer in (lax.rem(me + n - 1, n), lax.rem(me + 1, n)):
        pl.semaphore_signal(barrier, inc=1, device_id=(peer, col), device_id_type=pl.DeviceIdType.MESH)
    pl.semaphore_wait(barrier, 2)


def step_parts(step, direction, half, parts):
    if step < half:
        return range(parts)
    if direction == 0:
        return range(parts // 2)
    return range(parts // 2, parts)


def ring_kernel(steps, parts, rows, struct_ref, u_ref, out_ref, hit_ref, slot_ref, copy_sem, send_sem, recv_sem):
    n = out_ref.shape[0]
    chunk = out_ref.shape[1] // parts
    me = lax.axis_index("row")
    col = lax.axis_index("col")

    def link(step, direction, part):
        if direction == 0:
            slot = lax.rem(me - (step - 1) + n, n)
            peer = lax.rem(me + 1, n)
        else:
            slot = lax.rem(me + (step - 1), n)
            peer = lax.rem(me + n - 1, n)
        piece = pl.ds(part * chunk, chunk)
        return pltpu.make_async_remote_copy(
            src_ref=out_ref.at[slot, piece], dst_ref=out_ref.at[slot, piece],
            send_sem=send_sem.at[direction, step - 1, part],
            recv_sem=recv_sem.at[direction, step - 1, part],
            device_id=(peer, col), device_id_type=pl.DeviceIdType.MESH)

    own = pltpu.make_async_copy(u_ref, out_ref.at[me], copy_sem.at[0])
    own.start()
    greet_neighbours(me, col, n)
    own.wait()

    started = []
    for step in range(1, steps + 1):
        for direction in (0, 1):
            for part in range(parts):
                if step > 1:
                    link(step - 1, direction, part).wait_recv()
                copy = link(step, direction, part)
                copy.start()
                started.append(copy)
        if step == 1:
            base = me * rows

            def member(k, carry):
                for j in range(rows):
                    def scan(s, acc):
                        hit = (struct_ref[k, s] == base + j).astype(jnp.int32)
                        return acc[0] + hit, acc[1] + hit * s
                    hits, slot = lax.fori_loop(0, n, scan, (jnp.int32(0), jnp.int32(0)))
                    hit_ref[k, j] = hits
                    slot_ref[k, j] = slot
                return carry

            lax.fori_loop(0, struct_ref.shape[0], member, 0)
    for direction in (0, 1):
        for part in range(parts):
            link(steps, direction, part).wait_recv()
    for copy in started:
        copy.wait_send()


def ring_gather(struct, u_local, slots, rows, steps, parts):
    nodes, width, _ = u_local.shape
    return pl.pallas_call(
        functools.partial(ring_kernel, steps, parts, rows),
        out_shape=[
            jax.ShapeDtypeStruct((slots, nodes, width, width), jnp.float32),
            jax.ShapeDtypeStruct((nodes, rows), jnp.int32),
            jax.ShapeDtypeStruct((nodes, rows), jnp.int32),
        ],
        in_specs=[pl.BlockSpec(memory_space=pltpu.SMEM), pl.BlockSpec(memory_space=pl.ANY)],
        out_specs=[
            pl.BlockSpec(memory_space=pl.ANY),
            pl.BlockSpec(memory_space=pltpu.SMEM),
            pl.BlockSpec(memory_space=pltpu.SMEM),
        ],
        scratch_shapes=[
            pltpu.SemaphoreType.DMA((1,)),
            pltpu.SemaphoreType.DMA((2, steps, parts)),
            pltpu.SemaphoreType.DMA((2, steps, parts)),
        ],
        compiler_params=pltpu.CompilerParams(collective_id=0, has_side_effects=True),
    )(struct, u_local)


def fused_kernel(first, parts, struct_ref, hit_ref, slot_ref, sig_ref, inv_ref, u_in, zoff_ref, sum_ref,
                 u_vmem, y_acc, part_ref, gather_buf, inv_vmem, load_sem, send_sem, recv_sem, out_sem, in_sem,
                 inv_sem):
    n = u_in.shape[0]
    half = n // 2
    nodes = u_in.shape[1]
    chunk = nodes // parts
    rows = sig_ref.shape[0]
    width = sig_ref.shape[-1]
    me = lax.axis_index("row")
    col = lax.axis_index("col")

    def link(step, direction, part):
        if direction == 0:
            slot = lax.rem(me - (step - 1) + n, n)
            peer = lax.rem(me + 1, n)
        else:
            slot = lax.rem(me + (step - 1), n)
            peer = lax.rem(me + n - 1, n)
        piece = pl.ds(part * chunk, chunk)
        source = u_in if step == first + 1 else u_vmem
        return pltpu.make_async_remote_copy(
            src_ref=source.at[slot, piece], dst_ref=u_vmem.at[slot, piece],
            send_sem=send_sem.at[direction, step - 1 - first, part],
            recv_sem=recv_sem.at[direction, step - 1 - first, part],
            device_id=(peer, col), device_id_type=pl.DeviceIdType.MESH)

    def load(slot):
        return pltpu.make_async_copy(u_in.at[slot], u_vmem.at[slot], load_sem.at[slot])

    def wrap(offset):
        return lax.rem(me + offset + 2 * n, n)

    barrier = pltpu.get_barrier_semaphore()
    for offset in range(1, n):
        pl.semaphore_signal(barrier, inc=1, device_id=(lax.rem(me + offset, n), col),
                            device_id_type=pl.DeviceIdType.MESH)
    pl.semaphore_wait(barrier, n - 1)
    for offset in range(-first, first + 1):
        load(wrap(offset)).start()
    inv_copy = pltpu.make_async_copy(inv_ref.at[me], inv_vmem, inv_sem.at[0])
    inv_copy.start()

    started = []

    def send_step(step):
        for direction in (0, 1):
            for part in step_parts(step, direction, half, parts):
                copy = link(step, direction, part)
                copy.start()
                started.append(copy)

    send_step(first + 1)

    def lhs_block(k, slot):
        return sig_ref[:, struct_ref[k, slot]].reshape(rows * width, width)

    def add_single(slot):
        def node(k, carry):
            y_acc[k] += jnp.dot(lhs_block(k, slot), u_vmem[slot, k], precision=high,
                                preferred_element_type=jnp.float32)
            return carry
        lax.fori_loop(0, nodes, node, 0)

    def add_pair(one, two):
        def node(k, carry):
            lhs = jnp.concatenate([lhs_block(k, one), lhs_block(k, two)], axis=1)
            rhs = jnp.concatenate([u_vmem[one, k], u_vmem[two, k]], axis=0)
            y_acc[k] += jnp.dot(lhs, rhs, precision=high, preferred_element_type=jnp.float32)
            return carry
        lax.fori_loop(0, nodes, node, 0)

    def ring_event(step):
        for direction in (0, 1):
            for part in step_parts(step, direction, half, parts):
                link(step, direction, part).wait_recv()
        if step < half:
            send_step(step + 1)

    def arrived(step):
        if step < half:
            add_pair(wrap(-step), wrap(step))
        else:
            add_single(wrap(half))

    processed = first
    load(me).wait()
    y_acc[...] = jnp.zeros_like(y_acc)
    add_single(me)
    for offset in range(1, first + 1):
        load(wrap(-offset)).wait()
        load(wrap(offset)).wait()
        add_pair(wrap(-offset), wrap(offset))
        if offset % 2 == 0 and processed < half:
            processed += 1
            ring_event(processed)
    done = first + 1
    while done < half:
        if done <= processed:
            arrived(done)
            done += 1
        else:
            processed += 1
            ring_event(processed)
    while processed < half:
        processed += 1
        ring_event(processed)
    last = wrap(half)

    for copy in started:
        copy.wait_send()

    def share_to(k):
        return pltpu.make_async_remote_copy(
            src_ref=part_ref.at[k], dst_ref=gather_buf.at[me],
            send_sem=out_sem.at[k], recv_sem=in_sem.at[me],
            device_id=(k, col), device_id_type=pl.DeviceIdType.MESH)

    def share_from(j):
        return pltpu.make_async_remote_copy(
            src_ref=part_ref.at[j], dst_ref=gather_buf.at[j],
            send_sem=out_sem.at[j], recv_sem=in_sem.at[j],
            device_id=(j, col), device_id_type=pl.DeviceIdType.MESH)

    def finish(k, carry):
        y = y_acc[k] + jnp.dot(lhs_block(k, last), u_vmem[last, k], precision=high,
                               preferred_element_type=jnp.float32)
        y = y.reshape(rows, width, width)
        total = jnp.zeros((width, width), jnp.float32)
        for j in range(rows):
            hits = hit_ref[k, j]
            slot = jnp.minimum(slot_ref[k, j], n - 1)
            term = jnp.dot(jnp.transpose(u_vmem[slot, k]), y[j], precision=high,
                           preferred_element_type=jnp.float32)
            total = total + jnp.where(hits > 0, term, 0.0)
            zoff_ref[k, j] = jnp.where(hits > 0, -y[j], 0.0)
        part_ref[k] = total

        @pl.when((k >= 1) & (k - 1 != me))
        def _():
            share_to(k - 1).start()

        return carry

    lax.fori_loop(0, nodes, finish, 0)

    @pl.when(me != nodes - 1)
    def _():
        share_to(nodes - 1).start()

    gather_buf[me] = part_ref[me]
    for j in range(n):
        @pl.when(me != j)
        def _():
            share_to(j).wait_send()
            share_from(j).wait_recv()

    inv_copy.wait()
    inverse = inv_vmem[...]
    inverse_part = jnp.dot(jnp.transpose(inverse), inverse, precision=high,
                           preferred_element_type=jnp.float32)
    sum_ref[0] = inverse_part + jnp.sum(gather_buf[...], axis=0)


def fused_call(struct, hit, slot, sigma_rows, inverse_share, u_all, first, parts):
    slots, nodes, width, _ = u_all.shape
    rows = sigma_rows.shape[0]
    later = slots // 2 - first
    flops = 2 * nodes * slots * rows * width ** 3 * 3
    return pl.pallas_call(
        functools.partial(fused_kernel, first, parts),
        out_shape=[
            jax.ShapeDtypeStruct((nodes, rows, width, width), jnp.float32),
            jax.ShapeDtypeStruct((1, width, width), jnp.float32),
        ],
        in_specs=[
            pl.BlockSpec(memory_space=pltpu.SMEM),
            pl.BlockSpec(memory_space=pltpu.SMEM),
            pl.BlockSpec(memory_space=pltpu.SMEM),
            pl.BlockSpec(memory_space=pltpu.VMEM),
            pl.BlockSpec(memory_space=pl.ANY),
            pl.BlockSpec(memory_space=pl.ANY),
        ],
        out_specs=[
            pl.BlockSpec(memory_space=pltpu.VMEM),
            pl.BlockSpec(memory_space=pltpu.VMEM),
        ],
        scratch_shapes=[
            pltpu.VMEM(u_all.shape, jnp.float32),
            pltpu.VMEM((nodes, rows * width, width), jnp.float32),
            pltpu.VMEM((nodes, width, width), jnp.float32),
            pltpu.VMEM((slots, width, width), jnp.float32),
            pltpu.VMEM((width, width), jnp.float32),
            pltpu.SemaphoreType.DMA((slots,)),
            pltpu.SemaphoreType.DMA((2, later, parts)),
            pltpu.SemaphoreType.DMA((2, later, parts)),
            pltpu.SemaphoreType.DMA((slots,)),
            pltpu.SemaphoreType.DMA((slots,)),
            pltpu.SemaphoreType.DMA((1,)),
        ],
        compiler_params=pltpu.CompilerParams(collective_id=1, has_side_effects=True,
                                             vmem_limit_bytes=60 * 1024 * 1024),
        cost_estimate=pl.CostEstimate(flops=flops, transcendentals=0,
                                      bytes_accessed=4 * (sigma_rows.size + u_all.size)),
    )(struct, hit, slot, sigma_rows, inverse_share, u_all)


def body(sigma_anc, factor, diag_inv, struct):
    row_count = sigma_anc.shape[0]
    sigma_rows = lax.all_gather(sigma_anc, "col", axis=1, tiled=True)
    u_local = jnp.einsum("kij,kjl->kil", factor[0], diag_inv, precision=high)
    first, parts = 4, 8
    u_head, hit, slot = ring_gather(struct, u_local, lax.axis_size("row"), row_count, first, parts)
    z_off, z_diag = fused_call(struct, hit, slot, sigma_rows, diag_inv, u_head, first, parts)
    return (z_off, z_diag)


def solution(mesh):
    in_specs = (
        P("row", "col", None, None),
        P("row", "col", None, None),
        P("col", None, None),
        P("col", None),
    )
    out_specs = (P("col", "row", None, None), P(("col", "row"), None, None))
    return jax.shard_map(body, mesh=mesh, in_specs=in_specs, out_specs=out_specs, check_vma=False)
```

```python
import functools

import jax
import jax.numpy as jnp
from jax import lax
from jax.experimental import pallas as pl
from jax.experimental.pallas import tpu as pltpu
from jax.sharding import PartitionSpec as P

high = lax.Precision.HIGH


def greet_neighbours(me, col, n):
    barrier = pltpu.get_barrier_semaphore()
    for peer in (lax.rem(me + n - 1, n), lax.rem(me + 1, n)):
        pl.semaphore_signal(barrier, inc=1, device_id=(peer, col), device_id_type=pl.DeviceIdType.MESH)
    pl.semaphore_wait(barrier, 2)


def step_parts(step, direction, half, parts):
    if step < half:
        return range(parts)
    if direction == 0:
        return range(parts // 2)
    return range(parts // 2, parts)


def ring_kernel(steps, parts, rows, struct_ref, u_ref, out_ref, hit_ref, slot_ref, copy_sem, send_sem, recv_sem):
    n = out_ref.shape[0]
    chunk = out_ref.shape[1] // parts
    me = lax.axis_index("row")
    col = lax.axis_index("col")

    def link(step, direction, part):
        if direction == 0:
            slot = lax.rem(me - (step - 1) + n, n)
            peer = lax.rem(me + 1, n)
        else:
            slot = lax.rem(me + (step - 1), n)
            peer = lax.rem(me + n - 1, n)
        piece = pl.ds(part * chunk, chunk)
        return pltpu.make_async_remote_copy(
            src_ref=out_ref.at[slot, piece], dst_ref=out_ref.at[slot, piece],
            send_sem=send_sem.at[direction, step - 1, part],
            recv_sem=recv_sem.at[direction, step - 1, part],
            device_id=(peer, col), device_id_type=pl.DeviceIdType.MESH)

    own = pltpu.make_async_copy(u_ref, out_ref.at[me], copy_sem.at[0])
    own.start()
    greet_neighbours(me, col, n)
    own.wait()

    started = []
    for step in range(1, steps + 1):
        for direction in (0, 1):
            for part in range(parts):
                if step > 1:
                    link(step - 1, direction, part).wait_recv()
                copy = link(step, direction, part)
                copy.start()
                started.append(copy)
        if step <= rows:
            j = step - 1
            base = me * rows + j

            def member(k, carry):
                def scan(s, acc):
                    hit = (struct_ref[k, s] == base).astype(jnp.int32)
                    return acc[0] + hit, acc[1] + hit * s
                hits, slot = lax.fori_loop(0, n, scan, (jnp.int32(0), jnp.int32(0)))
                hit_ref[k, j] = hits
                slot_ref[k, j] = slot
                return carry

            lax.fori_loop(0, struct_ref.shape[0], member, 0)
    for direction in (0, 1):
        for part in range(parts):
            link(steps, direction, part).wait_recv()
    for copy in started:
        copy.wait_send()


def ring_gather(struct, u_local, slots, rows, steps, parts):
    nodes, width, _ = u_local.shape
    return pl.pallas_call(
        functools.partial(ring_kernel, steps, parts, rows),
        out_shape=[
            jax.ShapeDtypeStruct((slots, nodes, width, width), jnp.float32),
            jax.ShapeDtypeStruct((nodes, rows), jnp.int32),
            jax.ShapeDtypeStruct((nodes, rows), jnp.int32),
        ],
        in_specs=[pl.BlockSpec(memory_space=pltpu.SMEM), pl.BlockSpec(memory_space=pl.ANY)],
        out_specs=[
            pl.BlockSpec(memory_space=pl.ANY),
            pl.BlockSpec(memory_space=pltpu.SMEM),
            pl.BlockSpec(memory_space=pltpu.SMEM),
        ],
        scratch_shapes=[
            pltpu.SemaphoreType.DMA((1,)),
            pltpu.SemaphoreType.DMA((2, steps, parts)),
            pltpu.SemaphoreType.DMA((2, steps, parts)),
        ],
        compiler_params=pltpu.CompilerParams(collective_id=0, has_side_effects=True),
    )(struct, u_local)


def fused_kernel(first, parts, struct_ref, hit_ref, slot_ref, sig_ref, inv_ref, u_in, zoff_ref, sum_ref,
                 u_vmem, y_acc, part_ref, gather_buf, inv_vmem, load_sem, send_sem, recv_sem, out_sem, in_sem,
                 inv_sem):
    n = u_in.shape[0]
    half = n // 2
    nodes = u_in.shape[1]
    chunk = nodes // parts
    rows = sig_ref.shape[0]
    width = sig_ref.shape[-1]
    me = lax.axis_index("row")
    col = lax.axis_index("col")

    def link(step, direction, part):
        if direction == 0:
            slot = lax.rem(me - (step - 1) + n, n)
            peer = lax.rem(me + 1, n)
        else:
            slot = lax.rem(me + (step - 1), n)
            peer = lax.rem(me + n - 1, n)
        piece = pl.ds(part * chunk, chunk)
        source = u_in if step == first + 1 else u_vmem
        return pltpu.make_async_remote_copy(
            src_ref=source.at[slot, piece], dst_ref=u_vmem.at[slot, piece],
            send_sem=send_sem.at[direction, step - 1 - first, part],
            recv_sem=recv_sem.at[direction, step - 1 - first, part],
            device_id=(peer, col), device_id_type=pl.DeviceIdType.MESH)

    def load(slot):
        return pltpu.make_async_copy(u_in.at[slot], u_vmem.at[slot], load_sem.at[slot])

    def wrap(offset):
        return lax.rem(me + offset + 2 * n, n)

    barrier = pltpu.get_barrier_semaphore()
    for offset in range(1, n):
        pl.semaphore_signal(barrier, inc=1, device_id=(lax.rem(me + offset, n), col),
                            device_id_type=pl.DeviceIdType.MESH)
    pl.semaphore_wait(barrier, n - 1)
    for offset in range(-first, first + 1):
        load(wrap(offset)).start()
    inv_copy = pltpu.make_async_copy(inv_ref.at[me], inv_vmem, inv_sem.at[0])
    inv_copy.start()

    started = []

    def send_step(step):
        for direction in (0, 1):
            for part in step_parts(step, direction, half, parts):
                copy = link(step, direction, part)
                copy.start()
                started.append(copy)

    send_step(first + 1)

    def lhs_block(k, slot):
        return sig_ref[:, struct_ref[k, slot]].reshape(rows * width, width)

    def add_single(slot):
        def node(k, carry):
            y_acc[k] += jnp.dot(lhs_block(k, slot), u_vmem[slot, k], precision=high,
                                preferred_element_type=jnp.float32)
            return carry
        lax.fori_loop(0, nodes, node, 0)

    def add_pair(one, two):
        def node(k, carry):
            lhs = jnp.concatenate([lhs_block(k, one), lhs_block(k, two)], axis=1)
            rhs = jnp.concatenate([u_vmem[one, k], u_vmem[two, k]], axis=0)
            y_acc[k] += jnp.dot(lhs, rhs, precision=high, preferred_element_type=jnp.float32)
            return carry
        lax.fori_loop(0, nodes, node, 0)

    def ring_event(step):
        for direction in (0, 1):
            for part in step_parts(step, direction, half, parts):
                link(step, direction, part).wait_recv()
        if step < half:
            send_step(step + 1)

    def arrived(step):
        if step < half:
            add_pair(wrap(-step), wrap(step))
        else:
            add_single(wrap(half))

    processed = first
    load(me).wait()
    y_acc[...] = jnp.zeros_like(y_acc)
    add_single(me)
    for offset in range(1, first + 1):
        load(wrap(-offset)).wait()
        load(wrap(offset)).wait()
        add_pair(wrap(-offset), wrap(offset))
        if offset % 2 == 0 and processed < half:
            processed += 1
            ring_event(processed)
    done = first + 1
    while done < half:
        if done <= processed:
            arrived(done)
            done += 1
        else:
            processed += 1
            ring_event(processed)
    while processed < half:
        processed += 1
        ring_event(processed)
    last = wrap(half)

    for copy in started:
        copy.wait_send()

    def share_to(k):
        return pltpu.make_async_remote_copy(
            src_ref=part_ref.at[k], dst_ref=gather_buf.at[me],
            send_sem=out_sem.at[k], recv_sem=in_sem.at[me],
            device_id=(k, col), device_id_type=pl.DeviceIdType.MESH)

    def share_from(j):
        return pltpu.make_async_remote_copy(
            src_ref=part_ref.at[j], dst_ref=gather_buf.at[j],
            send_sem=out_sem.at[j], recv_sem=in_sem.at[j],
            device_id=(j, col), device_id_type=pl.DeviceIdType.MESH)

    def finish(k, carry):
        y = y_acc[k] + jnp.dot(lhs_block(k, last), u_vmem[last, k], precision=high,
                               preferred_element_type=jnp.float32)
        y = y.reshape(rows, width, width)
        total = jnp.zeros((width, width), jnp.float32)
        for j in range(rows):
            hits = hit_ref[k, j]
            slot = jnp.minimum(slot_ref[k, j], n - 1)
            term = jnp.dot(jnp.transpose(u_vmem[slot, k]), y[j], precision=high,
                           preferred_element_type=jnp.float32)
            total = total + jnp.where(hits > 0, term, 0.0)
            zoff_ref[k, j] = jnp.where(hits > 0, -y[j], 0.0)
        part_ref[k] = total

        @pl.when((k >= 1) & (k - 1 != me))
        def _():
            share_to(k - 1).start()

        return carry

    lax.fori_loop(0, nodes, finish, 0)

    @pl.when(me != nodes - 1)
    def _():
        share_to(nodes - 1).start()

    gather_buf[me] = part_ref[me]
    for j in range(n):
        @pl.when(me != j)
        def _():
            share_to(j).wait_send()
            share_from(j).wait_recv()

    inv_copy.wait()
    inverse = inv_vmem[...]
    inverse_part = jnp.dot(jnp.transpose(inverse), inverse, precision=high,
                           preferred_element_type=jnp.float32)
    sum_ref[0] = inverse_part + jnp.sum(gather_buf[...], axis=0)


def fused_call(struct, hit, slot, sigma_rows, inverse_share, u_all, first, parts):
    slots, nodes, width, _ = u_all.shape
    rows = sigma_rows.shape[0]
    later = slots // 2 - first
    flops = 2 * nodes * slots * rows * width ** 3 * 3
    return pl.pallas_call(
        functools.partial(fused_kernel, first, parts),
        out_shape=[
            jax.ShapeDtypeStruct((nodes, rows, width, width), jnp.float32),
            jax.ShapeDtypeStruct((1, width, width), jnp.float32),
        ],
        in_specs=[
            pl.BlockSpec(memory_space=pltpu.SMEM),
            pl.BlockSpec(memory_space=pltpu.SMEM),
            pl.BlockSpec(memory_space=pltpu.SMEM),
            pl.BlockSpec(memory_space=pltpu.VMEM),
            pl.BlockSpec(memory_space=pl.ANY),
            pl.BlockSpec(memory_space=pl.ANY),
        ],
        out_specs=[
            pl.BlockSpec(memory_space=pltpu.VMEM),
            pl.BlockSpec(memory_space=pltpu.VMEM),
        ],
        scratch_shapes=[
            pltpu.VMEM(u_all.shape, jnp.float32),
            pltpu.VMEM((nodes, rows * width, width), jnp.float32),
            pltpu.VMEM((nodes, width, width), jnp.float32),
            pltpu.VMEM((slots, width, width), jnp.float32),
            pltpu.VMEM((width, width), jnp.float32),
            pltpu.SemaphoreType.DMA((slots,)),
            pltpu.SemaphoreType.DMA((2, later, parts)),
            pltpu.SemaphoreType.DMA((2, later, parts)),
            pltpu.SemaphoreType.DMA((slots,)),
            pltpu.SemaphoreType.DMA((slots,)),
            pltpu.SemaphoreType.DMA((1,)),
        ],
        compiler_params=pltpu.CompilerParams(collective_id=1, has_side_effects=True,
                                             vmem_limit_bytes=60 * 1024 * 1024),
        cost_estimate=pl.CostEstimate(flops=flops, transcendentals=0,
                                      bytes_accessed=4 * (sigma_rows.size + u_all.size)),
    )(struct, hit, slot, sigma_rows, inverse_share, u_all)


def body(sigma_anc, factor, diag_inv, struct):
    row_count = sigma_anc.shape[0]
    sigma_rows = lax.all_gather(sigma_anc, "col", axis=1, tiled=True)
    u_local = jnp.einsum("kij,kjl->kil", factor[0], diag_inv, precision=high)
    first, parts = 4, 4
    u_head, hit, slot = ring_gather(struct, u_local, lax.axis_size("row"), row_count, first, parts)
    z_off, z_diag = fused_call(struct, hit, slot, sigma_rows, diag_inv, u_head, first, parts)
    return (z_off, z_diag)


def solution(mesh):
    in_specs = (
        P("row", "col", None, None),
        P("row", "col", None, None),
        P("col", None, None),
        P("col", None),
    )
    out_specs = (P("col", "row", None, None), P(("col", "row"), None, None))
    return jax.shard_map(body, mesh=mesh, in_specs=in_specs, out_specs=out_specs, check_vma=False)
```

```python
import functools

import jax
import jax.numpy as jnp
from jax import lax
from jax.experimental import pallas as pl
from jax.experimental.pallas import tpu as pltpu
from jax.sharding import PartitionSpec as P

high = lax.Precision.HIGH


def greet_neighbours(me, col, n):
    barrier = pltpu.get_barrier_semaphore()
    for peer in (lax.rem(me + n - 1, n), lax.rem(me + 1, n)):
        pl.semaphore_signal(barrier, inc=1, device_id=(peer, col), device_id_type=pl.DeviceIdType.MESH)
    pl.semaphore_wait(barrier, 2)


def step_parts(step, direction, half, parts):
    if step < half:
        return range(parts)
    if direction == 0:
        return range(parts // 2)
    return range(parts // 2, parts)


def ring_kernel(steps, parts, rows, struct_ref, factor_ref, inv_ref, out_ref, hit_ref, slot_ref, u_scr,
                copy_sem, send_sem, recv_sem):
    n = out_ref.shape[0]
    chunk = out_ref.shape[1] // parts
    me = lax.axis_index("row")
    col = lax.axis_index("col")

    def link(step, direction, part):
        if direction == 0:
            slot = lax.rem(me - (step - 1) + n, n)
            peer = lax.rem(me + 1, n)
        else:
            slot = lax.rem(me + (step - 1), n)
            peer = lax.rem(me + n - 1, n)
        piece = pl.ds(part * chunk, chunk)
        return pltpu.make_async_remote_copy(
            src_ref=out_ref.at[slot, piece], dst_ref=out_ref.at[slot, piece],
            send_sem=send_sem.at[direction, step - 1, part],
            recv_sem=recv_sem.at[direction, step - 1, part],
            device_id=(peer, col), device_id_type=pl.DeviceIdType.MESH)

    def make_u(k, carry):
        u_scr[k] = jnp.dot(factor_ref[k], inv_ref[k], precision=high, preferred_element_type=jnp.float32)
        return carry

    lax.fori_loop(0, u_scr.shape[0], make_u, 0)
    greet_neighbours(me, col, n)
    own = pltpu.make_async_copy(u_scr, out_ref.at[me], copy_sem.at[0])
    own.start()
    own.wait()

    started = []
    for step in range(1, steps + 1):
        for direction in (0, 1):
            for part in range(parts):
                if step > 1:
                    link(step - 1, direction, part).wait_recv()
                copy = link(step, direction, part)
                copy.start()
                started.append(copy)
        if step <= rows:
            j = step - 1
            base = me * rows + j

            def member(k, carry):
                def scan(s, acc):
                    hit = (struct_ref[k, s] == base).astype(jnp.int32)
                    return acc[0] + hit, acc[1] + hit * s
                hits, slot = lax.fori_loop(0, n, scan, (jnp.int32(0), jnp.int32(0)))
                hit_ref[k, j] = hits
                slot_ref[k, j] = slot
                return carry

            lax.fori_loop(0, struct_ref.shape[0], member, 0)
    for direction in (0, 1):
        for part in range(parts):
            link(steps, direction, part).wait_recv()
    for copy in started:
        copy.wait_send()


def ring_gather(struct, factor_own, diag_inv, slots, rows, steps, parts):
    nodes, width, _ = diag_inv.shape
    return pl.pallas_call(
        functools.partial(ring_kernel, steps, parts, rows),
        out_shape=[
            jax.ShapeDtypeStruct((slots, nodes, width, width), jnp.float32),
            jax.ShapeDtypeStruct((nodes, rows), jnp.int32),
            jax.ShapeDtypeStruct((nodes, rows), jnp.int32),
        ],
        in_specs=[pl.BlockSpec(memory_space=pltpu.SMEM), pl.BlockSpec(memory_space=pltpu.VMEM),
                  pl.BlockSpec(memory_space=pltpu.VMEM)],
        out_specs=[
            pl.BlockSpec(memory_space=pl.ANY),
            pl.BlockSpec(memory_space=pltpu.SMEM),
            pl.BlockSpec(memory_space=pltpu.SMEM),
        ],
        scratch_shapes=[
            pltpu.VMEM((nodes, width, width), jnp.float32),
            pltpu.SemaphoreType.DMA((1,)),
            pltpu.SemaphoreType.DMA((2, steps, parts)),
            pltpu.SemaphoreType.DMA((2, steps, parts)),
        ],
        compiler_params=pltpu.CompilerParams(collective_id=0, has_side_effects=True),
    )(struct, factor_own, diag_inv)


def fused_kernel(first, parts, struct_ref, hit_ref, slot_ref, sig_ref, inv_ref, u_in, zoff_ref, sum_ref,
                 u_vmem, y_acc, part_ref, gather_buf, inv_vmem, load_sem, send_sem, recv_sem, out_sem, in_sem,
                 inv_sem):
    n = u_in.shape[0]
    half = n // 2
    nodes = u_in.shape[1]
    chunk = nodes // parts
    rows = sig_ref.shape[0]
    width = sig_ref.shape[-1]
    me = lax.axis_index("row")
    col = lax.axis_index("col")

    def link(step, direction, part):
        if direction == 0:
            slot = lax.rem(me - (step - 1) + n, n)
            peer = lax.rem(me + 1, n)
        else:
            slot = lax.rem(me + (step - 1), n)
            peer = lax.rem(me + n - 1, n)
        piece = pl.ds(part * chunk, chunk)
        source = u_in if step == first + 1 else u_vmem
        return pltpu.make_async_remote_copy(
            src_ref=source.at[slot, piece], dst_ref=u_vmem.at[slot, piece],
            send_sem=send_sem.at[direction, step - 1 - first, part],
            recv_sem=recv_sem.at[direction, step - 1 - first, part],
            device_id=(peer, col), device_id_type=pl.DeviceIdType.MESH)

    def load(slot):
        return pltpu.make_async_copy(u_in.at[slot], u_vmem.at[slot], load_sem.at[slot])

    def wrap(offset):
        return lax.rem(me + offset + 2 * n, n)

    barrier = pltpu.get_barrier_semaphore()
    for offset in range(1, n):
        pl.semaphore_signal(barrier, inc=1, device_id=(lax.rem(me + offset, n), col),
                            device_id_type=pl.DeviceIdType.MESH)
    pl.semaphore_wait(barrier, n - 1)
    for offset in range(-first, first + 1):
        load(wrap(offset)).start()
    inv_copy = pltpu.make_async_copy(inv_ref.at[me], inv_vmem, inv_sem.at[0])
    inv_copy.start()

    started = []

    def send_step(step):
        for direction in (0, 1):
            for part in step_parts(step, direction, half, parts):
                copy = link(step, direction, part)
                copy.start()
                started.append(copy)

    send_step(first + 1)

    def lhs_block(k, slot):
        return sig_ref[:, struct_ref[k, slot]].reshape(rows * width, width)

    def add_single(slot):
        def node(k, carry):
            y_acc[k] += jnp.dot(lhs_block(k, slot), u_vmem[slot, k], precision=high,
                                preferred_element_type=jnp.float32)
            return carry
        lax.fori_loop(0, nodes, node, 0)

    def add_pair(one, two):
        def node(k, carry):
            lhs = jnp.concatenate([lhs_block(k, one), lhs_block(k, two)], axis=1)
            rhs = jnp.concatenate([u_vmem[one, k], u_vmem[two, k]], axis=0)
            y_acc[k] += jnp.dot(lhs, rhs, precision=high, preferred_element_type=jnp.float32)
            return carry
        lax.fori_loop(0, nodes, node, 0)

    def ring_event(step):
        for direction in (0, 1):
            for part in step_parts(step, direction, half, parts):
                link(step, direction, part).wait_recv()
        if step < half:
            send_step(step + 1)

    def arrived(step):
        if step < half:
            add_pair(wrap(-step), wrap(step))
        else:
            add_single(wrap(half))

    processed = first
    load(me).wait()
    y_acc[...] = jnp.zeros_like(y_acc)
    add_single(me)
    for offset in range(1, first + 1):
        load(wrap(-offset)).wait()
        load(wrap(offset)).wait()
        add_pair(wrap(-offset), wrap(offset))
        if offset % 2 == 0 and processed < half:
            processed += 1
            ring_event(processed)
    done = first + 1
    while done < half:
        if done <= processed:
            arrived(done)
            done += 1
        else:
            processed += 1
            ring_event(processed)
    while processed < half:
        processed += 1
        ring_event(processed)
    last = wrap(half)

    for copy in started:
        copy.wait_send()

    def share_to(k):
        return pltpu.make_async_remote_copy(
            src_ref=part_ref.at[k], dst_ref=gather_buf.at[me],
            send_sem=out_sem.at[k], recv_sem=in_sem.at[me],
            device_id=(k, col), device_id_type=pl.DeviceIdType.MESH)

    def share_from(j):
        return pltpu.make_async_remote_copy(
            src_ref=part_ref.at[j], dst_ref=gather_buf.at[j],
            send_sem=out_sem.at[j], recv_sem=in_sem.at[j],
            device_id=(j, col), device_id_type=pl.DeviceIdType.MESH)

    def finish(k, carry):
        y = y_acc[k] + jnp.dot(lhs_block(k, last), u_vmem[last, k], precision=high,
                               preferred_element_type=jnp.float32)
        y = y.reshape(rows, width, width)
        total = jnp.zeros((width, width), jnp.float32)
        for j in range(rows):
            hits = hit_ref[k, j]
            slot = jnp.minimum(slot_ref[k, j], n - 1)
            term = jnp.dot(jnp.transpose(u_vmem[slot, k]), y[j], precision=high,
                           preferred_element_type=jnp.float32)
            total = total + jnp.where(hits > 0, term, 0.0)
            zoff_ref[k, j] = jnp.where(hits > 0, -y[j], 0.0)
        part_ref[k] = total

        @pl.when((k >= 1) & (k - 1 != me))
        def _():
            share_to(k - 1).start()

        return carry

    lax.fori_loop(0, nodes, finish, 0)

    @pl.when(me != nodes - 1)
    def _():
        share_to(nodes - 1).start()

    gather_buf[me] = part_ref[me]
    for j in range(n):
        @pl.when(me != j)
        def _():
            share_to(j).wait_send()
            share_from(j).wait_recv()

    inv_copy.wait()
    inverse = inv_vmem[...]
    inverse_part = jnp.dot(jnp.transpose(inverse), inverse, precision=high,
                           preferred_element_type=jnp.float32)
    sum_ref[0] = inverse_part + jnp.sum(gather_buf[...], axis=0)


def fused_call(struct, hit, slot, sigma_rows, inverse_share, u_all, first, parts):
    slots, nodes, width, _ = u_all.shape
    rows = sigma_rows.shape[0]
    later = slots // 2 - first
    flops = 2 * nodes * slots * rows * width ** 3 * 3
    return pl.pallas_call(
        functools.partial(fused_kernel, first, parts),
        out_shape=[
            jax.ShapeDtypeStruct((nodes, rows, width, width), jnp.float32),
            jax.ShapeDtypeStruct((1, width, width), jnp.float32),
        ],
        in_specs=[
            pl.BlockSpec(memory_space=pltpu.SMEM),
            pl.BlockSpec(memory_space=pltpu.SMEM),
            pl.BlockSpec(memory_space=pltpu.SMEM),
            pl.BlockSpec(memory_space=pltpu.VMEM),
            pl.BlockSpec(memory_space=pl.ANY),
            pl.BlockSpec(memory_space=pl.ANY),
        ],
        out_specs=[
            pl.BlockSpec(memory_space=pltpu.VMEM),
            pl.BlockSpec(memory_space=pltpu.VMEM),
        ],
        scratch_shapes=[
            pltpu.VMEM(u_all.shape, jnp.float32),
            pltpu.VMEM((nodes, rows * width, width), jnp.float32),
            pltpu.VMEM((nodes, width, width), jnp.float32),
            pltpu.VMEM((slots, width, width), jnp.float32),
            pltpu.VMEM((width, width), jnp.float32),
            pltpu.SemaphoreType.DMA((slots,)),
            pltpu.SemaphoreType.DMA((2, later, parts)),
            pltpu.SemaphoreType.DMA((2, later, parts)),
            pltpu.SemaphoreType.DMA((slots,)),
            pltpu.SemaphoreType.DMA((slots,)),
            pltpu.SemaphoreType.DMA((1,)),
        ],
        compiler_params=pltpu.CompilerParams(collective_id=1, has_side_effects=True,
                                             vmem_limit_bytes=60 * 1024 * 1024),
        cost_estimate=pl.CostEstimate(flops=flops, transcendentals=0,
                                      bytes_accessed=4 * (sigma_rows.size + u_all.size)),
    )(struct, hit, slot, sigma_rows, inverse_share, u_all)


def body(sigma_anc, factor, diag_inv, struct):
    row_count = sigma_anc.shape[0]
    sigma_rows = lax.all_gather(sigma_anc, "col", axis=1, tiled=True)
    first, parts = 4, 4
    u_head, hit, slot = ring_gather(struct, factor[0], diag_inv, lax.axis_size("row"), row_count, first, parts)
    z_off, z_diag = fused_call(struct, hit, slot, sigma_rows, diag_inv, u_head, first, parts)
    return (z_off, z_diag)


def solution(mesh):
    in_specs = (
        P("row", "col", None, None),
        P("row", "col", None, None),
        P("col", None, None),
        P("col", None),
    )
    out_specs = (P("col", "row", None, None), P(("col", "row"), None, None))
    return jax.shard_map(body, mesh=mesh, in_specs=in_specs, out_specs=out_specs, check_vma=False)
```

```python
import functools

import jax
import jax.numpy as jnp
from jax import lax
from jax.experimental import pallas as pl
from jax.experimental.pallas import tpu as pltpu
from jax.sharding import PartitionSpec as P

high = lax.Precision.HIGH


def greet_neighbours(me, col, n):
    barrier = pltpu.get_barrier_semaphore()
    for peer in (lax.rem(me + n - 1, n), lax.rem(me + 1, n)):
        pl.semaphore_signal(barrier, inc=1, device_id=(peer, col), device_id_type=pl.DeviceIdType.MESH)
    pl.semaphore_wait(barrier, 2)


def step_parts(step, direction, half, parts):
    if step < half:
        return range(parts)
    if direction == 0:
        return range(parts // 2)
    return range(parts // 2, parts)


def ring_kernel(steps, parts, rows, struct_ref, factor_ref, inv_ref, out_ref, hit_ref, slot_ref, u_scr,
                copy_sem, send_sem, recv_sem):
    n = out_ref.shape[0]
    chunk = out_ref.shape[1] // parts
    me = lax.axis_index("row")
    col = lax.axis_index("col")

    def link(step, direction, part):
        if direction == 0:
            slot = lax.rem(me - (step - 1) + n, n)
            peer = lax.rem(me + 1, n)
        else:
            slot = lax.rem(me + (step - 1), n)
            peer = lax.rem(me + n - 1, n)
        piece = pl.ds(part * chunk, chunk)
        return pltpu.make_async_remote_copy(
            src_ref=out_ref.at[slot, piece], dst_ref=out_ref.at[slot, piece],
            send_sem=send_sem.at[direction, step - 1, part],
            recv_sem=recv_sem.at[direction, step - 1, part],
            device_id=(peer, col), device_id_type=pl.DeviceIdType.MESH)

    def make_u(k, carry):
        u_scr[k] = jnp.dot(factor_ref[k], inv_ref[k], precision=high, preferred_element_type=jnp.float32)
        return carry

    lax.fori_loop(0, u_scr.shape[0], make_u, 0)
    greet_neighbours(me, col, n)
    own = pltpu.make_async_copy(u_scr, out_ref.at[me], copy_sem.at[0])
    own.start()
    own.wait()

    started = []
    for step in range(1, steps + 1):
        for direction in (0, 1):
            for part in range(parts):
                if step > 1:
                    link(step - 1, direction, part).wait_recv()
                copy = link(step, direction, part)
                copy.start()
                started.append(copy)
        if step <= rows:
            j = step - 1
            base = me * rows + j

            def member(k, carry):
                def scan(s, acc):
                    hit = (struct_ref[k, s] == base).astype(jnp.int32)
                    return acc[0] + hit, acc[1] + hit * s
                hits, slot = lax.fori_loop(0, n, scan, (jnp.int32(0), jnp.int32(0)))
                hit_ref[k, j] = hits
                slot_ref[k, j] = slot
                return carry

            lax.fori_loop(0, struct_ref.shape[0], member, 0)
    for direction in (0, 1):
        for part in range(parts):
            link(steps, direction, part).wait_recv()
    for copy in started:
        copy.wait_send()


def ring_gather(struct, factor_own, diag_inv, slots, rows, steps, parts):
    nodes, width, _ = diag_inv.shape
    return pl.pallas_call(
        functools.partial(ring_kernel, steps, parts, rows),
        out_shape=[
            jax.ShapeDtypeStruct((slots, nodes, width, width), jnp.float32),
            jax.ShapeDtypeStruct((nodes, rows), jnp.int32),
            jax.ShapeDtypeStruct((nodes, rows), jnp.int32),
        ],
        in_specs=[pl.BlockSpec(memory_space=pltpu.SMEM), pl.BlockSpec(memory_space=pltpu.VMEM),
                  pl.BlockSpec(memory_space=pltpu.VMEM)],
        out_specs=[
            pl.BlockSpec(memory_space=pl.ANY),
            pl.BlockSpec(memory_space=pltpu.SMEM),
            pl.BlockSpec(memory_space=pltpu.SMEM),
        ],
        scratch_shapes=[
            pltpu.VMEM((nodes, width, width), jnp.float32),
            pltpu.SemaphoreType.DMA((1,)),
            pltpu.SemaphoreType.DMA((2, steps, parts)),
            pltpu.SemaphoreType.DMA((2, steps, parts)),
        ],
        compiler_params=pltpu.CompilerParams(collective_id=0, has_side_effects=True),
    )(struct, factor_own, diag_inv)


def fused_kernel(first, parts, struct_ref, hit_ref, slot_ref, sig_ref, inv_ref, u_in, zoff_ref, sum_ref,
                 u_vmem, y_acc, part_ref, gather_buf, inv_vmem, load_sem, send_sem, recv_sem, out_sem, in_sem,
                 inv_sem):
    n = u_in.shape[0]
    half = n // 2
    nodes = u_in.shape[1]
    chunk = nodes // parts
    rows = sig_ref.shape[0]
    width = sig_ref.shape[-1]
    me = lax.axis_index("row")
    col = lax.axis_index("col")

    def link(step, direction, part):
        if direction == 0:
            slot = lax.rem(me - (step - 1) + n, n)
            peer = lax.rem(me + 1, n)
        else:
            slot = lax.rem(me + (step - 1), n)
            peer = lax.rem(me + n - 1, n)
        piece = pl.ds(part * chunk, chunk)
        source = u_in if step == first + 1 else u_vmem
        return pltpu.make_async_remote_copy(
            src_ref=source.at[slot, piece], dst_ref=u_vmem.at[slot, piece],
            send_sem=send_sem.at[direction, step - 1 - first, part],
            recv_sem=recv_sem.at[direction, step - 1 - first, part],
            device_id=(peer, col), device_id_type=pl.DeviceIdType.MESH)

    def load(slot):
        return pltpu.make_async_copy(u_in.at[slot], u_vmem.at[slot], load_sem.at[slot])

    def wrap(offset):
        return lax.rem(me + offset + 2 * n, n)

    barrier = pltpu.get_barrier_semaphore()
    for offset in range(1, n):
        pl.semaphore_signal(barrier, inc=1, device_id=(lax.rem(me + offset, n), col),
                            device_id_type=pl.DeviceIdType.MESH)
    pl.semaphore_wait(barrier, n - 1)
    for offset in range(-first, first + 1):
        load(wrap(offset)).start()
    inv_copy = pltpu.make_async_copy(inv_ref.at[me], inv_vmem, inv_sem.at[0])
    inv_copy.start()

    started = []

    def send_step(step):
        for direction in (0, 1):
            for part in step_parts(step, direction, half, parts):
                copy = link(step, direction, part)
                copy.start()
                started.append(copy)

    send_step(first + 1)

    def lhs_block(k, slot):
        return sig_ref[:, struct_ref[k, slot]].reshape(rows * width, width)

    def add_single(slot):
        def node(k, carry):
            y_acc[k] += jnp.dot(lhs_block(k, slot), u_vmem[slot, k], precision=high,
                                preferred_element_type=jnp.float32)
            return carry
        lax.fori_loop(0, nodes, node, 0)

    def add_pair(one, two):
        def node(k, carry):
            lhs = jnp.concatenate([lhs_block(k, one), lhs_block(k, two)], axis=1)
            rhs = jnp.concatenate([u_vmem[one, k], u_vmem[two, k]], axis=0)
            y_acc[k] += jnp.dot(lhs, rhs, precision=high, preferred_element_type=jnp.float32)
            return carry
        lax.fori_loop(0, nodes, node, 0)

    def ring_event(step):
        for direction in (0, 1):
            for part in step_parts(step, direction, half, parts):
                link(step, direction, part).wait_recv()
        if step < half:
            send_step(step + 1)

    def arrived(step):
        if step < half:
            add_pair(wrap(-step), wrap(step))
        else:
            add_single(wrap(half))

    processed = first
    load(me).wait()
    y_acc[...] = jnp.zeros_like(y_acc)
    add_single(me)
    for offset in range(1, first + 1):
        load(wrap(-offset)).wait()
        load(wrap(offset)).wait()
        add_pair(wrap(-offset), wrap(offset))
        if offset % 2 == 0 and processed < half:
            processed += 1
            ring_event(processed)
    done = first + 1
    while done < half:
        if done <= processed:
            arrived(done)
            done += 1
        else:
            processed += 1
            ring_event(processed)
    while processed < half:
        processed += 1
        ring_event(processed)
    last = wrap(half)

    for copy in started:
        copy.wait_send()

    def share_to(k):
        return pltpu.make_async_remote_copy(
            src_ref=part_ref.at[k], dst_ref=gather_buf.at[me],
            send_sem=out_sem.at[k], recv_sem=in_sem.at[me],
            device_id=(k, col), device_id_type=pl.DeviceIdType.MESH)

    def share_from(j):
        return pltpu.make_async_remote_copy(
            src_ref=part_ref.at[j], dst_ref=gather_buf.at[j],
            send_sem=out_sem.at[j], recv_sem=in_sem.at[j],
            device_id=(j, col), device_id_type=pl.DeviceIdType.MESH)

    def finish(k, carry):
        y = y_acc[k] + jnp.dot(lhs_block(k, last), u_vmem[last, k], precision=high,
                               preferred_element_type=jnp.float32)
        y = y.reshape(rows, width, width)
        total = jnp.zeros((width, width), jnp.float32)
        for j in range(rows):
            hits = hit_ref[k, j]
            slot = jnp.minimum(slot_ref[k, j], n - 1)
            term = jnp.dot(jnp.transpose(u_vmem[slot, k]), y[j], precision=high,
                           preferred_element_type=jnp.float32)
            total = total + jnp.where(hits > 0, term, 0.0)
            zoff_ref[k, j] = jnp.where(hits > 0, -y[j], 0.0)
        part_ref[k] = total

        @pl.when((k >= 1) & (k - 1 != me))
        def _():
            share_to(k - 1).start()

        return carry

    lax.fori_loop(0, nodes, finish, 0)

    @pl.when(me != nodes - 1)
    def _():
        share_to(nodes - 1).start()

    gather_buf[me] = part_ref[me]
    for j in range(n):
        @pl.when(me != j)
        def _():
            share_to(j).wait_send()
            share_from(j).wait_recv()

    inv_copy.wait()
    inverse = inv_vmem[...]
    inverse_part = jnp.dot(jnp.transpose(inverse), inverse, precision=high,
                           preferred_element_type=jnp.float32)
    sum_ref[0] = inverse_part + jnp.sum(gather_buf[...], axis=0)


def fused_call(struct, hit, slot, sigma_rows, inverse_share, u_all, first, parts):
    slots, nodes, width, _ = u_all.shape
    rows = sigma_rows.shape[0]
    later = slots // 2 - first
    flops = 2 * nodes * slots * rows * width ** 3 * 3
    return pl.pallas_call(
        functools.partial(fused_kernel, first, parts),
        out_shape=[
            jax.ShapeDtypeStruct((nodes, rows, width, width), jnp.float32),
            jax.ShapeDtypeStruct((1, width, width), jnp.float32),
        ],
        in_specs=[
            pl.BlockSpec(memory_space=pltpu.SMEM),
            pl.BlockSpec(memory_space=pltpu.SMEM),
            pl.BlockSpec(memory_space=pltpu.SMEM),
            pl.BlockSpec(memory_space=pltpu.VMEM),
            pl.BlockSpec(memory_space=pl.ANY),
            pl.BlockSpec(memory_space=pl.ANY),
        ],
        out_specs=[
            pl.BlockSpec(memory_space=pltpu.VMEM),
            pl.BlockSpec(memory_space=pltpu.VMEM),
        ],
        scratch_shapes=[
            pltpu.VMEM(u_all.shape, jnp.float32),
            pltpu.VMEM((nodes, rows * width, width), jnp.float32),
            pltpu.VMEM((nodes, width, width), jnp.float32),
            pltpu.VMEM((slots, width, width), jnp.float32),
            pltpu.VMEM((width, width), jnp.float32),
            pltpu.SemaphoreType.DMA((slots,)),
            pltpu.SemaphoreType.DMA((2, later, parts)),
            pltpu.SemaphoreType.DMA((2, later, parts)),
            pltpu.SemaphoreType.DMA((slots,)),
            pltpu.SemaphoreType.DMA((slots,)),
            pltpu.SemaphoreType.DMA((1,)),
        ],
        compiler_params=pltpu.CompilerParams(collective_id=1, has_side_effects=True,
                                             vmem_limit_bytes=60 * 1024 * 1024),
        cost_estimate=pl.CostEstimate(flops=flops, transcendentals=0,
                                      bytes_accessed=4 * (sigma_rows.size + u_all.size)),
    )(struct, hit, slot, sigma_rows, inverse_share, u_all)


def body(sigma_anc, factor, diag_inv, struct):
    row_count = sigma_anc.shape[0]
    sigma_rows = lax.all_gather(sigma_anc, "col", axis=1, tiled=True)
    first, parts = 5, 4
    u_head, hit, slot = ring_gather(struct, factor[0], diag_inv, lax.axis_size("row"), row_count, first, parts)
    z_off, z_diag = fused_call(struct, hit, slot, sigma_rows, diag_inv, u_head, first, parts)
    return (z_off, z_diag)


def solution(mesh):
    in_specs = (
        P("row", "col", None, None),
        P("row", "col", None, None),
        P("col", None, None),
        P("col", None),
    )
    out_specs = (P("col", "row", None, None), P(("col", "row"), None, None))
    return jax.shard_map(body, mesh=mesh, in_specs=in_specs, out_specs=out_specs, check_vma=False)
```

```python
import functools

import jax
import jax.numpy as jnp
from jax import lax
from jax.experimental import pallas as pl
from jax.experimental.pallas import tpu as pltpu
from jax.sharding import PartitionSpec as P

high = lax.Precision.HIGH


def greet_neighbours(me, col, n):
    barrier = pltpu.get_barrier_semaphore()
    for peer in (lax.rem(me + n - 1, n), lax.rem(me + 1, n)):
        pl.semaphore_signal(barrier, inc=1, device_id=(peer, col), device_id_type=pl.DeviceIdType.MESH)
    pl.semaphore_wait(barrier, 2)


def step_parts(step, direction, half, parts):
    if step < half:
        return range(parts)
    if direction == 0:
        return range(parts // 2)
    return range(parts // 2, parts)


def ring_kernel(steps, parts, rows, struct_ref, factor_ref, inv_ref, out_ref, hit_ref, slot_ref, u_scr,
                copy_sem, send_sem, recv_sem):
    n = out_ref.shape[0]
    chunk = out_ref.shape[1] // parts
    me = lax.axis_index("row")
    col = lax.axis_index("col")

    def link(step, direction, part):
        if direction == 0:
            slot = lax.rem(me - (step - 1) + n, n)
            peer = lax.rem(me + 1, n)
        else:
            slot = lax.rem(me + (step - 1), n)
            peer = lax.rem(me + n - 1, n)
        piece = pl.ds(part * chunk, chunk)
        return pltpu.make_async_remote_copy(
            src_ref=out_ref.at[slot, piece], dst_ref=out_ref.at[slot, piece],
            send_sem=send_sem.at[direction, step - 1, part],
            recv_sem=recv_sem.at[direction, step - 1, part],
            device_id=(peer, col), device_id_type=pl.DeviceIdType.MESH)

    def make_u(k, carry):
        u_scr[k] = jnp.dot(factor_ref[k], inv_ref[k], precision=high, preferred_element_type=jnp.float32)
        return carry

    lax.fori_loop(0, u_scr.shape[0], make_u, 0)
    greet_neighbours(me, col, n)
    own = pltpu.make_async_copy(u_scr, out_ref.at[me], copy_sem.at[0])
    own.start()
    own.wait()

    started = []
    for step in range(1, steps + 1):
        for direction in (0, 1):
            for part in range(parts):
                if step > 1:
                    link(step - 1, direction, part).wait_recv()
                copy = link(step, direction, part)
                copy.start()
                started.append(copy)
        if step <= rows:
            j = step - 1
            base = me * rows + j

            def member(k, carry):
                def scan(s, acc):
                    hit = (struct_ref[k, s] == base).astype(jnp.int32)
                    return acc[0] + hit, acc[1] + hit * s
                hits, slot = lax.fori_loop(0, n, scan, (jnp.int32(0), jnp.int32(0)))
                hit_ref[k, j] = hits
                slot_ref[k, j] = slot
                return carry

            lax.fori_loop(0, struct_ref.shape[0], member, 0)
    for direction in (0, 1):
        for part in range(parts):
            link(steps, direction, part).wait_recv()
    for copy in started:
        copy.wait_send()


def ring_gather(struct, factor_own, diag_inv, slots, rows, steps, parts):
    nodes, width, _ = diag_inv.shape
    return pl.pallas_call(
        functools.partial(ring_kernel, steps, parts, rows),
        out_shape=[
            jax.ShapeDtypeStruct((slots, nodes, width, width), jnp.float32),
            jax.ShapeDtypeStruct((nodes, rows), jnp.int32),
            jax.ShapeDtypeStruct((nodes, rows), jnp.int32),
        ],
        in_specs=[pl.BlockSpec(memory_space=pltpu.SMEM), pl.BlockSpec(memory_space=pltpu.VMEM),
                  pl.BlockSpec(memory_space=pltpu.VMEM)],
        out_specs=[
            pl.BlockSpec(memory_space=pl.ANY),
            pl.BlockSpec(memory_space=pltpu.SMEM),
            pl.BlockSpec(memory_space=pltpu.SMEM),
        ],
        scratch_shapes=[
            pltpu.VMEM((nodes, width, width), jnp.float32),
            pltpu.SemaphoreType.DMA((1,)),
            pltpu.SemaphoreType.DMA((2, steps, parts)),
            pltpu.SemaphoreType.DMA((2, steps, parts)),
        ],
        compiler_params=pltpu.CompilerParams(collective_id=0, has_side_effects=True),
    )(struct, factor_own, diag_inv)


def fused_kernel(first, parts, struct_ref, hit_ref, slot_ref, sig_ref, inv_ref, u_in, zoff_ref, sum_ref,
                 u_vmem, y_acc, part_ref, gather_buf, inv_vmem, load_sem, send_sem, recv_sem, out_sem, in_sem,
                 inv_sem):
    n = u_in.shape[0]
    half = n // 2
    nodes = u_in.shape[1]
    chunk = nodes // parts
    rows = sig_ref.shape[0]
    width = sig_ref.shape[-1]
    me = lax.axis_index("row")
    col = lax.axis_index("col")

    def link(step, direction, part):
        if direction == 0:
            slot = lax.rem(me - (step - 1) + n, n)
            peer = lax.rem(me + 1, n)
        else:
            slot = lax.rem(me + (step - 1), n)
            peer = lax.rem(me + n - 1, n)
        piece = pl.ds(part * chunk, chunk)
        source = u_in if step == first + 1 else u_vmem
        return pltpu.make_async_remote_copy(
            src_ref=source.at[slot, piece], dst_ref=u_vmem.at[slot, piece],
            send_sem=send_sem.at[direction, step - 1 - first, part],
            recv_sem=recv_sem.at[direction, step - 1 - first, part],
            device_id=(peer, col), device_id_type=pl.DeviceIdType.MESH)

    def load(slot):
        return pltpu.make_async_copy(u_in.at[slot], u_vmem.at[slot], load_sem.at[slot])

    def wrap(offset):
        return lax.rem(me + offset + 2 * n, n)

    barrier = pltpu.get_barrier_semaphore()
    for offset in range(1, n):
        pl.semaphore_signal(barrier, inc=1, device_id=(lax.rem(me + offset, n), col),
                            device_id_type=pl.DeviceIdType.MESH)
    pl.semaphore_wait(barrier, n - 1)
    for offset in range(-first, first + 1):
        load(wrap(offset)).start()
    inv_copy = pltpu.make_async_copy(inv_ref.at[me], inv_vmem, inv_sem.at[0])
    inv_copy.start()

    started = []

    def send_step(step):
        for direction in (0, 1):
            for part in step_parts(step, direction, half, parts):
                copy = link(step, direction, part)
                copy.start()
                started.append(copy)

    send_step(first + 1)

    def lhs_block(k, slot):
        return sig_ref[:, struct_ref[k, slot]].reshape(rows * width, width)

    def add_single(slot):
        def node(k, carry):
            y_acc[k] += jnp.dot(lhs_block(k, slot), u_vmem[slot, k], precision=high,
                                preferred_element_type=jnp.float32)
            return carry
        lax.fori_loop(0, nodes, node, 0)

    def add_pair(one, two):
        def node(k, carry):
            lhs = jnp.concatenate([lhs_block(k, one), lhs_block(k, two)], axis=1)
            rhs = jnp.concatenate([u_vmem[one, k], u_vmem[two, k]], axis=0)
            y_acc[k] += jnp.dot(lhs, rhs, precision=high, preferred_element_type=jnp.float32)
            return carry
        lax.fori_loop(0, nodes, node, 0)

    def ring_event(step):
        for direction in (0, 1):
            for part in step_parts(step, direction, half, parts):
                link(step, direction, part).wait_recv()
        if step < half:
            send_step(step + 1)

    def arrived(step):
        if step < half:
            add_pair(wrap(-step), wrap(step))
        else:
            add_single(wrap(half))

    processed = first
    load(me).wait()
    y_acc[...] = jnp.zeros_like(y_acc)
    add_single(me)
    for offset in range(1, first + 1):
        load(wrap(-offset)).wait()
        load(wrap(offset)).wait()
        add_pair(wrap(-offset), wrap(offset))
        if offset % 2 == 0 and processed < half:
            processed += 1
            ring_event(processed)
    done = first + 1
    while done < half:
        if done <= processed:
            arrived(done)
            done += 1
        else:
            processed += 1
            ring_event(processed)
    while processed < half:
        processed += 1
        ring_event(processed)
    last = wrap(half)

    for copy in started:
        copy.wait_send()

    def share_to(k):
        return pltpu.make_async_remote_copy(
            src_ref=part_ref.at[k], dst_ref=gather_buf.at[me],
            send_sem=out_sem.at[k], recv_sem=in_sem.at[me],
            device_id=(k, col), device_id_type=pl.DeviceIdType.MESH)

    def share_from(j):
        return pltpu.make_async_remote_copy(
            src_ref=part_ref.at[j], dst_ref=gather_buf.at[j],
            send_sem=out_sem.at[j], recv_sem=in_sem.at[j],
            device_id=(j, col), device_id_type=pl.DeviceIdType.MESH)

    def finish(k, carry):
        y = y_acc[k] + jnp.dot(lhs_block(k, last), u_vmem[last, k], precision=high,
                               preferred_element_type=jnp.float32)
        y = y.reshape(rows, width, width)
        total = jnp.zeros((width, width), jnp.float32)
        for j in range(rows):
            hits = hit_ref[k, j]
            slot = jnp.minimum(slot_ref[k, j], n - 1)
            term = jnp.dot(jnp.transpose(u_vmem[slot, k]), y[j], precision=high,
                           preferred_element_type=jnp.float32)
            total = total + jnp.where(hits > 0, term, 0.0)
            zoff_ref[k, j] = jnp.where(hits > 0, -y[j], 0.0)
        part_ref[k] = total

        @pl.when((k >= 1) & (k - 1 != me))
        def _():
            share_to(k - 1).start()

        return carry

    lax.fori_loop(0, nodes, finish, 0)

    @pl.when(me != nodes - 1)
    def _():
        share_to(nodes - 1).start()

    gather_buf[me] = part_ref[me]
    for j in range(n):
        @pl.when(me != j)
        def _():
            share_to(j).wait_send()
            share_from(j).wait_recv()

    inv_copy.wait()
    inverse = inv_vmem[...]
    inverse_part = jnp.dot(jnp.transpose(inverse), inverse, precision=high,
                           preferred_element_type=jnp.float32)
    sum_ref[0] = inverse_part + jnp.sum(gather_buf[...], axis=0)


def fused_call(struct, hit, slot, sigma_rows, inverse_share, u_all, first, parts):
    slots, nodes, width, _ = u_all.shape
    rows = sigma_rows.shape[0]
    later = slots // 2 - first
    flops = 2 * nodes * slots * rows * width ** 3 * 3
    return pl.pallas_call(
        functools.partial(fused_kernel, first, parts),
        out_shape=[
            jax.ShapeDtypeStruct((nodes, rows, width, width), jnp.float32),
            jax.ShapeDtypeStruct((1, width, width), jnp.float32),
        ],
        in_specs=[
            pl.BlockSpec(memory_space=pltpu.SMEM),
            pl.BlockSpec(memory_space=pltpu.SMEM),
            pl.BlockSpec(memory_space=pltpu.SMEM),
            pl.BlockSpec(memory_space=pltpu.VMEM),
            pl.BlockSpec(memory_space=pl.ANY),
            pl.BlockSpec(memory_space=pl.ANY),
        ],
        out_specs=[
            pl.BlockSpec(memory_space=pltpu.VMEM),
            pl.BlockSpec(memory_space=pltpu.VMEM),
        ],
        scratch_shapes=[
            pltpu.VMEM(u_all.shape, jnp.float32),
            pltpu.VMEM((nodes, rows * width, width), jnp.float32),
            pltpu.VMEM((nodes, width, width), jnp.float32),
            pltpu.VMEM((slots, width, width), jnp.float32),
            pltpu.VMEM((width, width), jnp.float32),
            pltpu.SemaphoreType.DMA((slots,)),
            pltpu.SemaphoreType.DMA((2, later, parts)),
            pltpu.SemaphoreType.DMA((2, later, parts)),
            pltpu.SemaphoreType.DMA((slots,)),
            pltpu.SemaphoreType.DMA((slots,)),
            pltpu.SemaphoreType.DMA((1,)),
        ],
        compiler_params=pltpu.CompilerParams(collective_id=1, has_side_effects=True,
                                             vmem_limit_bytes=60 * 1024 * 1024),
        cost_estimate=pl.CostEstimate(flops=flops, transcendentals=0,
                                      bytes_accessed=4 * (sigma_rows.size + u_all.size)),
    )(struct, hit, slot, sigma_rows, inverse_share, u_all)


def body(sigma_anc, factor, diag_inv, struct):
    row_count = sigma_anc.shape[0]
    sigma_rows = lax.all_gather(sigma_anc, "col", axis=1, tiled=True)
    first, parts = 6, 4
    u_head, hit, slot = ring_gather(struct, factor[0], diag_inv, lax.axis_size("row"), row_count, first, parts)
    z_off, z_diag = fused_call(struct, hit, slot, sigma_rows, diag_inv, u_head, first, parts)
    return (z_off, z_diag)


def solution(mesh):
    in_specs = (
        P("row", "col", None, None),
        P("row", "col", None, None),
        P("col", None, None),
        P("col", None),
    )
    out_specs = (P("col", "row", None, None), P(("col", "row"), None, None))
    return jax.shard_map(body, mesh=mesh, in_specs=in_specs, out_specs=out_specs, check_vma=False)
```

```python
import functools

import jax
import jax.numpy as jnp
from jax import lax
from jax.experimental import pallas as pl
from jax.experimental.pallas import tpu as pltpu
from jax.sharding import PartitionSpec as P

high = lax.Precision.HIGH


def greet_neighbours(me, col, n):
    barrier = pltpu.get_barrier_semaphore()
    for peer in (lax.rem(me + n - 1, n), lax.rem(me + 1, n)):
        pl.semaphore_signal(barrier, inc=1, device_id=(peer, col), device_id_type=pl.DeviceIdType.MESH)
    pl.semaphore_wait(barrier, 2)


def step_parts(step, direction, half, parts):
    if step < half:
        return range(parts)
    if direction == 0:
        return range(parts // 2)
    return range(parts // 2, parts)


def ring_kernel(steps, parts, rows, struct_ref, factor_ref, inv_ref, out_ref, hit_ref, slot_ref, u_scr,
                copy_sem, send_sem, recv_sem):
    n = out_ref.shape[0]
    chunk = out_ref.shape[1] // parts
    me = lax.axis_index("row")
    col = lax.axis_index("col")

    def link(step, direction, part):
        if direction == 0:
            slot = lax.rem(me - (step - 1) + n, n)
            peer = lax.rem(me + 1, n)
        else:
            slot = lax.rem(me + (step - 1), n)
            peer = lax.rem(me + n - 1, n)
        piece = pl.ds(part * chunk, chunk)
        return pltpu.make_async_remote_copy(
            src_ref=out_ref.at[slot, piece], dst_ref=out_ref.at[slot, piece],
            send_sem=send_sem.at[direction, step - 1, part],
            recv_sem=recv_sem.at[direction, step - 1, part],
            device_id=(peer, col), device_id_type=pl.DeviceIdType.MESH)

    def make_u(k, carry):
        u_scr[k] = jnp.dot(factor_ref[k], inv_ref[k], precision=high, preferred_element_type=jnp.float32)
        return carry

    lax.fori_loop(0, u_scr.shape[0], make_u, 0)
    greet_neighbours(me, col, n)
    own = pltpu.make_async_copy(u_scr, out_ref.at[me], copy_sem.at[0])
    own.start()
    own.wait()

    started = []
    for step in range(1, steps + 1):
        for direction in (0, 1):
            for part in range(parts):
                if step > 1:
                    link(step - 1, direction, part).wait_recv()
                copy = link(step, direction, part)
                copy.start()
                started.append(copy)
        if step <= rows:
            j = step - 1
            base = me * rows + j

            def member(k, carry):
                def scan(s, acc):
                    hit = (struct_ref[k, s] == base).astype(jnp.int32)
                    return acc[0] + hit, acc[1] + hit * s
                hits, slot = lax.fori_loop(0, n, scan, (jnp.int32(0), jnp.int32(0)))
                hit_ref[k, j] = hits
                slot_ref[k, j] = slot
                return carry

            lax.fori_loop(0, struct_ref.shape[0], member, 0)
    for direction in (0, 1):
        for part in range(parts):
            link(steps, direction, part).wait_recv()
    for copy in started:
        copy.wait_send()


def ring_gather(struct, factor_own, diag_inv, slots, rows, steps, parts):
    nodes, width, _ = diag_inv.shape
    return pl.pallas_call(
        functools.partial(ring_kernel, steps, parts, rows),
        out_shape=[
            jax.ShapeDtypeStruct((slots, nodes, width, width), jnp.float32),
            jax.ShapeDtypeStruct((nodes, rows), jnp.int32),
            jax.ShapeDtypeStruct((nodes, rows), jnp.int32),
        ],
        in_specs=[pl.BlockSpec(memory_space=pltpu.SMEM), pl.BlockSpec(memory_space=pltpu.VMEM),
                  pl.BlockSpec(memory_space=pltpu.VMEM)],
        out_specs=[
            pl.BlockSpec(memory_space=pl.ANY),
            pl.BlockSpec(memory_space=pltpu.SMEM),
            pl.BlockSpec(memory_space=pltpu.SMEM),
        ],
        scratch_shapes=[
            pltpu.VMEM((nodes, width, width), jnp.float32),
            pltpu.SemaphoreType.DMA((1,)),
            pltpu.SemaphoreType.DMA((2, steps, parts)),
            pltpu.SemaphoreType.DMA((2, steps, parts)),
        ],
        compiler_params=pltpu.CompilerParams(collective_id=0, has_side_effects=True),
    )(struct, factor_own, diag_inv)


def fused_kernel(first, parts, struct_ref, hit_ref, slot_ref, sig_ref, inv_ref, u_in, zoff_ref, sum_ref,
                 u_vmem, y_acc, part_ref, gather_buf, inv_vmem, load_sem, send_sem, recv_sem, out_sem, in_sem,
                 inv_sem):
    n = u_in.shape[0]
    half = n // 2
    nodes = u_in.shape[1]
    chunk = nodes // parts
    rows = sig_ref.shape[0]
    width = sig_ref.shape[-1]
    me = lax.axis_index("row")
    col = lax.axis_index("col")

    def link(step, direction, part):
        if direction == 0:
            slot = lax.rem(me - (step - 1) + n, n)
            peer = lax.rem(me + 1, n)
        else:
            slot = lax.rem(me + (step - 1), n)
            peer = lax.rem(me + n - 1, n)
        piece = pl.ds(part * chunk, chunk)
        source = u_in if step == first + 1 else u_vmem
        return pltpu.make_async_remote_copy(
            src_ref=source.at[slot, piece], dst_ref=u_vmem.at[slot, piece],
            send_sem=send_sem.at[direction, step - 1 - first, part],
            recv_sem=recv_sem.at[direction, step - 1 - first, part],
            device_id=(peer, col), device_id_type=pl.DeviceIdType.MESH)

    def load(slot):
        return pltpu.make_async_copy(u_in.at[slot], u_vmem.at[slot], load_sem.at[slot])

    def wrap(offset):
        return lax.rem(me + offset + 2 * n, n)

    barrier = pltpu.get_barrier_semaphore()
    for offset in range(1, n):
        pl.semaphore_signal(barrier, inc=1, device_id=(lax.rem(me + offset, n), col),
                            device_id_type=pl.DeviceIdType.MESH)
    pl.semaphore_wait(barrier, n - 1)
    for offset in range(-first, first + 1):
        load(wrap(offset)).start()
    inv_copy = pltpu.make_async_copy(inv_ref.at[me], inv_vmem, inv_sem.at[0])
    inv_copy.start()

    started = []

    def send_step(step):
        for direction in (0, 1):
            for part in step_parts(step, direction, half, parts):
                copy = link(step, direction, part)
                copy.start()
                started.append(copy)

    send_step(first + 1)

    def lhs_block(k, slot):
        return sig_ref[:, struct_ref[k, slot]].reshape(rows * width, width)

    def add_single(slot):
        def node(k, carry):
            y_acc[k] += jnp.dot(lhs_block(k, slot), u_vmem[slot, k], precision=high,
                                preferred_element_type=jnp.float32)
            return carry
        lax.fori_loop(0, nodes, node, 0)

    def add_pair(one, two):
        def node(k, carry):
            lhs = jnp.concatenate([lhs_block(k, one), lhs_block(k, two)], axis=1)
            rhs = jnp.concatenate([u_vmem[one, k], u_vmem[two, k]], axis=0)
            y_acc[k] += jnp.dot(lhs, rhs, precision=high, preferred_element_type=jnp.float32)
            return carry
        lax.fori_loop(0, nodes, node, 0)

    def ring_event(step):
        for direction in (0, 1):
            for part in step_parts(step, direction, half, parts):
                link(step, direction, part).wait_recv()
        if step < half:
            send_step(step + 1)

    def arrived(step):
        if step < half:
            add_pair(wrap(-step), wrap(step))
        else:
            add_single(wrap(half))

    processed = first
    load(me).wait()
    y_acc[...] = jnp.zeros_like(y_acc)
    add_single(me)
    for offset in range(1, first + 1):
        load(wrap(-offset)).wait()
        load(wrap(offset)).wait()
        add_pair(wrap(-offset), wrap(offset))
        if offset % 2 == 0 and processed < half:
            processed += 1
            ring_event(processed)
    done = first + 1
    while done < half:
        if done <= processed:
            arrived(done)
            done += 1
        else:
            processed += 1
            ring_event(processed)
    while processed < half:
        processed += 1
        ring_event(processed)
    last = wrap(half)

    for copy in started:
        copy.wait_send()

    def share_to(k):
        return pltpu.make_async_remote_copy(
            src_ref=part_ref.at[k], dst_ref=gather_buf.at[me],
            send_sem=out_sem.at[k], recv_sem=in_sem.at[me],
            device_id=(k, col), device_id_type=pl.DeviceIdType.MESH)

    def share_from(j):
        return pltpu.make_async_remote_copy(
            src_ref=part_ref.at[j], dst_ref=gather_buf.at[j],
            send_sem=out_sem.at[j], recv_sem=in_sem.at[j],
            device_id=(j, col), device_id_type=pl.DeviceIdType.MESH)

    def finish(k, carry):
        y = y_acc[k] + jnp.dot(lhs_block(k, last), u_vmem[last, k], precision=high,
                               preferred_element_type=jnp.float32)
        y = y.reshape(rows, width, width)
        total = jnp.zeros((width, width), jnp.float32)
        for j in range(rows):
            hits = hit_ref[k, j]
            slot = jnp.minimum(slot_ref[k, j], n - 1)
            term = lax.dot_general(u_vmem[slot, k], y[j], (((0,), (0,)), ((), ())), precision=high,
                                   preferred_element_type=jnp.float32)
            total = total + jnp.where(hits > 0, term, 0.0)
            zoff_ref[k, j] = jnp.where(hits > 0, -y[j], 0.0)
        part_ref[k] = total

        @pl.when((k >= 1) & (k - 1 != me))
        def _():
            share_to(k - 1).start()

        return carry

    lax.fori_loop(0, nodes, finish, 0)

    @pl.when(me != nodes - 1)
    def _():
        share_to(nodes - 1).start()

    gather_buf[me] = part_ref[me]
    for j in range(n):
        @pl.when(me != j)
        def _():
            share_to(j).wait_send()
            share_from(j).wait_recv()

    inv_copy.wait()
    inverse = inv_vmem[...]
    inverse_part = jnp.dot(jnp.transpose(inverse), inverse, precision=high,
                           preferred_element_type=jnp.float32)
    sum_ref[0] = inverse_part + jnp.sum(gather_buf[...], axis=0)


def fused_call(struct, hit, slot, sigma_rows, inverse_share, u_all, first, parts):
    slots, nodes, width, _ = u_all.shape
    rows = sigma_rows.shape[0]
    later = slots // 2 - first
    flops = 2 * nodes * slots * rows * width ** 3 * 3
    return pl.pallas_call(
        functools.partial(fused_kernel, first, parts),
        out_shape=[
            jax.ShapeDtypeStruct((nodes, rows, width, width), jnp.float32),
            jax.ShapeDtypeStruct((1, width, width), jnp.float32),
        ],
        in_specs=[
            pl.BlockSpec(memory_space=pltpu.SMEM),
            pl.BlockSpec(memory_space=pltpu.SMEM),
            pl.BlockSpec(memory_space=pltpu.SMEM),
            pl.BlockSpec(memory_space=pltpu.VMEM),
            pl.BlockSpec(memory_space=pl.ANY),
            pl.BlockSpec(memory_space=pl.ANY),
        ],
        out_specs=[
            pl.BlockSpec(memory_space=pltpu.VMEM),
            pl.BlockSpec(memory_space=pltpu.VMEM),
        ],
        scratch_shapes=[
            pltpu.VMEM(u_all.shape, jnp.float32),
            pltpu.VMEM((nodes, rows * width, width), jnp.float32),
            pltpu.VMEM((nodes, width, width), jnp.float32),
            pltpu.VMEM((slots, width, width), jnp.float32),
            pltpu.VMEM((width, width), jnp.float32),
            pltpu.SemaphoreType.DMA((slots,)),
            pltpu.SemaphoreType.DMA((2, later, parts)),
            pltpu.SemaphoreType.DMA((2, later, parts)),
            pltpu.SemaphoreType.DMA((slots,)),
            pltpu.SemaphoreType.DMA((slots,)),
            pltpu.SemaphoreType.DMA((1,)),
        ],
        compiler_params=pltpu.CompilerParams(collective_id=1, has_side_effects=True,
                                             vmem_limit_bytes=60 * 1024 * 1024),
        cost_estimate=pl.CostEstimate(flops=flops, transcendentals=0,
                                      bytes_accessed=4 * (sigma_rows.size + u_all.size)),
    )(struct, hit, slot, sigma_rows, inverse_share, u_all)


def body(sigma_anc, factor, diag_inv, struct):
    row_count = sigma_anc.shape[0]
    sigma_rows = lax.all_gather(sigma_anc, "col", axis=1, tiled=True)
    first, parts = 6, 4
    u_head, hit, slot = ring_gather(struct, factor[0], diag_inv, lax.axis_size("row"), row_count, first, parts)
    z_off, z_diag = fused_call(struct, hit, slot, sigma_rows, diag_inv, u_head, first, parts)
    return (z_off, z_diag)


def solution(mesh):
    in_specs = (
        P("row", "col", None, None),
        P("row", "col", None, None),
        P("col", None, None),
        P("col", None),
    )
    out_specs = (P("col", "row", None, None), P(("col", "row"), None, None))
    return jax.shard_map(body, mesh=mesh, in_specs=in_specs, out_specs=out_specs, check_vma=False)
```

```python
import functools

import jax
import jax.numpy as jnp
from jax import lax
from jax.experimental import pallas as pl
from jax.experimental.pallas import tpu as pltpu
from jax.sharding import PartitionSpec as P

high = lax.Precision.HIGH


def greet_neighbours(me, col, n):
    barrier = pltpu.get_barrier_semaphore()
    for peer in (lax.rem(me + n - 1, n), lax.rem(me + 1, n)):
        pl.semaphore_signal(barrier, inc=1, device_id=(peer, col), device_id_type=pl.DeviceIdType.MESH)
    pl.semaphore_wait(barrier, 2)


def step_parts(step, direction, half, parts):
    if step < half:
        return range(parts)
    if direction == 0:
        return range(parts // 2)
    return range(parts // 2, parts)


def ring_kernel(steps, parts, rows, struct_ref, factor_ref, inv_ref, out_ref, hit_ref, slot_ref, u_scr,
                copy_sem, send_sem, recv_sem):
    n = out_ref.shape[0]
    chunk = out_ref.shape[1] // parts
    me = lax.axis_index("row")
    col = lax.axis_index("col")

    def link(step, direction, part):
        if direction == 0:
            slot = lax.rem(me - (step - 1) + n, n)
            peer = lax.rem(me + 1, n)
        else:
            slot = lax.rem(me + (step - 1), n)
            peer = lax.rem(me + n - 1, n)
        piece = pl.ds(part * chunk, chunk)
        return pltpu.make_async_remote_copy(
            src_ref=out_ref.at[slot, piece], dst_ref=out_ref.at[slot, piece],
            send_sem=send_sem.at[direction, step - 1, part],
            recv_sem=recv_sem.at[direction, step - 1, part],
            device_id=(peer, col), device_id_type=pl.DeviceIdType.MESH)

    def make_u(k, carry):
        u_scr[k] = jnp.dot(factor_ref[k], inv_ref[k], precision=high, preferred_element_type=jnp.float32)
        return carry

    lax.fori_loop(0, u_scr.shape[0], make_u, 0)
    greet_neighbours(me, col, n)
    own = pltpu.make_async_copy(u_scr, out_ref.at[me], copy_sem.at[0])
    own.start()
    own.wait()

    started = []
    for step in range(1, steps + 1):
        for direction in (0, 1):
            for part in range(parts):
                if step > 1:
                    link(step - 1, direction, part).wait_recv()
                copy = link(step, direction, part)
                copy.start()
                started.append(copy)
        if step <= rows:
            j = step - 1
            base = me * rows + j

            def member(k, carry):
                def scan(s, acc):
                    hit = (struct_ref[k, s] == base).astype(jnp.int32)
                    return acc[0] + hit, acc[1] + hit * s
                hits, slot = lax.fori_loop(0, n, scan, (jnp.int32(0), jnp.int32(0)))
                hit_ref[k, j] = hits
                slot_ref[k, j] = slot
                return carry

            lax.fori_loop(0, struct_ref.shape[0], member, 0)
    for direction in (0, 1):
        for part in range(parts):
            link(steps, direction, part).wait_recv()
    for copy in started:
        copy.wait_send()


def ring_gather(struct, factor_own, diag_inv, slots, rows, steps, parts):
    nodes, width, _ = diag_inv.shape
    return pl.pallas_call(
        functools.partial(ring_kernel, steps, parts, rows),
        out_shape=[
            jax.ShapeDtypeStruct((slots, nodes, width, width), jnp.float32),
            jax.ShapeDtypeStruct((nodes, rows), jnp.int32),
            jax.ShapeDtypeStruct((nodes, rows), jnp.int32),
        ],
        in_specs=[pl.BlockSpec(memory_space=pltpu.SMEM), pl.BlockSpec(memory_space=pltpu.VMEM),
                  pl.BlockSpec(memory_space=pltpu.VMEM)],
        out_specs=[
            pl.BlockSpec(memory_space=pl.ANY),
            pl.BlockSpec(memory_space=pltpu.SMEM),
            pl.BlockSpec(memory_space=pltpu.SMEM),
        ],
        scratch_shapes=[
            pltpu.VMEM((nodes, width, width), jnp.float32),
            pltpu.SemaphoreType.DMA((1,)),
            pltpu.SemaphoreType.DMA((2, steps, parts)),
            pltpu.SemaphoreType.DMA((2, steps, parts)),
        ],
        compiler_params=pltpu.CompilerParams(collective_id=0, has_side_effects=True),
    )(struct, factor_own, diag_inv)


def fused_kernel(first, parts, struct_ref, hit_ref, slot_ref, sig_ref, inv_ref, u_in, zoff_ref, sum_ref,
                 u_vmem, y_acc, part_ref, gather_buf, inv_vmem, load_sem, send_sem, recv_sem, out_sem, in_sem,
                 inv_sem):
    n = u_in.shape[0]
    half = n // 2
    nodes = u_in.shape[1]
    chunk = nodes // parts
    rows = sig_ref.shape[0]
    width = sig_ref.shape[-1]
    me = lax.axis_index("row")
    col = lax.axis_index("col")

    def link(step, direction, part):
        if direction == 0:
            slot = lax.rem(me - (step - 1) + n, n)
            peer = lax.rem(me + 1, n)
        else:
            slot = lax.rem(me + (step - 1), n)
            peer = lax.rem(me + n - 1, n)
        piece = pl.ds(part * chunk, chunk)
        source = u_in if step == first + 1 else u_vmem
        return pltpu.make_async_remote_copy(
            src_ref=source.at[slot, piece], dst_ref=u_vmem.at[slot, piece],
            send_sem=send_sem.at[direction, step - 1 - first, part],
            recv_sem=recv_sem.at[direction, step - 1 - first, part],
            device_id=(peer, col), device_id_type=pl.DeviceIdType.MESH)

    def load(slot):
        return pltpu.make_async_copy(u_in.at[slot], u_vmem.at[slot], load_sem.at[slot])

    def wrap(offset):
        return lax.rem(me + offset + 2 * n, n)

    barrier = pltpu.get_barrier_semaphore()
    for offset in range(1, n):
        pl.semaphore_signal(barrier, inc=1, device_id=(lax.rem(me + offset, n), col),
                            device_id_type=pl.DeviceIdType.MESH)
    pl.semaphore_wait(barrier, n - 1)
    for offset in range(-first, first + 1):
        load(wrap(offset)).start()
    inv_copy = pltpu.make_async_copy(inv_ref.at[me], inv_vmem, inv_sem.at[0])
    inv_copy.start()

    started = []

    def send_step(step):
        for direction in (0, 1):
            for part in step_parts(step, direction, half, parts):
                copy = link(step, direction, part)
                copy.start()
                started.append(copy)

    send_step(first + 1)

    def lhs_block(k, slot):
        return sig_ref[:, struct_ref[k, slot]].reshape(rows * width, width)

    def add_single(slot):
        def node(k, carry):
            y_acc[k] += jnp.dot(lhs_block(k, slot), u_vmem[slot, k], precision=high,
                                preferred_element_type=jnp.float32)
            return carry
        lax.fori_loop(0, nodes, node, 0)

    def add_pair(one, two):
        def node(k, carry):
            lhs = jnp.concatenate([lhs_block(k, one), lhs_block(k, two)], axis=1)
            rhs = jnp.concatenate([u_vmem[one, k], u_vmem[two, k]], axis=0)
            y_acc[k] += jnp.dot(lhs, rhs, precision=high, preferred_element_type=jnp.float32)
            return carry
        lax.fori_loop(0, nodes, node, 0)

    def ring_event(step):
        for direction in (0, 1):
            for part in step_parts(step, direction, half, parts):
                link(step, direction, part).wait_recv()
        if step < half:
            send_step(step + 1)

    def arrived(step):
        if step < half:
            add_pair(wrap(-step), wrap(step))
        else:
            add_single(wrap(half))

    processed = first
    load(me).wait()
    y_acc[...] = jnp.zeros_like(y_acc)
    add_single(me)
    for offset in range(1, first + 1):
        load(wrap(-offset)).wait()
        load(wrap(offset)).wait()
        add_pair(wrap(-offset), wrap(offset))
        if offset % 2 == 1 and processed < half:
            processed += 1
            ring_event(processed)
    done = first + 1
    while done < half:
        if done <= processed:
            arrived(done)
            done += 1
        else:
            processed += 1
            ring_event(processed)
    while processed < half:
        processed += 1
        ring_event(processed)
    last = wrap(half)

    for copy in started:
        copy.wait_send()

    def share_to(k):
        return pltpu.make_async_remote_copy(
            src_ref=part_ref.at[k], dst_ref=gather_buf.at[me],
            send_sem=out_sem.at[k], recv_sem=in_sem.at[me],
            device_id=(k, col), device_id_type=pl.DeviceIdType.MESH)

    def share_from(j):
        return pltpu.make_async_remote_copy(
            src_ref=part_ref.at[j], dst_ref=gather_buf.at[j],
            send_sem=out_sem.at[j], recv_sem=in_sem.at[j],
            device_id=(j, col), device_id_type=pl.DeviceIdType.MESH)

    def finish(k, carry):
        y = y_acc[k] + jnp.dot(lhs_block(k, last), u_vmem[last, k], precision=high,
                               preferred_element_type=jnp.float32)
        y = y.reshape(rows, width, width)
        total = jnp.zeros((width, width), jnp.float32)
        for j in range(rows):
            hits = hit_ref[k, j]
            slot = jnp.minimum(slot_ref[k, j], n - 1)
            term = jnp.dot(jnp.transpose(u_vmem[slot, k]), y[j], precision=high,
                           preferred_element_type=jnp.float32)
            total = total + jnp.where(hits > 0, term, 0.0)
            zoff_ref[k, j] = jnp.where(hits > 0, -y[j], 0.0)
        part_ref[k] = total

        @pl.when((k >= 1) & (k - 1 != me))
        def _():
            share_to(k - 1).start()

        return carry

    lax.fori_loop(0, nodes, finish, 0)

    @pl.when(me != nodes - 1)
    def _():
        share_to(nodes - 1).start()

    gather_buf[me] = part_ref[me]
    for j in range(n):
        @pl.when(me != j)
        def _():
            share_to(j).wait_send()
            share_from(j).wait_recv()

    inv_copy.wait()
    inverse = inv_vmem[...]
    inverse_part = jnp.dot(jnp.transpose(inverse), inverse, precision=high,
                           preferred_element_type=jnp.float32)
    sum_ref[0] = inverse_part + jnp.sum(gather_buf[...], axis=0)


def fused_call(struct, hit, slot, sigma_rows, inverse_share, u_all, first, parts):
    slots, nodes, width, _ = u_all.shape
    rows = sigma_rows.shape[0]
    later = slots // 2 - first
    flops = 2 * nodes * slots * rows * width ** 3 * 3
    return pl.pallas_call(
        functools.partial(fused_kernel, first, parts),
        out_shape=[
            jax.ShapeDtypeStruct((nodes, rows, width, width), jnp.float32),
            jax.ShapeDtypeStruct((1, width, width), jnp.float32),
        ],
        in_specs=[
            pl.BlockSpec(memory_space=pltpu.SMEM),
            pl.BlockSpec(memory_space=pltpu.SMEM),
            pl.BlockSpec(memory_space=pltpu.SMEM),
            pl.BlockSpec(memory_space=pltpu.VMEM),
            pl.BlockSpec(memory_space=pl.ANY),
            pl.BlockSpec(memory_space=pl.ANY),
        ],
        out_specs=[
            pl.BlockSpec(memory_space=pltpu.VMEM),
            pl.BlockSpec(memory_space=pltpu.VMEM),
        ],
        scratch_shapes=[
            pltpu.VMEM(u_all.shape, jnp.float32),
            pltpu.VMEM((nodes, rows * width, width), jnp.float32),
            pltpu.VMEM((nodes, width, width), jnp.float32),
            pltpu.VMEM((slots, width, width), jnp.float32),
            pltpu.VMEM((width, width), jnp.float32),
            pltpu.SemaphoreType.DMA((slots,)),
            pltpu.SemaphoreType.DMA((2, later, parts)),
            pltpu.SemaphoreType.DMA((2, later, parts)),
            pltpu.SemaphoreType.DMA((slots,)),
            pltpu.SemaphoreType.DMA((slots,)),
            pltpu.SemaphoreType.DMA((1,)),
        ],
        compiler_params=pltpu.CompilerParams(collective_id=1, has_side_effects=True,
                                             vmem_limit_bytes=60 * 1024 * 1024),
        cost_estimate=pl.CostEstimate(flops=flops, transcendentals=0,
                                      bytes_accessed=4 * (sigma_rows.size + u_all.size)),
    )(struct, hit, slot, sigma_rows, inverse_share, u_all)


def body(sigma_anc, factor, diag_inv, struct):
    row_count = sigma_anc.shape[0]
    sigma_rows = lax.all_gather(sigma_anc, "col", axis=1, tiled=True)
    first, parts = 6, 4
    u_head, hit, slot = ring_gather(struct, factor[0], diag_inv, lax.axis_size("row"), row_count, first, parts)
    z_off, z_diag = fused_call(struct, hit, slot, sigma_rows, diag_inv, u_head, first, parts)
    return (z_off, z_diag)


def solution(mesh):
    in_specs = (
        P("row", "col", None, None),
        P("row", "col", None, None),
        P("col", None, None),
        P("col", None),
    )
    out_specs = (P("col", "row", None, None), P(("col", "row"), None, None))
    return jax.shard_map(body, mesh=mesh, in_specs=in_specs, out_specs=out_specs, check_vma=False)
```

```python
import functools

import jax
import jax.numpy as jnp
from jax import lax
from jax.experimental import pallas as pl
from jax.experimental.pallas import tpu as pltpu
from jax.sharding import PartitionSpec as P

high = lax.Precision.HIGH


def greet_neighbours(me, col, n):
    barrier = pltpu.get_barrier_semaphore()
    for peer in (lax.rem(me + n - 1, n), lax.rem(me + 1, n)):
        pl.semaphore_signal(barrier, inc=1, device_id=(peer, col), device_id_type=pl.DeviceIdType.MESH)
    pl.semaphore_wait(barrier, 2)


def step_parts(step, direction, half, parts):
    if step < half:
        return range(parts)
    if direction == 0:
        return range(parts // 2)
    return range(parts // 2, parts)


def ring_kernel(steps, parts, rows, struct_ref, factor_ref, inv_ref, out_ref, hit_ref, slot_ref, u_scr,
                copy_sem, send_sem, recv_sem):
    n = out_ref.shape[0]
    chunk = out_ref.shape[1] // parts
    me = lax.axis_index("row")
    col = lax.axis_index("col")

    def link(step, direction, part):
        if direction == 0:
            slot = lax.rem(me - (step - 1) + n, n)
            peer = lax.rem(me + 1, n)
        else:
            slot = lax.rem(me + (step - 1), n)
            peer = lax.rem(me + n - 1, n)
        piece = pl.ds(part * chunk, chunk)
        return pltpu.make_async_remote_copy(
            src_ref=out_ref.at[slot, piece], dst_ref=out_ref.at[slot, piece],
            send_sem=send_sem.at[direction, step - 1, part],
            recv_sem=recv_sem.at[direction, step - 1, part],
            device_id=(peer, col), device_id_type=pl.DeviceIdType.MESH)

    def make_u(k, carry):
        u_scr[k] = jnp.dot(factor_ref[k], inv_ref[k], precision=high, preferred_element_type=jnp.float32)
        return carry

    lax.fori_loop(0, u_scr.shape[0], make_u, 0)
    greet_neighbours(me, col, n)
    own = pltpu.make_async_copy(u_scr, out_ref.at[me], copy_sem.at[0])
    own.start()
    own.wait()

    started = []
    for step in range(1, steps + 1):
        for direction in (0, 1):
            for part in range(parts):
                if step > 1:
                    link(step - 1, direction, part).wait_recv()
                copy = link(step, direction, part)
                copy.start()
                started.append(copy)
        if step <= rows:
            j = step - 1
            base = me * rows + j

            def member(k, carry):
                def scan(s, acc):
                    hit = (struct_ref[k, s] == base).astype(jnp.int32)
                    return acc[0] + hit, acc[1] + hit * s
                hits, slot = lax.fori_loop(0, n, scan, (jnp.int32(0), jnp.int32(0)))
                hit_ref[k, j] = hits
                slot_ref[k, j] = slot
                return carry

            lax.fori_loop(0, struct_ref.shape[0], member, 0)
    for direction in (0, 1):
        for part in range(parts):
            link(steps, direction, part).wait_recv()
    for copy in started:
        copy.wait_send()


def ring_gather(struct, factor_own, diag_inv, slots, rows, steps, parts):
    nodes, width, _ = diag_inv.shape
    return pl.pallas_call(
        functools.partial(ring_kernel, steps, parts, rows),
        out_shape=[
            jax.ShapeDtypeStruct((slots, nodes, width, width), jnp.float32),
            jax.ShapeDtypeStruct((nodes, rows), jnp.int32),
            jax.ShapeDtypeStruct((nodes, rows), jnp.int32),
        ],
        in_specs=[pl.BlockSpec(memory_space=pltpu.SMEM), pl.BlockSpec(memory_space=pltpu.VMEM),
                  pl.BlockSpec(memory_space=pltpu.VMEM)],
        out_specs=[
            pl.BlockSpec(memory_space=pl.ANY),
            pl.BlockSpec(memory_space=pltpu.SMEM),
            pl.BlockSpec(memory_space=pltpu.SMEM),
        ],
        scratch_shapes=[
            pltpu.VMEM((nodes, width, width), jnp.float32),
            pltpu.SemaphoreType.DMA((1,)),
            pltpu.SemaphoreType.DMA((2, steps, parts)),
            pltpu.SemaphoreType.DMA((2, steps, parts)),
        ],
        compiler_params=pltpu.CompilerParams(collective_id=0, has_side_effects=True),
    )(struct, factor_own, diag_inv)


def fused_kernel(first, parts, struct_ref, hit_ref, slot_ref, sig_ref, inv_ref, u_in, zoff_ref, sum_ref,
                 u_vmem, y_acc, part_ref, gather_buf, inv_vmem, load_sem, send_sem, recv_sem, out_sem, in_sem,
                 inv_sem):
    n = u_in.shape[0]
    half = n // 2
    nodes = u_in.shape[1]
    chunk = nodes // parts
    rows = sig_ref.shape[0]
    width = sig_ref.shape[-1]
    me = lax.axis_index("row")
    col = lax.axis_index("col")

    def link(step, direction, part):
        if direction == 0:
            slot = lax.rem(me - (step - 1) + n, n)
            peer = lax.rem(me + 1, n)
        else:
            slot = lax.rem(me + (step - 1), n)
            peer = lax.rem(me + n - 1, n)
        piece = pl.ds(part * chunk, chunk)
        source = u_in if step == first + 1 else u_vmem
        return pltpu.make_async_remote_copy(
            src_ref=source.at[slot, piece], dst_ref=u_vmem.at[slot, piece],
            send_sem=send_sem.at[direction, step - 1 - first, part],
            recv_sem=recv_sem.at[direction, step - 1 - first, part],
            device_id=(peer, col), device_id_type=pl.DeviceIdType.MESH)

    def load(slot):
        return pltpu.make_async_copy(u_in.at[slot], u_vmem.at[slot], load_sem.at[slot])

    def wrap(offset):
        return lax.rem(me + offset + 2 * n, n)

    barrier = pltpu.get_barrier_semaphore()
    for offset in range(1, n):
        pl.semaphore_signal(barrier, inc=1, device_id=(lax.rem(me + offset, n), col),
                            device_id_type=pl.DeviceIdType.MESH)
    pl.semaphore_wait(barrier, n - 1)
    for offset in range(-first, first + 1):
        load(wrap(offset)).start()
    inv_copy = pltpu.make_async_copy(inv_ref.at[me], inv_vmem, inv_sem.at[0])
    inv_copy.start()

    started = []

    def send_step(step):
        for direction in (0, 1):
            for part in step_parts(step, direction, half, parts):
                copy = link(step, direction, part)
                copy.start()
                started.append(copy)

    send_step(first + 1)

    def lhs_block(k, slot):
        return sig_ref[:, struct_ref[k, slot]].reshape(rows * width, width)

    def add_single(slot):
        def node(k, carry):
            y_acc[k] += jnp.dot(lhs_block(k, slot), u_vmem[slot, k], precision=high,
                                preferred_element_type=jnp.float32)
            return carry
        lax.fori_loop(0, nodes, node, 0)

    def add_pair(one, two):
        def node(k, carry):
            lhs = jnp.concatenate([lhs_block(k, one), lhs_block(k, two)], axis=1)
            rhs = jnp.concatenate([u_vmem[one, k], u_vmem[two, k]], axis=0)
            y_acc[k] += jnp.dot(lhs, rhs, precision=high, preferred_element_type=jnp.float32)
            return carry
        lax.fori_loop(0, nodes, node, 0)

    def ring_event(step):
        for direction in (0, 1):
            for part in step_parts(step, direction, half, parts):
                link(step, direction, part).wait_recv()
        if step < half:
            send_step(step + 1)

    def arrived(step):
        if step < half:
            add_pair(wrap(-step), wrap(step))
        else:
            add_single(wrap(half))

    processed = first
    load(me).wait()
    y_acc[...] = jnp.zeros_like(y_acc)
    add_single(me)
    for offset in range(1, first + 1):
        load(wrap(-offset)).wait()
        load(wrap(offset)).wait()
        add_pair(wrap(-offset), wrap(offset))
        if offset % 2 == 0 and processed < half:
            processed += 1
            ring_event(processed)
    done = first + 1
    while done < half:
        if done <= processed:
            arrived(done)
            done += 1
        else:
            processed += 1
            ring_event(processed)
    while processed < half:
        processed += 1
        ring_event(processed)
    last = wrap(half)

    for copy in started:
        copy.wait_send()

    def share_to(k):
        return pltpu.make_async_remote_copy(
            src_ref=part_ref.at[k], dst_ref=gather_buf.at[me],
            send_sem=out_sem.at[k], recv_sem=in_sem.at[me],
            device_id=(k, col), device_id_type=pl.DeviceIdType.MESH)

    def share_from(j):
        return pltpu.make_async_remote_copy(
            src_ref=part_ref.at[j], dst_ref=gather_buf.at[j],
            send_sem=out_sem.at[j], recv_sem=in_sem.at[j],
            device_id=(j, col), device_id_type=pl.DeviceIdType.MESH)

    def finish(k, carry):
        y = y_acc[k] + jnp.dot(lhs_block(k, last), u_vmem[last, k], precision=high,
                               preferred_element_type=jnp.float32)
        y = y.reshape(rows, width, width)
        total = jnp.zeros((width, width), jnp.float32)
        for j in range(rows):
            hits = hit_ref[k, j]
            slot = jnp.minimum(slot_ref[k, j], n - 1)
            term = jnp.dot(jnp.transpose(u_vmem[slot, k]), y[j], precision=high,
                           preferred_element_type=jnp.float32)
            total = total + jnp.where(hits > 0, term, 0.0)
            zoff_ref[k, j] = jnp.where(hits > 0, -y[j], 0.0)
        part_ref[k] = total

        @pl.when((k >= 1) & (k - 1 != me))
        def _():
            share_to(k - 1).start()

        return carry

    lax.fori_loop(0, nodes, finish, 0)

    @pl.when(me != nodes - 1)
    def _():
        share_to(nodes - 1).start()

    gather_buf[me] = part_ref[me]
    for j in range(n):
        @pl.when(me != j)
        def _():
            share_to(j).wait_send()
            share_from(j).wait_recv()

    inv_copy.wait()
    inverse = inv_vmem[...]
    inverse_part = jnp.dot(jnp.transpose(inverse), inverse, precision=high,
                           preferred_element_type=jnp.float32)
    sum_ref[0] = inverse_part + jnp.sum(gather_buf[...], axis=0)


def fused_call(struct, hit, slot, sigma_rows, inverse_share, u_all, first, parts):
    slots, nodes, width, _ = u_all.shape
    rows = sigma_rows.shape[0]
    later = slots // 2 - first
    flops = 2 * nodes * slots * rows * width ** 3 * 3
    return pl.pallas_call(
        functools.partial(fused_kernel, first, parts),
        out_shape=[
            jax.ShapeDtypeStruct((nodes, rows, width, width), jnp.float32),
            jax.ShapeDtypeStruct((1, width, width), jnp.float32),
        ],
        in_specs=[
            pl.BlockSpec(memory_space=pltpu.SMEM),
            pl.BlockSpec(memory_space=pltpu.SMEM),
            pl.BlockSpec(memory_space=pltpu.SMEM),
            pl.BlockSpec(memory_space=pltpu.VMEM),
            pl.BlockSpec(memory_space=pl.ANY),
            pl.BlockSpec(memory_space=pl.ANY),
        ],
        out_specs=[
            pl.BlockSpec(memory_space=pltpu.VMEM),
            pl.BlockSpec(memory_space=pltpu.VMEM),
        ],
        scratch_shapes=[
            pltpu.VMEM(u_all.shape, jnp.float32),
            pltpu.VMEM((nodes, rows * width, width), jnp.float32),
            pltpu.VMEM((nodes, width, width), jnp.float32),
            pltpu.VMEM((slots, width, width), jnp.float32),
            pltpu.VMEM((width, width), jnp.float32),
            pltpu.SemaphoreType.DMA((slots,)),
            pltpu.SemaphoreType.DMA((2, later, parts)),
            pltpu.SemaphoreType.DMA((2, later, parts)),
            pltpu.SemaphoreType.DMA((slots,)),
            pltpu.SemaphoreType.DMA((slots,)),
            pltpu.SemaphoreType.DMA((1,)),
        ],
        compiler_params=pltpu.CompilerParams(collective_id=1, has_side_effects=True,
                                             vmem_limit_bytes=60 * 1024 * 1024),
        cost_estimate=pl.CostEstimate(flops=flops, transcendentals=0,
                                      bytes_accessed=4 * (sigma_rows.size + u_all.size)),
    )(struct, hit, slot, sigma_rows, inverse_share, u_all)


def body(sigma_anc, factor, diag_inv, struct):
    row_count = sigma_anc.shape[0]
    sigma_rows = lax.all_gather(sigma_anc, "col", axis=1, tiled=True)
    first, parts = 6, 2
    u_head, hit, slot = ring_gather(struct, factor[0], diag_inv, lax.axis_size("row"), row_count, first, parts)
    z_off, z_diag = fused_call(struct, hit, slot, sigma_rows, diag_inv, u_head, first, parts)
    return (z_off, z_diag)


def solution(mesh):
    in_specs = (
        P("row", "col", None, None),
        P("row", "col", None, None),
        P("col", None, None),
        P("col", None),
    )
    out_specs = (P("col", "row", None, None), P(("col", "row"), None, None))
    return jax.shard_map(body, mesh=mesh, in_specs=in_specs, out_specs=out_specs, check_vma=False)
```
